32 devices in a mesh: dp: 2 (over x), uly: 4 (over z), blk: 4 (over y, core).
Axes of the slice: x: 2, y: 2, z: 4, core: 2. Of those that a mesh axis runs over, the one named last changes fastest.
Arguments:
- inputs: float32 [1, 4096, 768], P(None, ('dp', 'uly', 'blk')), may hold values from -6 to 6
- cotangent: float32 [1, 4096, 768], P(None, ('dp', 'uly', 'blk')), may hold values from -6 to 6
- qkv_weight: bfloat16 [768, 2304], P(('dp', 'blk')), may hold values from -0.21875 to 0.21875
- query_bias: bfloat16 [768], P(('dp', 'blk')), may hold values from -4 to 4
- value_bias: bfloat16 [768], P(('dp', 'blk')), may hold values from -0.75 to 0.75
- out_weight: bfloat16 [768, 768], P(('dp', 'blk')), may hold values from -3 to 3
- out_bias: bfloat16 [768], P(('dp', 'blk')), may hold values from -4 to 4
- norm1_gain: bfloat16 [768], P(('dp', 'blk')), may hold values from 0.099609375 to 1.8984375
- norm1_bias: bfloat16 [768], P(('dp', 'blk')), may hold values from -4 to 4
- norm2_gain: bfloat16 [768], P(('dp', 'blk')), may hold values from 0.099609375 to 1.8984375
- norm2_bias: bfloat16 [768], P(('dp', 'blk')), may hold values from -4 to 4
- up_weight: bfloat16 [768, 3072], P(('dp', 'blk')), may hold values from -0.21875 to 0.21875
- up_bias: bfloat16 [3072], P(('dp', 'blk')), may hold values from -4 to 4
- down_weight: bfloat16 [3072, 768], P(None, ('dp', 'blk')), may hold values from -0.109375 to 0.109375
- down_bias: bfloat16 [768], P(('dp', 'blk')), may hold values from -4 to 4
- doc_lengths: int32 [1, 2, 8], P(None, 'dp'), may hold values from 1 to 1024, 2048 in all within a row
- pad_mask: int32 [1, 4096], P(None, 'dp'), may hold values 0 or 1
Outputs:
- output: float32 [1, 4096, 768], P(None, ('dp', 'uly', 'blk'))
- grad_inputs: float32 [1, 4096, 768], P(None, ('dp', 'uly', 'blk'))
- grad_qkv_weight: float32 [768, 2304], P(('dp', 'blk'))
- grad_query_bias: float32 [768], P(('dp', 'blk'))
- grad_value_bias: float32 [768], P(('dp', 'blk'))
- grad_out_weight: float32 [768, 768], P(('dp', 'blk'))
- grad_out_bias: float32 [768], P(('dp', 'blk'))
- grad_norm1_gain: float32 [768], P(('dp', 'blk'))
- grad_norm1_bias: float32 [768], P(('dp', 'blk'))
- grad_norm2_gain: float32 [768], P(('dp', 'blk'))
- grad_norm2_bias: float32 [768], P(('dp', 'blk'))
- grad_up_weight: float32 [768, 3072], P(('dp', 'blk'))
- grad_up_bias: float32 [3072], P(('dp', 'blk'))
- grad_down_weight: float32 [3072, 768], P(None, ('dp', 'blk'))
- grad_down_bias: float32 [768], P(('dp', 'blk'))
The draws below stay inside these ranges and needn't reach their ends.
Inputs may be any that keep to these rules, and one draw needn't show every extreme that they name: `doc_lengths`: the 8 lengths of a sequence sum to 2048; the longest document of every sequence has 1024 rows.
All inputs are finite; a program needn't handle non-finite values. No bound on the sum of `pad_mask` on one device may be relied on, other than what follows from the above.
Results may differ from the reference program's by a relative error of at most 0.025.
Values may be sent and summed in bfloat16 or wider, within the bound.
No kernel may reach another device: no remote copies, remote signals or barrier semaphores. Data moves between devices by JAX's collectives and lax.ppermute only.
A program may use at most 192 MiB of HBM per device.

```python
import math
import jax
import jax.numpy as jnp
import numpy as np
from jax import lax

D = 768
HEADS = 12
HEAD_DIM = 64
FF = 3072
SEQ_DEV = 1
DOCS = 8
LEN = 2048
SEQS = 2
N_DP = 2


def with_ends(drawn, own_key, low, top_value):
    longest = drawn.shape.index(max(drawn.shape))
    spots = []
    for shift in (0, 1):
        where = [jax.random.randint(jax.random.fold_in(own_key, axis), (), 0, length) for axis, length in enumerate(drawn.shape)]
        where[longest] = (where[longest] + shift) % drawn.shape[longest]
        spots.append(tuple(where))
    return drawn.at[spots[0]].set(low).at[spots[1]].set(top_value)


def shard_levels(stream_key, extent, shards, low, high):
    level, own = 1.0, jax.random.fold_in(stream_key, 6)
    for position, shards_of in shards:
        draws = jnp.exp(jax.random.uniform(jax.random.fold_in(own, position), (shards_of,), jnp.float32, low / len(shards), high / len(shards)))
        level = level * jnp.repeat(draws, extent[position] // shards_of).reshape([-1 if axis == position else 1 for axis in range(len(extent))])
    return level


def split_up(count, total, reach, slope):
    portions = [(1 << 20) // math.isqrt(standing ** slope) + 1 for standing in range(2, count + 1)]
    surplus, counts = total - reach - (count - 1), [1] * (count - 1)
    while surplus > 0:
        candidates = [i for i in range(count - 1) if counts[i] < reach]
        pool, budget = sum([portions[i] for i in candidates]), surplus
        for i in candidates:
            more = min(reach - counts[i], max(1, budget * portions[i] // pool), surplus)
            counts[i] = counts[i] + more
            surplus = surplus - more
    return np.array([reach] + counts)


def ragged(own_key, amount, total, most, slope):
    if amount == 2:
        one = jax.random.randint(own_key, (), max(1, total - most), min(most, total - 1) + 1)
        return jnp.stack([one, total - one])
    lengths = jnp.asarray(split_up(amount, total, most, slope), jnp.int32)
    pairs = (amount - 1) // 2
    donor, receiver = lengths[1:1 + 2 * pairs:2], lengths[2:2 + 2 * pairs:2]
    room = jnp.minimum(donor - 1, most - receiver)
    passed = jax.random.randint(jax.random.fold_in(own_key, 1), (pairs,), 0, 1 << 20) % (room + 1)
    lengths = lengths.at[1:1 + 2 * pairs:2].set(donor - passed).at[2:2 + 2 * pairs:2].set(receiver + passed)
    return lengths[jax.random.permutation(jax.random.fold_in(own_key, 2), amount)]


def bell_draw(stream_key, extent, deviation, limit, split=(), held_as=jnp.bfloat16):
    drawn = jax.random.normal(stream_key, extent, jnp.float32) * deviation
    if len(split) > 0:
        drawn = shard_levels(stream_key, extent, split, -0.22, 0.18) * drawn
    return jnp.clip(drawn, min=-limit, max=limit).astype(held_as)


def setup_inputs(seed: int = 0) -> dict:
    seeds = jax.random.split(jax.random.key(seed), 18)
    return {
        "inputs": bell_draw(seeds[0], (SEQ_DEV, N_DP * LEN, D), 1.0, 6.0, ((1, 32),), jnp.float32),
        "cotangent": bell_draw(seeds[1], (SEQ_DEV, N_DP * LEN, D), 1.0, 6.0, ((1, 32),), jnp.float32),
        "qkv_weight": bell_draw(seeds[2], (D, 3 * D), D ** -0.5, 0.21875, ((0, 8),)),
        "query_bias": bell_draw(seeds[3], (D,), 0.3, 4.0, ((0, 8),)),
        "value_bias": bell_draw(seeds[4], (D,), 0.05, 0.75, ((0, 8),)),
        "out_weight": bell_draw(seeds[5], (D, D), 4 ** -0.5, 3.0, ((0, 8),)),
        "out_bias": bell_draw(seeds[6], (D,), 0.3, 4.0, ((0, 8),)),
        "norm1_gain": jnp.clip(1.0 + 0.18 * jax.random.normal(seeds[7], (D,), jnp.float32), 0.099609375, 1.8984375).astype(jnp.bfloat16),
        "norm1_bias": bell_draw(seeds[8], (D,), 0.3, 4.0, ((0, 8),)),
        "norm2_gain": jnp.clip(1.0 + 0.18 * jax.random.normal(seeds[9], (D,), jnp.float32), 0.099609375, 1.8984375).astype(jnp.bfloat16),
        "norm2_bias": bell_draw(seeds[10], (D,), 0.3, 4.0, ((0, 8),)),
        "up_weight": bell_draw(seeds[11], (D, FF), D ** -0.5, 0.21875, ((0, 8),)),
        "up_bias": bell_draw(seeds[12], (FF,), 0.3, 4.0, ((0, 8),)),
        "down_weight": bell_draw(seeds[13], (FF, D), FF ** -0.5, 0.109375, ((1, 8),)),
        "down_bias": bell_draw(seeds[14], (D,), 0.3, 4.0, ((0, 8),)),
        "doc_lengths": jax.vmap(lambda own: ragged(own, DOCS, LEN, LEN // 2, 2))(jax.random.split(seeds[15], SEQ_DEV * N_DP)).reshape((SEQ_DEV, N_DP, DOCS)).astype(jnp.int32),
        "pad_mask": with_ends((jax.random.randint(seeds[16], (SEQ_DEV, N_DP * LEN), 0, 8) < 7).astype(jnp.int32), jax.random.fold_in(seeds[16], 1), 0, 1),
    }


@jax.custom_vjp
def low(v):
    return lax.optimization_barrier(v.astype(jnp.bfloat16)).astype(jnp.float32)

@jax.custom_vjp
def low_back(v):
    return v

def low_keep(v):
    return (low(v), None)

def low_pass(kept, grad):
    return (grad,)

def back_keep(v):
    return (v, None)

def back_low(kept, grad):
    return (low(grad),)
low.defvjp(low_keep, low_pass)
low_back.defvjp(back_keep, back_low)

def matmul_high(left_rows, right_rows):
    return jnp.dot(left_rows, right_rows, precision=lax.Precision.HIGHEST, preferred_element_type=jnp.float32)

def layer_norm(values_in, gain_vec, shift_vec):
    mean_v = lax.optimization_barrier(jnp.mean(values_in, axis=-1, keepdims=True))
    centered = values_in - mean_v
    var_v = lax.optimization_barrier(jnp.mean(centered * centered, axis=-1, keepdims=True))
    return centered * lax.rsqrt(var_v + 1e-12) * gain_vec + shift_vec

def attend_block(query_rows, seg_query, place_query, keys_all, values_all, seg_keys, valid_keys):
    raw_scores = jnp.einsum('qhe,khe->hqk', query_rows, keys_all, precision=lax.Precision.HIGHEST) * HEAD_DIM ** (-0.5)
    raw_scores = low_back(raw_scores)
    place_keys = jnp.arange(keys_all.shape[0], dtype=jnp.int32)
    allowed = (seg_query[:, None] == seg_keys[None, :]) & ((valid_keys[None, :] > 0) | (place_query[:, None] == place_keys[None, :]))
    scores = jnp.where(allowed[None], raw_scores, -jnp.inf)
    row_max = lax.optimization_barrier(jnp.max(scores, axis=-1, keepdims=True))
    exponent = jnp.exp(scores - row_max)
    totals = lax.optimization_barrier(jnp.sum(exponent, axis=-1, keepdims=True))
    mixture = jnp.einsum('hqk,khe->qhe', low(exponent), values_all, precision=lax.Precision.HIGHEST)
    mixture = mixture / jnp.transpose(totals, (1, 0, 2))
    return mixture.reshape(query_rows.shape[0], D)

def sequence_layer(rows_in, seg_row, valid_row, params):
    qkv_weight, query_bias, value_bias, out_weight, out_bias, norm1_gain, norm1_bias, norm2_gain, norm2_bias, up_weight, up_bias, down_weight, down_bias = params
    h_first = low(layer_norm(rows_in, norm1_gain, norm1_bias))
    zero_bias = jnp.zeros_like(query_bias)
    projected = matmul_high(h_first, qkv_weight) + jnp.concatenate([query_bias, zero_bias, value_bias])
    projected = low_back(low(projected))
    queries = projected[:, :D].reshape(LEN, HEADS, HEAD_DIM)
    keys_all = projected[:, D:2 * D].reshape(LEN, HEADS, HEAD_DIM)
    values_all = projected[:, 2 * D:].reshape(LEN, HEADS, HEAD_DIM)
    query_block = math.gcd(LEN, 512)
    block_count = LEN // query_block
    places = jnp.arange(LEN, dtype=jnp.int32)
    block_fn = jax.checkpoint(attend_block)
    attn_blocks = lax.map(lambda block_item: block_fn(block_item[0], block_item[1], block_item[2], keys_all, values_all, seg_row, valid_row), (queries.reshape(block_count, query_block, HEADS, HEAD_DIM), seg_row.reshape(block_count, query_block), places.reshape(block_count, query_block)))
    attn_rows = low_back(low(attn_blocks.reshape(LEN, D)))
    residual = rows_in + low_back(matmul_high(attn_rows, out_weight) + out_bias)
    h_second = low(layer_norm(residual, norm2_gain, norm2_bias))
    hidden = low_back(matmul_high(h_second, up_weight) + up_bias)
    activated = low(jax.nn.gelu(hidden, approximate=False))
    return residual + low_back(matmul_high(activated, down_weight) + down_bias)

def segment_table(doc_lengths):
    doc_ends = jnp.cumsum(doc_lengths, axis=-1, dtype=jnp.int32)
    places = jnp.arange(LEN, dtype=jnp.int32)
    return lax.optimization_barrier(jnp.sum((places[None, :, None] >= doc_ends[:, None, :]).astype(jnp.int32), axis=-1, dtype=jnp.int32))

def reference(inputs, cotangent, qkv_weight, query_bias, value_bias, out_weight, out_bias, norm1_gain, norm1_bias, norm2_gain, norm2_bias, up_weight, up_bias, down_weight, down_bias, doc_lengths, pad_mask):
    floats = [a.astype(jnp.float32) for a in (inputs, qkv_weight, query_bias, value_bias, out_weight, out_bias, norm1_gain, norm1_bias, norm2_gain, norm2_bias, up_weight, up_bias, down_weight, down_bias)]
    segments = segment_table(doc_lengths.reshape(SEQS, DOCS))
    valid_rows = pad_mask.reshape(SEQS, LEN)

    def whole_layer(rows_all, *params):

        def per_sequence(carried, seq_item):
            return (carried, sequence_layer(seq_item[0], seq_item[1], seq_item[2], params))
        _, layer_out = lax.scan(per_sequence, jnp.zeros((), jnp.float32), (rows_all.reshape(SEQS, LEN, D), segments, valid_rows))
        return layer_out.reshape(SEQ_DEV, N_DP * LEN, D)
    output, pullback = jax.vjp(whole_layer, *floats)
    gradients = pullback(cotangent.astype(jnp.float32))
    return (output, gradients[0], gradients[1], gradients[2], gradients[3], gradients[4], gradients[5], gradients[6], gradients[7], gradients[8], gradients[9], gradients[10], gradients[11], gradients[12], gradients[13])
```

```python
import functools

import jax
import jax.numpy as jnp
from jax import lax
from jax.experimental import pallas as pl
from jax.experimental.pallas import tpu as pltpu
from jax.sharding import PartitionSpec as P

HEADS = 12
HEAD_DIM = 64
FF = 3072
F32 = jnp.float32
BF16 = jnp.bfloat16
NEG = -1e30
VMEM_LIMIT = 60 * 1024 * 1024

ROWS = 128
ULY = 4
BLK = 4
GROUP = ROWS * ULY
KEYS = GROUP * BLK
WIDTH = HEADS * HEAD_DIM
HW = WIDTH // ULY
LOCAL_HEADS = HEADS // ULY
OWNERS = 8
OWN = WIDTH // OWNERS
PANEL = OWN + 16
HALF = FF // 2


def swap(array, axis, by):
    peers = lax.axis_size(axis)
    return lax.ppermute(array, axis, [(i, i ^ by) for i in range(peers)])


def vm():
    return pl.BlockSpec(memory_space=pltpu.VMEM)


def anyspace():
    return pl.BlockSpec(memory_space=pl.ANY)


def smem():
    return pl.BlockSpec(memory_space=pltpu.SMEM)


def call(kernel, outs, args, scratch=(), flops=0, in_any=()):
    specs = [smem()] + [anyspace() if i in in_any else vm() for i in range(1, len(args))]
    nbytes = sum(a.size * a.dtype.itemsize for a in args) + sum(
        o.size * o.dtype.itemsize for o in outs
    )
    return pl.pallas_call(
        kernel,
        out_shape=outs,
        in_specs=specs,
        out_specs=[vm() for _ in outs],
        scratch_shapes=list(scratch),
        cost_estimate=pl.CostEstimate(flops=flops, bytes_accessed=nbytes, transcendentals=0),
        compiler_params=pltpu.CompilerParams(vmem_limit_bytes=VMEM_LIMIT),
    )(*args)


def sds(shape, dtype):
    return jax.ShapeDtypeStruct(shape, dtype)


def nn(a, b):
    return lax.dot_general(a, b, (((1,), (0,)), ((), ())), preferred_element_type=F32)


def nt(a, b):
    return lax.dot_general(a, b, (((1,), (1,)), ((), ())), preferred_element_type=F32)


def tn(a, b):
    return lax.dot_general(a, b, (((0,), (0,)), ((), ())), preferred_element_type=F32)


def rows_at(index, size):
    return pl.ds(pl.multiple_of(index * size, 32), size)


def vec(vv_ref, row, lane):
    return jnp.concatenate(
        [vv_ref[o].astype(F32)[row : row + 1, lane : lane + OWN] for o in range(OWNERS)], axis=1
    )


def norm_stats(v):
    mean = jnp.mean(v, axis=-1, keepdims=True)
    cen = v - mean
    var = jnp.mean(cen * cen, axis=-1, keepdims=True)
    r = lax.rsqrt(var + 1e-12)
    return cen * r, r


def norm_kernel(tab, x_ref, n_ref):
    n_ref[...] = norm_stats(x_ref[...])[0].astype(BF16)


def qkv_kernel(owner_bits, tab, n0, n1, n2, n3, *rest):
    arrays = rest[: len(owner_bits)]
    q_ref, kv_ref, h_ref, w_ref, vv_ref = rest[len(owner_bits) :]
    me, z = tab[0], tab[1]
    for ref, bits in zip(arrays, owner_bits):
        for i, bit in enumerate(bits):
            o = jnp.bitwise_xor(me, bit)
            w_ref[rows_at(o, OWN), :] = ref[i, :OWN, :]
            vv_ref[o] = ref[i, OWN:PANEL, :]
    gain = vec(vv_ref, 0, 0)
    shift = vec(vv_ref, 0, OWN)
    lo = vv_ref[2 * z].astype(F32)
    hi = vv_ref[2 * z + 1].astype(F32)
    zero = jnp.zeros((1, HW), F32)
    bias = jnp.concatenate(
        [
            lo[0:1, 2 * OWN : 3 * OWN],
            hi[0:1, 2 * OWN : 3 * OWN],
            zero,
            lo[0:1, 3 * OWN : 4 * OWN],
            hi[0:1, 3 * OWN : 4 * OWN],
        ],
        axis=1,
    )
    for i, ref in enumerate((n0, n1, n2, n3)):
        rows = slice(i * ROWS, (i + 1) * ROWS)
        h = (ref[...].astype(F32) * gain + shift).astype(BF16)
        h_ref[rows, :] = h
        proj = (nn(h, w_ref[...]) + bias).astype(BF16)
        q_ref[rows, :] = proj[:, :HW] * jnp.asarray(HEAD_DIM ** (-0.5), BF16)
        kv_ref[rows, :] = proj[:, HW:]


def placed(piece, upper):
    zero = jnp.zeros_like(piece)
    return jnp.concatenate([zero, piece] if upper else [piece, zero], axis=1)


def head_cols(h):
    return slice(h * HEAD_DIM, (h + 1) * HEAD_DIM)


def window(index):
    lane = index * HEAD_DIM
    start = lane // 128 * 128
    return slice(start, start + 128), (lane % 128) >= 64


def attend_kernel(tab, q_ref, k0, k1, k2, k3, qc_ref, kc_ref, o0, o1, o2, o3, all_ref, lse_ref):
    kvs = (k0, k1, k2, k3)
    outs = (o0, o1, o2, o3)

    lane = lax.broadcasted_iota(jnp.int32, (ROWS, 128), 1)
    for i in range(ULY):
        rows = slice(i * ROWS, (i + 1) * ROWS)
        code1 = qc_ref[rows, 0:1]
        code2 = qc_ref[rows, 1:2]
        masks = []
        for j in range(BLK):
            kc = kc_ref[0:1, j * GROUP : (j + 1) * GROUP]
            masks.append((kc == code1) | (kc == code2))
        heads = []
        lse = jnp.zeros((ROWS, 128), F32)
        for h in range(LOCAL_HEADS):
            kwin, kup = window(h)
            vwin, vup = window(LOCAL_HEADS + h)
            qp = placed(q_ref[rows, head_cols(h)], kup)
            scores = [
                jnp.where(masks[j], nt(qp, kvs[j][:, kwin]), NEG) for j in range(BLK)
            ]
            top = functools.reduce(jnp.maximum, [jnp.max(s, axis=1, keepdims=True) for s in scores])
            total = jnp.zeros((ROWS, 1), F32)
            acc = jnp.zeros((ROWS, 128), F32)
            for j in range(BLK):
                e = jnp.exp(scores[j] - top)
                total = total + jnp.sum(e, axis=1, keepdims=True)
                acc = acc + nn(e.astype(BF16), kvs[j][:, vwin])
            acc = acc[:, 64:] if vup else acc[:, :64]
            heads.append((acc / total).astype(BF16))
            lse = jnp.where(lane == h, top + jnp.log(total), lse)
        full = jnp.concatenate(heads, axis=1)
        outs[i][...] = full
        all_ref[rows, :] = full
        lse_ref[rows, :] = lse


def mix_kernel(owner_bits, tab, a0, a1, a2, a3, x_ref, vv_ref, *rest):
    arrays = rest[: len(owner_bits)]
    resid_ref, h_ref, ow_ref = rest[len(owner_bits) :]
    me, z = tab[0], tab[1]
    for ref, bits in zip(arrays, owner_bits):
        for i, bit in enumerate(bits):
            ow_ref[rows_at(jnp.bitwise_xor(me, bit), OWN), :] = ref[i]
    acc = x_ref[...] + vec(vv_ref, 0, 4 * OWN)
    for j, ref in enumerate((a0, a1, a2, a3)):
        acc = acc + nn(ref[...], ow_ref[rows_at(jnp.bitwise_xor(z, j), HW), :])
    resid_ref[...] = acc
    n, _ = norm_stats(acc)
    h_ref[...] = (n * vec(vv_ref, 0, 5 * OWN) + vec(vv_ref, 1, 0)).astype(BF16)


CHUNK = 256


def ffn_kernel(owner_bits, tab, h_ref, hp_ref, c_ref, cp_ref, vv_ref, *rest):
    count = len(owner_bits)
    uparts, dparts = rest[:count], rest[count : 2 * count]
    (
        act_ref,
        dhid_ref,
        yo_ref,
        yp_ref,
        go_ref,
        gp_ref,
        u_ref,
        d_ref,
        hall,
        call_ref,
        bias_ref,
        yacc,
        gacc,
        sems,
    ) = rest[2 * count :]
    me, core = tab[0], tab[2]
    copies = []
    for refs, target in ((uparts, u_ref), (dparts, d_ref)):
        for ref, bits in zip(refs, owner_bits):
            for i, bit in enumerate(bits):
                copy = pltpu.make_async_copy(
                    ref.at[i],
                    target.at[rows_at(jnp.bitwise_xor(me, bit), OWN), :],
                    sems.at[len(copies)],
                )
                copy.start()
                copies.append(copy)
    hall[:ROWS, :] = h_ref[...]
    hall[ROWS:, :] = hp_ref[...]
    call_ref[:ROWS, :] = c_ref[...]
    call_ref[ROWS:, :] = cp_ref[...]
    for k in range(4):
        bias_ref[:, k * 384 : (k + 1) * 384] = vv_ref[4 * core + k].astype(F32)[1:2, 192:576]
    yacc[...] = jnp.zeros_like(yacc)
    gacc[...] = jnp.zeros_like(gacc)
    for copy in copies:
        copy.wait()

    def step(k, carry):
        cols = pl.ds(pl.multiple_of(k * CHUNK, CHUNK), CHUNK)
        hid = nn(hall[...], u_ref[:, cols]) + bias_ref[:, cols]
        dact = nn(call_ref[...], d_ref[:, cols])
        cdf = 0.5 * (1.0 + lax.erf(hid * 0.7071067811865476))
        act = (hid * cdf).astype(BF16)
        pdf = jnp.exp(-0.5 * hid * hid) * 0.3989422804014327
        dhid = (dact * (cdf + hid * pdf)).astype(BF16)
        act_ref[:, cols] = act
        dhid_ref[:, cols] = dhid
        yacc[...] += nt(act, d_ref[:, cols])
        gacc[...] += nt(dhid, u_ref[:, cols])
        return carry

    lax.fori_loop(0, HALF // CHUNK, step, 0)
    yo_ref[...] = yacc[:ROWS, :]
    yp_ref[...] = yacc[ROWS:, :].astype(BF16)
    go_ref[...] = gacc[:ROWS, :]
    gp_ref[...] = gacc[ROWS:, :].astype(BF16)


def ffn_grad_kernel(
    tab,
    h_ref,
    hp_ref,
    c_ref,
    cp_ref,
    act_ref,
    dhid_ref,
    ukeep,
    usend,
    dkeep,
    dsend,
    left,
    left2,
    vrow,
):
    me, core = tab[0], tab[2]
    usum = jnp.sum(dhid_ref[...].astype(F32), axis=0, keepdims=True)
    csum = jnp.sum(c_ref[...].astype(F32), axis=0, keepdims=True)
    for o in range(OWNERS):
        part = usum[:, (o % 4) * 384 : (o % 4 + 1) * 384]
        part = jnp.where(core == o // 4, part, 0.0)
        row = jnp.concatenate(
            [part, csum[:, o * OWN : (o + 1) * OWN], jnp.zeros((1, HALF - 480), F32)], axis=1
        )
        vrow[o] = jnp.broadcast_to(row, (16, HALF)).astype(BF16)
    left[:, :ROWS] = h_ref[...].T
    left[:, ROWS:] = hp_ref[...].T
    for ref, base in ((ukeep, 0), (usend, 2)):
        for s in range(4):
            o = jnp.bitwise_xor(me, base + (s // 2) * 4 + s % 2)
            ref[s, :OWN, :] = nn(left[rows_at(o, OWN), :], dhid_ref[...]).astype(BF16)
            ref[s, OWN:, :] = vrow[o]
    left2[:, :ROWS] = c_ref[...].T
    left2[:, ROWS:] = cp_ref[...].T
    for ref, base in ((dkeep, 0), (dsend, 4)):
        for s in range(4):
            o = jnp.bitwise_xor(me, base + (s // 2) * 2 + s % 2)
            ref[s] = nn(left2[rows_at(o, OWN), :], act_ref[...]).astype(BF16)


def back_mix_kernel(
    tab, resid_ref, cot_ref, go_ref, gr_ref, ow_ref, vv_ref, dres_ref, dmix_ref, d0, d1, d2, d3, vs_ref
):
    z = tab[1]
    grad = go_ref[...] + gr_ref[...].astype(F32)
    n, r = norm_stats(resid_ref[...])
    dn = grad * vec(vv_ref, 0, 5 * OWN)
    dres = cot_ref[...] + r * (
        dn
        - jnp.mean(dn, axis=-1, keepdims=True)
        - n * jnp.mean(dn * n, axis=-1, keepdims=True)
    )
    dres_ref[...] = dres
    dmix = dres.astype(BF16)
    dmix_ref[...] = dmix
    for j, ref in enumerate((d0, d1, d2, d3)):
        ref[...] = nt(dmix, ow_ref[rows_at(jnp.bitwise_xor(z, j), HW), :]).astype(BF16)
    vs_ref[0:1, :] = jnp.sum(dmix.astype(F32), axis=0, keepdims=True)
    vs_ref[1:2, :] = jnp.sum(grad * n, axis=0, keepdims=True)
    vs_ref[2:3, :] = jnp.sum(grad, axis=0, keepdims=True)
    vs_ref[3:8, :] = jnp.zeros((5, WIDTH), F32)


def out_grad_kernel(tab, a0, a1, a2, a3, dmix_ref, vs_ref, keep, send, left, vrow):
    me, z = tab[0], tab[1]
    for j, ref in enumerate((a0, a1, a2, a3)):
        left[rows_at(jnp.bitwise_xor(z, j), HW), :] = ref[...].astype(F32).T.astype(BF16)
    vs = vs_ref[...]
    for o in range(OWNERS):
        row = jnp.concatenate(
            [vs[k : k + 1, o * OWN : (o + 1) * OWN] for k in range(3)]
            + [jnp.zeros((1, WIDTH - 3 * OWN), F32)],
            axis=1,
        )
        vrow[o] = jnp.broadcast_to(row, (16, WIDTH)).astype(BF16)
    for ref, base in ((keep, 0), (send, 1)):
        for s in range(4):
            o = jnp.bitwise_xor(me, base + (s // 2) * 2 + (s % 2) * 4)
            ref[s, :OWN, :] = nn(left[rows_at(o, OWN), :], dmix_ref[...]).astype(BF16)
            ref[s, OWN:, :] = vrow[o]


def back_attend_kernel(
    tab,
    q_ref,
    k0,
    k1,
    k2,
    k3,
    g0,
    g1,
    g2,
    g3,
    all_ref,
    lse_ref,
    qr_ref,
    kcol_ref,
    dq_ref,
    keep,
    send,
    acc,
):
    kvs = (k0, k1, k2, k3)
    acc[...] = jnp.zeros_like(acc)
    lane = lax.broadcasted_iota(jnp.int32, (ROWS, 128), 1)
    for i, g_ref in enumerate((g0, g1, g2, g3)):
        rows = slice(i * ROWS, (i + 1) * ROWS)
        prod = g_ref[...].astype(F32) * all_ref[rows, :].astype(F32)
        stat = jnp.zeros((ROWS, 128), F32)
        for h in range(LOCAL_HEADS):
            stat = jnp.where(
                lane == h, jnp.sum(prod[:, head_cols(h)], axis=1, keepdims=True), stat
            )
        rowdot = stat.T
        lse = lse_ref[rows, :].T
        code1 = qr_ref[0:1, rows]
        code2 = qr_ref[1:2, rows]
        dq = [jnp.zeros((ROWS, 128), F32) for _ in range(LOCAL_HEADS)]
        for j in range(BLK):
            kc = kcol_ref[j * GROUP : (j + 1) * GROUP, :]
            mask = (kc == code1) | (kc == code2)
            for h in range(LOCAL_HEADS):
                kwin, kup = window(h)
                vwin, vup = window(LOCAL_HEADS + h)
                qp = placed(q_ref[rows, head_cols(h)], kup)
                gp = placed(g_ref[:, head_cols(h)], vup)
                kk = kvs[j][:, kwin]
                scores = nt(kk, qp)
                p = jnp.where(mask, jnp.exp(scores - lse[h : h + 1, :]), 0.0)
                dp = nt(kvs[j][:, vwin], gp)
                ds = (p * (dp - rowdot[h : h + 1, :])).astype(BF16)
                acc[j, :, vwin] += nn(p.astype(BF16), gp)
                acc[j, :, kwin] += nn(ds, qp)
                dq[h] = dq[h] + tn(ds, kk)
        parts = []
        for h in range(LOCAL_HEADS):
            _, kup = window(h)
            parts.append(dq[h][:, 64:] if kup else dq[h][:, :64])
        dq_ref[rows, :] = (jnp.concatenate(parts, axis=1) * HEAD_DIM ** (-0.5)).astype(BF16)
    keep[0] = acc[0].astype(BF16)
    keep[1] = acc[2].astype(BF16)
    send[0] = acc[1].astype(BF16)
    send[1] = acc[3].astype(BF16)


def back_proj_kernel(
    tab, dq_ref, keep, recv, w_ref, n0, n1, n2, n3, dproj_ref, h0, h1, h2, h3, vs_ref
):
    dproj_ref[:, :HW] = dq_ref[...]
    dproj_ref[:, HW:] = (keep[...].astype(F32) + recv[...].astype(F32)).astype(BF16)
    gain = jnp.zeros((1, WIDTH), F32)
    shift = jnp.zeros((1, WIDTH), F32)
    for i, (n_ref, out) in enumerate(((n0, h0), (n1, h1), (n2, h2), (n3, h3))):
        rows = slice(i * ROWS, (i + 1) * ROWS)
        grad = nt(dproj_ref[rows, :], w_ref[...])
        out[...] = grad.astype(out.dtype)
        gain = gain + jnp.sum(grad * n_ref[...].astype(F32), axis=0, keepdims=True)
        shift = shift + jnp.sum(grad, axis=0, keepdims=True)
    vs_ref[0:1, :] = gain
    vs_ref[1:2, :] = shift
    cols = jnp.sum(dproj_ref[...].astype(F32), axis=0, keepdims=True)
    vs_ref[2:3, :] = jnp.concatenate([cols, jnp.zeros((1, WIDTH - 3 * HW), F32)], axis=1)
    vs_ref[3:8, :] = jnp.zeros((5, WIDTH), F32)


def qkv_grad_kernel(tab, h_ref, dproj_ref, vs_ref, keep, send, left, vrow):
    me, z = tab[0], tab[1]
    vs = vs_ref[...]
    for o in range(OWNERS):
        row = [vs[k : k + 1, o * OWN : (o + 1) * OWN] for k in range(2)]
        for lane in (0, 2 * HW):
            lane = lane + (o % 2) * OWN
            row.append(jnp.where(z == o // 2, vs[2:3, lane : lane + OWN], 0.0))
        row.append(jnp.zeros((1, 3 * HW - 4 * OWN), F32))
        vrow[o] = jnp.broadcast_to(jnp.concatenate(row, axis=1), (16, 3 * HW)).astype(BF16)
    for i in range(ULY):
        rows = slice(i * ROWS, (i + 1) * ROWS)
        left[:, rows] = h_ref[rows, :].T
    for ref, base in ((keep, 0), (send, 1)):
        for s in range(4):
            o = jnp.bitwise_xor(me, base + (s // 2) * 2 + (s % 2) * 4)
            ref[s, :OWN, :] = nn(left[rows_at(o, OWN), :], dproj_ref[...]).astype(BF16)
            ref[s, OWN:, :] = vrow[o]


def back_norm_kernel(tab, x_ref, dres_ref, h0, h1, h2, h3, vv_ref, out_ref):
    grad = h0[...] + h1[...].astype(F32) + h2[...].astype(F32) + h3[...].astype(F32)
    n, r = norm_stats(x_ref[...])
    dn = grad * vec(vv_ref, 0, 0)
    out_ref[...] = dres_ref[...] + r * (
        dn
        - jnp.mean(dn, axis=-1, keepdims=True)
        - n * jnp.mean(dn * n, axis=-1, keepdims=True)
    )


def output_kernel(tab, resid_ref, yo_ref, yr_ref, vv_ref, out_ref):
    out_ref[...] = (
        resid_ref[...] + yo_ref[...] + yr_ref[...].astype(F32) + vec(vv_ref, 1, OWN)
    )


def add_low(a, b):
    return (a.astype(F32) + b.astype(F32)).astype(BF16)


def xor_order(array, axis, index):
    shape = array.shape
    two = array.reshape(shape[:axis] + (2, 2) + shape[axis + 1 :])
    two = jnp.where((index & 1) == 1, jnp.flip(two, axis + 1), two)
    two = jnp.where((index & 2) == 2, jnp.flip(two, axis), two)
    return two.reshape(shape)


def body(
    inputs,
    cotangent,
    qkv_weight,
    query_bias,
    value_bias,
    out_weight,
    out_bias,
    norm1_gain,
    norm1_bias,
    norm2_gain,
    norm2_bias,
    up_weight,
    up_bias,
    down_weight,
    down_bias,
    doc_lengths,
    pad_mask,
):
    dp_count = lax.axis_size("dp")
    near = dp_count == 2
    dp = lax.axis_index("dp")
    z = lax.axis_index("uly")
    b = lax.axis_index("blk")
    core = b & 1
    rank = dp * BLK + b
    me = rank if near else jnp.int32(0)
    tab = jnp.stack([me, z, core, b]).astype(jnp.int32)
    own_rows = WIDTH // (dp_count * BLK)
    axes = ("dp", "blk")

    x = inputs.reshape(ROWS, WIDTH)
    cot = cotangent.reshape(ROWS, WIDTH)
    (n0,) = call(norm_kernel, [sds((ROWS, WIDTH), BF16)], [tab, x])
    n1, n2, n3 = (swap(n0, "uly", k) for k in (1, 2, 3))

    qkv_cols = lax.dynamic_index_in_dim(
        qkv_weight.reshape(own_rows, 3, ULY, HW), z, axis=2, keepdims=False
    ).reshape(own_rows, 3 * HW)
    downt = down_weight.T
    ups = up_weight.reshape(own_rows, 2, HALF)
    downs = downt.reshape(own_rows, 2, HALF)
    if near:
        row0 = jnp.concatenate(
            [norm1_gain, norm1_bias, query_bias, value_bias, out_bias, norm2_gain]
        )
        row1 = jnp.concatenate([norm2_bias, down_bias, up_bias])
        panel = jnp.concatenate(
            [qkv_cols, row0[None], row1[None], jnp.zeros((14, 3 * HW), BF16)], axis=0
        )
        a_0 = jnp.stack([panel, swap(panel, "dp", 1)])
        a_2 = swap(a_0, "blk", 2)
        a_parts = [a_0, a_2, swap(a_0, "blk", 1), swap(a_2, "blk", 1)]
        four_bits = [[0, 4], [2, 6], [1, 5], [3, 7]]
        o_0 = jnp.stack([out_weight, swap(out_weight, "dp", 1)])
        o_2 = swap(o_0, "blk", 2)
        o_parts = [o_0, o_2, swap(o_0, "blk", 1), swap(o_2, "blk", 1)]
        mine = jnp.stack(
            [
                lax.dynamic_index_in_dim(ups, core, 1, False),
                lax.dynamic_index_in_dim(downs, core, 1, False),
            ]
        )
        other = jnp.stack(
            [
                lax.dynamic_index_in_dim(ups, 1 - core, 1, False),
                lax.dynamic_index_in_dim(downs, 1 - core, 1, False),
            ]
        )
        part = swap(other, "blk", 1)
        u_0 = jnp.stack([mine[0], part[0]])
        d_0 = jnp.stack([mine[1], part[1]])
        u_x = swap(u_0, "dp", 1)
        u_y = swap(u_0, "blk", 2)
        u_xy = swap(u_x, "blk", 2)
        d_x = swap(d_0, "dp", 1)
        d_y = swap(d_0, "blk", 2)
        d_xy = swap(d_y, "dp", 1)
        u_parts = [u_0, u_x, u_y, u_xy]
        d_parts = [d_0, d_x, d_y, d_xy]
        ffn_bits = [[0, 1], [4, 5], [2, 3], [6, 7]]
    else:

        def full(array):
            return lax.all_gather(array, axes, axis=0, tiled=True)

        def eight(vector):
            return full(vector).reshape(OWNERS, 1, -1)

        row0 = jnp.concatenate(
            [
                eight(v)
                for v in (norm1_gain, norm1_bias, query_bias, value_bias, out_bias, norm2_gain)
            ],
            axis=2,
        )
        row1 = jnp.concatenate([eight(v) for v in (norm2_bias, down_bias, up_bias)], axis=2)
        a_parts = [
            jnp.concatenate(
                [
                    full(qkv_cols).reshape(OWNERS, OWN, 3 * HW),
                    row0,
                    row1,
                    jnp.zeros((OWNERS, 14, 3 * HW), BF16),
                ],
                axis=1,
            )
        ]
        four_bits = [list(range(OWNERS))]
        ffn_bits = four_bits
        o_parts = [full(out_weight).reshape(OWNERS, OWN, WIDTH)]
        u_parts = [
            full(lax.dynamic_index_in_dim(ups, core, 1, False)).reshape(OWNERS, OWN, HALF)
        ]
        d_parts = [
            full(lax.dynamic_index_in_dim(downs, core, 1, False)).reshape(OWNERS, OWN, HALF)
        ]

    ends = jnp.cumsum(doc_lengths.reshape(-1), dtype=jnp.int32)
    zs = jnp.arange(ULY, dtype=jnp.int32) ^ z
    bs = jnp.arange(BLK, dtype=jnp.int32) ^ b
    within = jnp.arange(ROWS, dtype=jnp.int32)
    kplace = ((zs[None, :, None] * BLK + bs[:, None, None]) * ROWS + within).reshape(KEYS)
    kseg = jnp.sum((kplace[:, None] >= ends[None, :]).astype(jnp.int32), axis=1)
    valid = pad_mask.reshape(ULY, BLK, ROWS)
    valid = xor_order(xor_order(valid, 0, z), 1, b).transpose(1, 0, 2).reshape(KEYS)
    kcode = jnp.where(valid > 0, kseg, kplace + 64)
    qcodes = jnp.stack([kseg[:GROUP], kplace[:GROUP] + 64])

    q, kv, h1, w_qkv, vv = call(
        functools.partial(qkv_kernel, four_bits),
        [
            sds((GROUP, HW), BF16),
            sds((GROUP, 2 * HW), BF16),
            sds((GROUP, WIDTH), BF16),
            sds((WIDTH, 3 * HW), BF16),
            sds((OWNERS, 16, 3 * HW), BF16),
        ],
        [tab, n0, n1, n2, n3, *a_parts],
        flops=2 * GROUP * WIDTH * 3 * HW,
    )
    kv_y = swap(kv, "blk", 2)
    kv_c = swap(kv, "blk", 1)
    kv_yc = swap(kv_y, "blk", 1)
    kvs = [kv, kv_c, kv_y, kv_yc]

    *attn_slots, attn_all, lse = call(
        attend_kernel,
        [sds((ROWS, HW), BF16)] * ULY + [sds((GROUP, HW), BF16), sds((GROUP, 128), F32)],
        [tab, q, *kvs, qcodes.T, kcode[None, :]],
        flops=4 * GROUP * KEYS * HW,
    )
    attn = [attn_slots[0]] + [swap(attn_slots[k], "uly", k) for k in (1, 2, 3)]

    resid, h2, ow = call(
        functools.partial(mix_kernel, four_bits),
        [sds((ROWS, WIDTH), F32), sds((ROWS, WIDTH), BF16), sds((WIDTH, WIDTH), BF16)],
        [tab, *attn, x, vv, *o_parts],
        flops=2 * ROWS * WIDTH * WIDTH,
    )
    cb = cot.astype(BF16)
    cb_p = swap(cb, "blk", 1)
    h2_p = swap(h2, "blk", 1)
    parts = len(u_parts)
    act, dhid, yo, yp, go, gp = call(
        functools.partial(ffn_kernel, ffn_bits),
        [
            sds((2 * ROWS, HALF), BF16),
            sds((2 * ROWS, HALF), BF16),
            sds((ROWS, WIDTH), F32),
            sds((ROWS, WIDTH), BF16),
            sds((ROWS, WIDTH), F32),
            sds((ROWS, WIDTH), BF16),
        ],
        [tab, h2, h2_p, cb, cb_p, vv, *u_parts, *d_parts],
        scratch=[
            pltpu.VMEM((WIDTH, HALF), BF16),
            pltpu.VMEM((WIDTH, HALF), BF16),
            pltpu.VMEM((2 * ROWS, WIDTH), BF16),
            pltpu.VMEM((2 * ROWS, WIDTH), BF16),
            pltpu.VMEM((1, HALF), F32),
            pltpu.VMEM((2 * ROWS, WIDTH), F32),
            pltpu.VMEM((2 * ROWS, WIDTH), F32),
            pltpu.SemaphoreType.DMA((2 * OWNERS,)),
        ],
        flops=8 * 2 * ROWS * WIDTH * HALF,
        in_any=range(6, 6 + 2 * parts),
    )
    gr = swap(gp, "blk", 1)
    yr = swap(yp, "blk", 1)
    (output,) = call(output_kernel, [sds((ROWS, WIDTH), F32)], [tab, resid, yo, yr, vv])

    dres, dmix, *dattn_slots, vs2 = call(
        back_mix_kernel,
        [sds((ROWS, WIDTH), F32), sds((ROWS, WIDTH), BF16)]
        + [sds((ROWS, HW), BF16)] * ULY
        + [sds((8, WIDTH), F32)],
        [tab, resid, cot, go, gr, ow, vv],
        flops=2 * ROWS * WIDTH * WIDTH,
    )
    dattn = [dattn_slots[0]] + [swap(dattn_slots[k], "uly", k) for k in (1, 2, 3)]

    ukeep, usend, dkeep, dsend = call(
        ffn_grad_kernel,
        [sds((4, PANEL, HALF), BF16)] * 2 + [sds((4, OWN, HALF), BF16)] * 2,
        [tab, h2, h2_p, cb, cb_p, act, dhid],
        scratch=[pltpu.VMEM((WIDTH, 2 * ROWS), BF16)] * 2 + [pltpu.VMEM((OWNERS, 16, HALF), BF16)],
        flops=4 * 2 * ROWS * WIDTH * HALF,
    )
    okeep, osend = call(
        out_grad_kernel,
        [sds((4, PANEL, WIDTH), BF16)] * 2,
        [tab, *attn, dmix, vs2],
        scratch=[pltpu.VMEM((WIDTH, ROWS), BF16), pltpu.VMEM((OWNERS, 16, WIDTH), BF16)],
        flops=2 * ROWS * WIDTH * WIDTH,
    )

    dq, keep_kv, send_kv = call(
        back_attend_kernel,
        [sds((GROUP, HW), BF16), sds((2, GROUP, 2 * HW), BF16), sds((2, GROUP, 2 * HW), BF16)],
        [tab, q, *kvs, *dattn, attn_all, lse, qcodes, kcode[:, None]],
        scratch=[pltpu.VMEM((BLK, GROUP, 2 * HW), F32)],
        flops=10 * GROUP * KEYS * HW,
    )
    got = swap(send_kv, "blk", 1)
    kv_keep = add_low(keep_kv[0], got[0])
    kv_got = swap(add_low(keep_kv[1], got[1]), "blk", 2)
    dproj, g0, g1, g2, g3, vs1 = call(
        back_proj_kernel,
        [sds((GROUP, 3 * HW), BF16), sds((ROWS, WIDTH), F32)]
        + [sds((ROWS, WIDTH), BF16)] * 3
        + [sds((8, WIDTH), F32)],
        [tab, dq, kv_keep, kv_got, w_qkv, n0, n1, n2, n3],
        flops=2 * GROUP * WIDTH * 3 * HW,
    )
    qkeep, qsend = call(
        qkv_grad_kernel,
        [sds((4, PANEL, 3 * HW), BF16)] * 2,
        [tab, h1, dproj, vs1],
        scratch=[pltpu.VMEM((WIDTH, GROUP), BF16), pltpu.VMEM((OWNERS, 16, 3 * HW), BF16)],
        flops=2 * GROUP * WIDTH * 3 * HW,
    )
    g1, g2, g3 = (swap(g, "uly", k) for k, g in ((1, g1), (2, g2), (3, g3)))
    (grad_inputs,) = call(
        back_norm_kernel, [sds((ROWS, WIDTH), F32)], [tab, x, dres, g0, g1, g2, g3, vv]
    )

    if near:
        def halve(keep, send, axis, by):
            total = add_low(keep, swap(send, axis, by))
            return total

        u1 = halve(ukeep, usend, "blk", 2)
        u2 = halve(u1[:2], u1[2:], "dp", 1)
        d1 = halve(dkeep, dsend, "dp", 1)
        d2 = halve(d1[:2], d1[2:], "blk", 2)
        u_own, d_own = u2[0], d2[0]
        u_par = swap(u2[1], "blk", 1)
        d_par = swap(d2[1], "blk", 1)
        zero_rows = jnp.zeros((16, HALF), BF16)
        up_pair = jnp.stack([u_own, u_par])
        down_pair = jnp.concatenate(
            [jnp.stack([d_own, d_par]), jnp.zeros((2, 16, HALF), BF16)], axis=1
        )
        odd = (z & 1) == 1
        high = (z & 2) == 2
        got1 = swap(jnp.where(odd, up_pair, down_pair), "uly", 1)
        pair = add_low(jnp.where(odd, down_pair, up_pair), got1)
        got2 = swap(jnp.where(high, pair[0], pair[1]), "uly", 2)
        piece = add_low(jnp.where(high, pair[1], pair[0]), got2)
        back2 = swap(piece, "uly", 2)
        pair = jnp.stack([jnp.where(high, back2, piece), jnp.where(high, piece, back2)])
        back1 = swap(pair, "uly", 1)
        up_pair = jnp.where(odd, back1, pair).astype(F32)
        down_pair = jnp.where(odd, pair, back1).astype(F32)

        def ordered(pair):
            a = jnp.concatenate([pair[0, :OWN], pair[1, :OWN]], axis=1)
            c = jnp.concatenate([pair[1, :OWN], pair[0, :OWN]], axis=1)
            return jnp.where(core == 1, c, a)

        grad_up = ordered(up_pair)
        grad_downt = ordered(down_pair)
        uvec = up_pair[0, OWN] + up_pair[1, OWN]
        grad_ubias, grad_dbias = uvec[:384], uvec[384:480]

        o1 = add_low(okeep, swap(osend, "blk", 1))
        o2 = add_low(o1[:2], swap(o1[2:], "blk", 2))
        o3 = add_low(o2[0], swap(o2[1], "dp", 1))
        o4 = add_low(o3, swap(o3, "uly", 1))
        o5 = o4.astype(F32) + swap(o4, "uly", 2).astype(F32)
        grad_ow = o5[:OWN]
        grad_obias, grad_gain2, grad_shift2 = (o5[OWN, k * OWN : (k + 1) * OWN] for k in range(3))

        q1 = add_low(qkeep, swap(qsend, "blk", 1))
        q2 = add_low(q1[:2], swap(q1[2:], "blk", 2))
        q3 = add_low(q2[0], swap(q2[1], "dp", 1))
        slots = jnp.stack([q3] + [swap(q3, "uly", k) for k in (1, 2, 3)])
        qvec = jnp.sum(slots[:, OWN].astype(F32), axis=0)
        order = xor_order(slots[:, :OWN].astype(F32), 0, z)
        grad_qkv = (
            order.reshape(ULY, OWN, 3, HW).transpose(1, 2, 0, 3).reshape(OWN, 3 * WIDTH)
        )
        grad_gain1, grad_shift1, grad_qbias, grad_vbias = (
            qvec[k * OWN : (k + 1) * OWN] for k in range(4)
        )
    else:

        def owned(array):
            shard = lax.psum_scatter(
                array.astype(F32), axes, scatter_dimension=0, tiled=True
            )
            return lax.psum(shard.astype(BF16), "uly").astype(F32)

        def by_owner(keep, send, order):
            both = jnp.concatenate([keep, send], axis=0)
            return both[jnp.array(order)]

        u8 = by_owner(ukeep, usend, [0, 1, 4, 5, 2, 3, 6, 7])
        d8 = by_owner(dkeep, dsend, [0, 1, 2, 3, 4, 5, 6, 7])
        o8 = by_owner(okeep, osend, [0, 4, 2, 6, 1, 5, 3, 7])
        q8 = by_owner(qkeep, qsend, [0, 4, 2, 6, 1, 5, 3, 7])

        def widen(panel8):
            flat = panel8[:, :OWN].reshape(WIDTH, HALF)
            zero = jnp.zeros_like(flat)
            low = jnp.concatenate([flat, zero], axis=1)
            return jnp.where(core == 1, jnp.concatenate([zero, flat], axis=1), low)

        grad_up = owned(widen(u8))
        grad_downt = owned(widen(d8))
        grad_ubias = owned(u8[:, OWN, :384].reshape(FF))
        grad_dbias = owned(u8[:, OWN, 384:480].reshape(WIDTH))
        grad_ow = owned(o8[:, :OWN].reshape(WIDTH, WIDTH))
        grad_obias, grad_gain2, grad_shift2 = (
            owned(o8[:, OWN, k * OWN : (k + 1) * OWN].reshape(WIDTH)) for k in range(3)
        )
        mine = q8[:, :OWN].reshape(WIDTH, 3, 1, HW)
        spread = jnp.where(
            (jnp.arange(ULY) == z)[None, None, :, None], mine, jnp.zeros_like(mine)
        )
        grad_qkv = owned(spread.reshape(WIDTH, 3 * WIDTH))
        grad_gain1, grad_shift1, grad_qbias, grad_vbias = (
            owned(q8[:, OWN, k * OWN : (k + 1) * OWN].reshape(WIDTH)) for k in range(4)
        )

    return (
        output.reshape(inputs.shape),
        grad_inputs.reshape(inputs.shape),
        grad_qkv,
        grad_qbias,
        grad_vbias,
        grad_ow,
        grad_obias,
        grad_gain1,
        grad_shift1,
        grad_gain2,
        grad_shift2,
        grad_up,
        grad_ubias,
        grad_downt.T,
        grad_dbias,
    )


def solution(mesh):
    rows = P(None, ("dp", "uly", "blk"), None)
    first = P(("dp", "blk"), None)
    flat = P(("dp", "blk"))
    second = P(None, ("dp", "blk"))
    return jax.shard_map(
        body,
        mesh=mesh,
        in_specs=(
            rows,
            rows,
            first,
            flat,
            flat,
            first,
            flat,
            flat,
            flat,
            flat,
            flat,
            first,
            flat,
            second,
            flat,
            P(None, "dp", None),
            P(None, "dp"),
        ),
        out_specs=(
            rows,
            rows,
            first,
            flat,
            flat,
            first,
            flat,
            flat,
            flat,
            flat,
            flat,
            first,
            flat,
            second,
            flat,
        ),
        check_vma=False,
    )
```

```python
import functools

import jax
import jax.numpy as jnp
from jax import lax
from jax.experimental import pallas as pl
from jax.experimental.pallas import tpu as pltpu
from jax.sharding import PartitionSpec as P

HEADS = 12
HEAD_DIM = 64
FF = 3072
F32 = jnp.float32
BF16 = jnp.bfloat16
NEG = -1e30
VMEM_LIMIT = 60 * 1024 * 1024

ROWS = 128
ULY = 4
BLK = 4
GROUP = ROWS * ULY
KEYS = GROUP * BLK
WIDTH = HEADS * HEAD_DIM
HW = WIDTH // ULY
LOCAL_HEADS = HEADS // ULY
OWNERS = 8
OWN = WIDTH // OWNERS
PANEL = OWN + 16
QUART = FF // BLK
COST = 1


def swap(array, axis, by):
    peers = lax.axis_size(axis)
    return lax.ppermute(array, axis, [(i, i ^ by) for i in range(peers)])


def vm():
    return pl.BlockSpec(memory_space=pltpu.VMEM)


def anyspace():
    return pl.BlockSpec(memory_space=pl.ANY)


def smem():
    return pl.BlockSpec(memory_space=pltpu.SMEM)


def call(kernel, outs, args, scratch=(), flops=0, in_any=()):
    specs = [smem()] + [anyspace() if i in in_any else vm() for i in range(1, len(args))]
    nbytes = sum(a.size * a.dtype.itemsize for a in args) + sum(
        o.size * o.dtype.itemsize for o in outs
    )
    return pl.pallas_call(
        kernel,
        out_shape=outs,
        in_specs=specs,
        out_specs=[vm() for _ in outs],
        scratch_shapes=list(scratch),
        cost_estimate=pl.CostEstimate(
            flops=flops // COST, bytes_accessed=nbytes // COST, transcendentals=0
        ),
        compiler_params=pltpu.CompilerParams(vmem_limit_bytes=VMEM_LIMIT),
    )(*args)


def sds(shape, dtype):
    return jax.ShapeDtypeStruct(shape, dtype)


def nn(a, b):
    return lax.dot_general(a, b, (((1,), (0,)), ((), ())), preferred_element_type=F32)


def nt(a, b):
    return lax.dot_general(a, b, (((1,), (1,)), ((), ())), preferred_element_type=F32)


def tn(a, b):
    return lax.dot_general(a, b, (((0,), (0,)), ((), ())), preferred_element_type=F32)


def rows_at(index, size):
    return pl.ds(pl.multiple_of(index * size, 32), size)


def vec(vv_ref, row, lane):
    return jnp.concatenate(
        [vv_ref[o].astype(F32)[row : row + 1, lane : lane + OWN] for o in range(OWNERS)], axis=1
    )


def norm_stats(v):
    mean = jnp.mean(v, axis=-1, keepdims=True)
    cen = v - mean
    var = jnp.mean(cen * cen, axis=-1, keepdims=True)
    r = lax.rsqrt(var + 1e-12)
    return cen * r, r


def norm_kernel(tab, x_ref, n_ref):
    n_ref[...] = norm_stats(x_ref[...])[0].astype(BF16)


def prep_kernel(tab, x_ref, w_ref, rows_ref, n_ref, panel_ref):
    z = tab[1]
    panel_ref[OWN:, :] = rows_ref[...]
    for k in range(ULY):

        @pl.when(z == k)
        def _():
            parts = [w_ref[:, p * WIDTH + k * HW : p * WIDTH + (k + 1) * HW] for p in range(3)]
            panel_ref[:OWN, :] = jnp.concatenate(parts, axis=1)

    n_ref[...] = norm_stats(x_ref[...])[0].astype(BF16)


def quarter(index):
    return pl.ds(pl.multiple_of(index * QUART, 128), QUART)


def ffn_prep_kernel(tab, u_ref, d_ref, a_ref, b_ref, turned):
    b = tab[3]
    for q in range(BLK):
        part = d_ref[q * QUART : (q + 1) * QUART, :]
        turned[q] = part.astype(F32).T.astype(BF16)
    for s in range(BLK):
        q = jnp.bitwise_xor(b, s)
        ref = (a_ref, b_ref)[s // 2]
        ref[s % 2, 0] = u_ref[:, quarter(q)]
        ref[s % 2, 1] = turned[q]


def qkv_kernel(owner_bits, tab, n0, n1, n2, n3, *rest):
    arrays = rest[: len(owner_bits)]
    q_ref, kv_ref, h_ref, w_ref, vv_ref = rest[len(owner_bits) :]
    me, z = tab[0], tab[1]
    for ref, bits in zip(arrays, owner_bits):
        for i, bit in enumerate(bits):
            o = jnp.bitwise_xor(me, bit)
            w_ref[rows_at(o, OWN), :] = ref[i, :OWN, :]
            vv_ref[o] = ref[i, OWN:PANEL, :]
    gain = vec(vv_ref, 0, 0)
    shift = vec(vv_ref, 0, OWN)
    lo = vv_ref[2 * z].astype(F32)
    hi = vv_ref[2 * z + 1].astype(F32)
    zero = jnp.zeros((1, HW), F32)
    bias = jnp.concatenate(
        [
            lo[0:1, 2 * OWN : 3 * OWN],
            hi[0:1, 2 * OWN : 3 * OWN],
            zero,
            lo[0:1, 3 * OWN : 4 * OWN],
            hi[0:1, 3 * OWN : 4 * OWN],
        ],
        axis=1,
    )
    for i, ref in enumerate((n0, n1, n2, n3)):
        rows = slice(i * ROWS, (i + 1) * ROWS)
        h = (ref[...].astype(F32) * gain + shift).astype(BF16)
        h_ref[rows, :] = h
        proj = (nn(h, w_ref[...]) + bias).astype(BF16)
        q_ref[rows, :] = proj[:, :HW] * jnp.asarray(HEAD_DIM ** (-0.5), BF16)
        kv_ref[rows, :] = proj[:, HW:]


def placed(piece, upper):
    zero = jnp.zeros_like(piece)
    return jnp.concatenate([zero, piece] if upper else [piece, zero], axis=1)


def head_cols(h):
    return slice(h * HEAD_DIM, (h + 1) * HEAD_DIM)


def window(index):
    lane = index * HEAD_DIM
    start = lane // 128 * 128
    return slice(start, start + 128), (lane % 128) >= 64


def attend_kernel(tab, q_ref, k0, k1, k2, k3, qc_ref, kc_ref, o0, o1, o2, o3, all_ref, lse_ref):
    kvs = (k0, k1, k2, k3)
    outs = (o0, o1, o2, o3)

    lane = lax.broadcasted_iota(jnp.int32, (ROWS, 128), 1)

    def step(i, carry):
        rows = rows_at(i, ROWS)
        code1 = qc_ref[rows, 0:1]
        code2 = qc_ref[rows, 1:2]
        masks = []
        for j in range(BLK):
            kc = kc_ref[0:1, j * GROUP : (j + 1) * GROUP]
            masks.append((kc == code1) | (kc == code2))
        heads = []
        lse = jnp.zeros((ROWS, 128), F32)
        for h in range(LOCAL_HEADS):
            kwin, kup = window(h)
            vwin, vup = window(LOCAL_HEADS + h)
            qp = placed(q_ref[rows, head_cols(h)], kup)
            scores = [
                jnp.where(masks[j], nt(qp, kvs[j][:, kwin]), NEG) for j in range(BLK)
            ]
            top = functools.reduce(jnp.maximum, [jnp.max(s, axis=1, keepdims=True) for s in scores])
            total = jnp.zeros((ROWS, 1), F32)
            acc = jnp.zeros((ROWS, 128), F32)
            for j in range(BLK):
                e = jnp.exp(scores[j] - top)
                total = total + jnp.sum(e, axis=1, keepdims=True)
                acc = acc + nn(e.astype(BF16), kvs[j][:, vwin])
            acc = acc[:, 64:] if vup else acc[:, :64]
            heads.append((acc / total).astype(BF16))
            lse = jnp.where(lane == h, top + jnp.log(total), lse)
        all_ref[rows, :] = jnp.concatenate(heads, axis=1)
        lse_ref[rows, :] = lse
        return carry

    lax.fori_loop(0, ULY, step, 0)
    for i in range(ULY):
        outs[i][...] = all_ref[i * ROWS : (i + 1) * ROWS, :]


def mix_kernel(owner_bits, tab, a0, a1, a2, a3, x_ref, vv_ref, *rest):
    arrays = rest[: len(owner_bits)]
    resid_ref, h_ref, ow_ref = rest[len(owner_bits) :]
    me, z = tab[0], tab[1]
    for ref, bits in zip(arrays, owner_bits):
        for i, bit in enumerate(bits):
            ow_ref[rows_at(jnp.bitwise_xor(me, bit), OWN), :] = ref[i]
    acc = x_ref[...] + vec(vv_ref, 0, 4 * OWN)
    for j, ref in enumerate((a0, a1, a2, a3)):
        acc = acc + nn(ref[...], ow_ref[rows_at(jnp.bitwise_xor(z, j), HW), :])
    resid_ref[...] = acc
    n, _ = norm_stats(acc)
    h_ref[...] = (n * vec(vv_ref, 0, 5 * OWN) + vec(vv_ref, 1, 0)).astype(BF16)


CHUNK = 256


def ffn_kernel(plan, tab, h0, h1, h2, h3, c0, c1, c2, c3, vv_ref, *rest):
    count = 1 + max(index for index, _, _ in plan)
    parts = rest[:count]
    act_ref, dhid_ref, yo_ref, y1, y2, y3, go_ref, g1, g2, g3 = rest[count : count + 10]
    u_ref, d_ref, hall, call_ref, bias_ref, yacc, gacc, sems = rest[count + 10 :]
    me, b = tab[0], tab[3]
    copies = []
    for index, slot, bit in plan:
        rows = rows_at(jnp.bitwise_xor(me, bit), OWN)
        for k, target in enumerate((u_ref, d_ref)):
            copy = pltpu.make_async_copy(
                parts[index].at[slot, k], target.at[rows, :], sems.at[len(copies)]
            )
            copy.start()
            copies.append(copy)
    for i, (h_ref, c_ref) in enumerate(((h0, c0), (h1, c1), (h2, c2), (h3, c3))):
        rows = slice(i * ROWS, (i + 1) * ROWS)
        hall[rows, :] = h_ref[...]
        call_ref[rows, :] = c_ref[...]
    for k in range(2):
        bias_ref[:, k * 384 : (k + 1) * 384] = vv_ref[2 * b + k].astype(F32)[1:2, 192:576]
    yacc[...] = jnp.zeros_like(yacc)
    gacc[...] = jnp.zeros_like(gacc)
    for copy in copies:
        copy.wait()

    def step(k, carry):
        cols = pl.ds(pl.multiple_of(k * CHUNK, CHUNK), CHUNK)
        hid = nn(hall[...], u_ref[:, cols]) + bias_ref[:, cols]
        dact = nn(call_ref[...], d_ref[:, cols])
        cdf = 0.5 * (1.0 + lax.erf(hid * 0.7071067811865476))
        act = (hid * cdf).astype(BF16)
        pdf = jnp.exp(-0.5 * hid * hid) * 0.3989422804014327
        dhid = (dact * (cdf + hid * pdf)).astype(BF16)
        act_ref[:, cols] = act
        dhid_ref[:, cols] = dhid
        yacc[...] += nt(act, d_ref[:, cols])
        gacc[...] += nt(dhid, u_ref[:, cols])
        return carry

    lax.fori_loop(0, QUART // CHUNK, step, 0)
    yo_ref[...] = yacc[:ROWS, :]
    go_ref[...] = gacc[:ROWS, :]
    for i, (y_ref, g_ref) in enumerate(((y1, g1), (y2, g2), (y3, g3)), 1):
        rows = slice(i * ROWS, (i + 1) * ROWS)
        y_ref[...] = yacc[rows, :].astype(BF16)
        g_ref[...] = gacc[rows, :].astype(BF16)


def ffn_grad_kernel(tab, r0, r1, r2, r3, right_ref, keep, send, left):
    me = tab[0]
    for i, ref in enumerate((r0, r1, r2, r3)):
        left[:, i * ROWS : (i + 1) * ROWS] = ref[...].T
    for ref, base in ((send, 4), (keep, 0)):
        for s in range(BLK):
            o = jnp.bitwise_xor(me, base + s)
            ref[s] = nn(left[rows_at(o, OWN), :], right_ref[...]).astype(BF16)


def back_mix_kernel(
    tab, resid_ref, cot_ref, go_ref, g1, g2, g3, ow_ref, vv_ref, dres_ref, dmix_ref, d0, d1, d2, d3, vs_ref
):
    z = tab[1]
    grad = go_ref[...] + g1[...].astype(F32) + g2[...].astype(F32) + g3[...].astype(F32)
    n, r = norm_stats(resid_ref[...])
    dn = grad * vec(vv_ref, 0, 5 * OWN)
    dres = cot_ref[...] + r * (
        dn
        - jnp.mean(dn, axis=-1, keepdims=True)
        - n * jnp.mean(dn * n, axis=-1, keepdims=True)
    )
    dres_ref[...] = dres
    dmix = dres.astype(BF16)
    dmix_ref[...] = dmix
    for j, ref in enumerate((d0, d1, d2, d3)):
        ref[...] = nt(dmix, ow_ref[rows_at(jnp.bitwise_xor(z, j), HW), :]).astype(BF16)
    vs_ref[0:1, :] = jnp.sum(dmix.astype(F32), axis=0, keepdims=True)
    vs_ref[1:2, :] = jnp.sum(grad * n, axis=0, keepdims=True)
    vs_ref[2:3, :] = jnp.sum(grad, axis=0, keepdims=True)
    vs_ref[3:8, :] = jnp.zeros((5, WIDTH), F32)


def out_grad_kernel(tab, a0, a1, a2, a3, dmix_ref, vs_ref, dhid_ref, c_ref, keep, send, left, vrow):
    me, z, b = tab[0], tab[1], tab[3]
    for j, ref in enumerate((a0, a1, a2, a3)):
        left[rows_at(jnp.bitwise_xor(z, j), HW), :] = ref[...].astype(F32).T.astype(BF16)
    vs = vs_ref[...]
    usum = jnp.sum(dhid_ref[...].astype(F32), axis=0, keepdims=True)
    csum = jnp.sum(c_ref[...].astype(F32), axis=0, keepdims=True)
    for o in range(OWNERS):
        part = usum[:, (o % 2) * 384 : (o % 2 + 1) * 384]
        row = jnp.concatenate(
            [vs[k : k + 1, o * OWN : (o + 1) * OWN] for k in range(3)]
            + [jnp.where(b == o // 2, part, 0.0), csum[:, o * OWN : (o + 1) * OWN]],
            axis=1,
        )
        vrow[o] = jnp.broadcast_to(row, (16, WIDTH)).astype(BF16)
    for ref, base in ((send, 1), (keep, 0)):
        for s in range(4):
            o = jnp.bitwise_xor(me, base + (s // 2) * 2 + (s % 2) * 4)
            ref[s, :OWN, :] = nn(left[rows_at(o, OWN), :], dmix_ref[...]).astype(BF16)
            ref[s, OWN:, :] = vrow[o]


def back_attend_kernel(
    tab,
    q_ref,
    k0,
    k1,
    k2,
    k3,
    g0,
    g1,
    g2,
    g3,
    all_ref,
    lse_ref,
    qr_ref,
    kcol_ref,
    dq_ref,
    keep,
    send,
    acc,
    gall,
):
    kvs = (k0, k1, k2, k3)
    acc[...] = jnp.zeros_like(acc)
    for i, g_ref in enumerate((g0, g1, g2, g3)):
        gall[i * ROWS : (i + 1) * ROWS, :] = g_ref[...]
    lane = lax.broadcasted_iota(jnp.int32, (ROWS, 128), 1)

    def step(i, carry):
        rows = rows_at(i, ROWS)
        prod = gall[rows, :].astype(F32) * all_ref[rows, :].astype(F32)
        stat = jnp.zeros((ROWS, 128), F32)
        for h in range(LOCAL_HEADS):
            stat = jnp.where(
                lane == h, jnp.sum(prod[:, head_cols(h)], axis=1, keepdims=True), stat
            )
        rowdot = stat.T
        lse = lse_ref[rows, :].T
        code1 = qr_ref[0:1, rows]
        code2 = qr_ref[1:2, rows]
        dq = [jnp.zeros((ROWS, 128), F32) for _ in range(LOCAL_HEADS)]
        for j in range(BLK):
            kc = kcol_ref[j * GROUP : (j + 1) * GROUP, :]
            mask = (kc == code1) | (kc == code2)
            for h in range(LOCAL_HEADS):
                kwin, kup = window(h)
                vwin, vup = window(LOCAL_HEADS + h)
                qp = placed(q_ref[rows, head_cols(h)], kup)
                gp = placed(gall[rows, head_cols(h)], vup)
                kk = kvs[j][:, kwin]
                scores = nt(kk, qp)
                p = jnp.where(mask, jnp.exp(scores - lse[h : h + 1, :]), 0.0)
                dp = nt(kvs[j][:, vwin], gp)
                ds = (p * (dp - rowdot[h : h + 1, :])).astype(BF16)
                acc[j, :, vwin] += nn(p.astype(BF16), gp)
                acc[j, :, kwin] += nn(ds, qp)
                dq[h] = dq[h] + tn(ds, kk)
        parts = []
        for h in range(LOCAL_HEADS):
            _, kup = window(h)
            parts.append(dq[h][:, 64:] if kup else dq[h][:, :64])
        dq_ref[rows, :] = (jnp.concatenate(parts, axis=1) * HEAD_DIM ** (-0.5)).astype(BF16)
        return carry

    lax.fori_loop(0, ULY, step, 0)
    keep[0] = acc[0].astype(BF16)
    keep[1] = acc[2].astype(BF16)
    send[0] = acc[1].astype(BF16)
    send[1] = acc[3].astype(BF16)


def back_proj_kernel(
    tab, dq_ref, keep, recv, w_ref, n0, n1, n2, n3, dproj_ref, h0, h1, h2, h3, vs_ref
):
    dproj_ref[:, :HW] = dq_ref[...]
    dproj_ref[:, HW:] = (keep[...].astype(F32) + recv[...].astype(F32)).astype(BF16)
    gain = jnp.zeros((1, WIDTH), F32)
    shift = jnp.zeros((1, WIDTH), F32)
    for i, (n_ref, out) in enumerate(((n0, h0), (n1, h1), (n2, h2), (n3, h3))):
        rows = slice(i * ROWS, (i + 1) * ROWS)
        grad = nt(dproj_ref[rows, :], w_ref[...])
        out[...] = grad.astype(out.dtype)
        gain = gain + jnp.sum(grad * n_ref[...].astype(F32), axis=0, keepdims=True)
        shift = shift + jnp.sum(grad, axis=0, keepdims=True)
    vs_ref[0:1, :] = gain
    vs_ref[1:2, :] = shift
    cols = jnp.sum(dproj_ref[...].astype(F32), axis=0, keepdims=True)
    vs_ref[2:3, :] = jnp.concatenate([cols, jnp.zeros((1, WIDTH - 3 * HW), F32)], axis=1)
    vs_ref[3:8, :] = jnp.zeros((5, WIDTH), F32)


def qkv_grad_kernel(tab, h_ref, dproj_ref, vs_ref, keep, send, left, vrow):
    me, z = tab[0], tab[1]
    vs = vs_ref[...]
    for o in range(OWNERS):
        row = [vs[k : k + 1, o * OWN : (o + 1) * OWN] for k in range(2)]
        for lane in (0, 2 * HW):
            lane = lane + (o % 2) * OWN
            row.append(jnp.where(z == o // 2, vs[2:3, lane : lane + OWN], 0.0))
        row.append(jnp.zeros((1, 3 * HW - 4 * OWN), F32))
        vrow[o] = jnp.broadcast_to(jnp.concatenate(row, axis=1), (16, 3 * HW)).astype(BF16)
    for i in range(ULY):
        rows = slice(i * ROWS, (i + 1) * ROWS)
        left[:, rows] = h_ref[rows, :].T
    for ref, base in ((keep, 0), (send, 1)):
        for s in range(4):
            o = jnp.bitwise_xor(me, base + (s // 2) * 2 + (s % 2) * 4)
            ref[s, :OWN, :] = nn(left[rows_at(o, OWN), :], dproj_ref[...]).astype(BF16)
            ref[s, OWN:, :] = vrow[o]


def back_norm_kernel(tab, x_ref, dres_ref, h0, h1, h2, h3, vv_ref, out_ref):
    grad = h0[...] + h1[...].astype(F32) + h2[...].astype(F32) + h3[...].astype(F32)
    n, r = norm_stats(x_ref[...])
    dn = grad * vec(vv_ref, 0, 0)
    out_ref[...] = dres_ref[...] + r * (
        dn
        - jnp.mean(dn, axis=-1, keepdims=True)
        - n * jnp.mean(dn * n, axis=-1, keepdims=True)
    )


def output_kernel(tab, resid_ref, yo_ref, y1, y2, y3, vv_ref, out_ref):
    got = y1[...].astype(F32) + y2[...].astype(F32) + y3[...].astype(F32)
    out_ref[...] = resid_ref[...] + yo_ref[...] + got + vec(vv_ref, 1, OWN)


def low_sum(a, b):
    return (a.astype(F32) + b.astype(F32)).astype(BF16)


def split_kernel(bit, tab, a_ref, ac_ref, by_ref, byc_ref, keep, send):
    for value, low_out, high_out in ((0, keep, send), (1, send, keep)):

        @pl.when(tab[bit] == value)
        def _():
            low_out[0] = a_ref[0]
            low_out[1] = ac_ref[1]
            high_out[0] = by_ref[0]
            high_out[1] = byc_ref[1]


def merge_kernel(bit, tab, a_ref, b_ref, keep, send):
    for value, low_out, high_out in ((0, keep, send), (1, send, keep)):

        @pl.when(tab[bit] == value)
        def _():
            low_out[...] = low_sum(a_ref[0], b_ref[0])
            high_out[...] = low_sum(a_ref[1], b_ref[1])


def up_final_kernel(tab, p0, p1, p2, p3, out_ref):
    b, odd, high = tab[3], tab[4], tab[5]
    for flip, ref in ((0, p0), (2, p1), (1, p2), (3, p3)):
        q = jnp.bitwise_xor(jnp.bitwise_xor(b, 2 * odd + high), flip)
        out_ref[:, quarter(q)] = ref[...].astype(F32)


def down_final_kernel(tab, p0, p1, p2, p3, out_ref):
    b, odd, high = tab[3], tab[4], tab[5]
    for flip, ref in ((0, p0), (1, p1), (2, p2), (3, p3)):
        q = jnp.bitwise_xor(jnp.bitwise_xor(b, 2 * high + odd), flip)
        out_ref[quarter(q), :] = ref[...].astype(F32).T


def qkv_final_kernel(tab, p0, p1, p2, p3, out_ref, vec_ref):
    z = tab[1]
    refs = (p0, p1, p2, p3)
    for k in range(ULY):

        @pl.when(z == k)
        def _():
            for p in range(3):
                cols = [
                    refs[t ^ k][:OWN, p * HW : (p + 1) * HW].astype(F32) for t in range(ULY)
                ]
                out_ref[:, p * WIDTH : (p + 1) * WIDTH] = jnp.concatenate(cols, axis=1)

    total = jnp.zeros((16, 3 * HW), F32)
    for ref in refs:
        total = total + ref[OWN:, :].astype(F32)
    vec_ref[...] = total[:8, :]


def add_low(a, b):
    return (a.astype(F32) + b.astype(F32)).astype(BF16)


def xor_order(array, axis, index):
    shape = array.shape
    two = array.reshape(shape[:axis] + (2, 2) + shape[axis + 1 :])
    two = jnp.where((index & 1) == 1, jnp.flip(two, axis + 1), two)
    two = jnp.where((index & 2) == 2, jnp.flip(two, axis), two)
    return two.reshape(shape)


def body(
    inputs,
    cotangent,
    qkv_weight,
    query_bias,
    value_bias,
    out_weight,
    out_bias,
    norm1_gain,
    norm1_bias,
    norm2_gain,
    norm2_bias,
    up_weight,
    up_bias,
    down_weight,
    down_bias,
    doc_lengths,
    pad_mask,
):
    dp_count = lax.axis_size("dp")
    near = dp_count == 2
    dp = lax.axis_index("dp")
    z = lax.axis_index("uly")
    b = lax.axis_index("blk")
    core = b & 1
    rank = dp * BLK + b
    me = rank if near else jnp.int32(0)
    tab = jnp.stack([me, z, core, b, z & 1, z >> 1]).astype(jnp.int32)
    own_rows = WIDTH // (dp_count * BLK)
    axes = ("dp", "blk")

    x = inputs.reshape(ROWS, WIDTH)
    cot = cotangent.reshape(ROWS, WIDTH)

    if near:
        row0 = jnp.concatenate(
            [norm1_gain, norm1_bias, query_bias, value_bias, out_bias, norm2_gain]
        )
        row1 = jnp.concatenate([norm2_bias, down_bias, up_bias])
        vec_rows = jnp.concatenate(
            [row0[None], row1[None], jnp.zeros((14, 3 * HW), BF16)], axis=0
        )
        n0, panel = call(
            prep_kernel,
            [sds((ROWS, WIDTH), BF16), sds((PANEL, 3 * HW), BF16)],
            [tab, x, qkv_weight, vec_rows],
        )

        def spread(array):
            far = swap(array, "dp", 1)
            near_y = swap(array, "blk", 2)
            far_y = swap(far, "blk", 2)
            direct = [array, near_y, far, far_y]
            return direct + [swap(a, "blk", 1) for a in direct]

        a_parts = [a[None] for a in spread(panel)]
        o_parts = [a[None] for a in spread(out_weight)]
        four_bits = [[0], [2], [4], [6], [1], [3], [5], [7]]
        w_a, w_b = call(
            ffn_prep_kernel,
            [sds((2, 2, OWN, QUART), BF16)] * 2,
            [tab, up_weight, down_weight],
            scratch=[pltpu.VMEM((BLK, OWN, QUART), BF16)],
        )
        w_ax, w_bx = swap(w_a, "dp", 1), swap(w_b, "dp", 1)
        w_by, w_bxy = swap(w_b, "blk", 2), swap(w_bx, "blk", 2)
        w_parts = [w_a, w_by, w_ax, w_bxy]
        w_parts = w_parts + [swap(a, "blk", 1) for a in w_parts]
        w_plan = [
            (0, 0, 0), (1, 0, 2), (2, 0, 4), (3, 0, 6), (4, 1, 1), (5, 1, 3), (6, 1, 5), (7, 1, 7)
        ]
    else:
        (n0,) = call(norm_kernel, [sds((ROWS, WIDTH), BF16)], [tab, x])
        qkv_cols = lax.dynamic_index_in_dim(
            qkv_weight.reshape(own_rows, 3, ULY, HW), z, axis=2, keepdims=False
        ).reshape(own_rows, 3 * HW)

        def full(array):
            return lax.all_gather(array, axes, axis=0, tiled=True)

        def eight(vector):
            return full(vector).reshape(OWNERS, 1, -1)

        def mine(array):
            cols = full(array).reshape(WIDTH, BLK, QUART)
            return lax.dynamic_index_in_dim(cols, b, 1, False).reshape(OWNERS, OWN, QUART)

        row0 = jnp.concatenate(
            [
                eight(v)
                for v in (norm1_gain, norm1_bias, query_bias, value_bias, out_bias, norm2_gain)
            ],
            axis=2,
        )
        row1 = jnp.concatenate([eight(v) for v in (norm2_bias, down_bias, up_bias)], axis=2)
        a_parts = [
            jnp.concatenate(
                [
                    full(qkv_cols).reshape(OWNERS, OWN, 3 * HW),
                    row0,
                    row1,
                    jnp.zeros((OWNERS, 14, 3 * HW), BF16),
                ],
                axis=1,
            )
        ]
        four_bits = [list(range(OWNERS))]
        o_parts = [full(out_weight).reshape(OWNERS, OWN, WIDTH)]
        w_parts = [jnp.stack([mine(up_weight), mine(down_weight.T)], axis=1)]
        w_plan = [(0, o, o) for o in range(OWNERS)]
    n1, n2, n3 = (swap(n0, "uly", k) for k in (1, 2, 3))

    ends = jnp.cumsum(doc_lengths.reshape(-1), dtype=jnp.int32)
    zs = jnp.arange(ULY, dtype=jnp.int32) ^ z
    bs = jnp.arange(BLK, dtype=jnp.int32) ^ b
    within = jnp.arange(ROWS, dtype=jnp.int32)
    kplace = ((zs[None, :, None] * BLK + bs[:, None, None]) * ROWS + within).reshape(KEYS)
    kseg = jnp.sum((kplace[:, None] >= ends[None, :]).astype(jnp.int32), axis=1)
    valid = pad_mask.reshape(ULY, BLK, ROWS)
    valid = xor_order(xor_order(valid, 0, z), 1, b).transpose(1, 0, 2).reshape(KEYS)
    kcode = jnp.where(valid > 0, kseg, kplace + 64)
    qcodes = jnp.stack([kseg[:GROUP], kplace[:GROUP] + 64])

    q, kv, h1, w_qkv, vv = call(
        functools.partial(qkv_kernel, four_bits),
        [
            sds((GROUP, HW), BF16),
            sds((GROUP, 2 * HW), BF16),
            sds((GROUP, WIDTH), BF16),
            sds((WIDTH, 3 * HW), BF16),
            sds((OWNERS, 16, 3 * HW), BF16),
        ],
        [tab, n0, n1, n2, n3, *a_parts],
        flops=2 * GROUP * WIDTH * 3 * HW,
    )
    kv_y = swap(kv, "blk", 2)
    kv_c = swap(kv, "blk", 1)
    kv_yc = swap(kv_y, "blk", 1)
    kvs = [kv, kv_c, kv_y, kv_yc]

    *attn_slots, attn_all, lse = call(
        attend_kernel,
        [sds((ROWS, HW), BF16)] * ULY + [sds((GROUP, HW), BF16), sds((GROUP, 128), F32)],
        [tab, q, *kvs, qcodes.T, kcode[None, :]],
        flops=4 * GROUP * KEYS * HW,
    )
    attn = [attn_slots[0]] + [swap(attn_slots[k], "uly", k) for k in (1, 2, 3)]

    resid, h2, ow = call(
        functools.partial(mix_kernel, four_bits),
        [sds((ROWS, WIDTH), F32), sds((ROWS, WIDTH), BF16), sds((WIDTH, WIDTH), BF16)],
        [tab, *attn, x, vv, *o_parts],
        flops=2 * ROWS * WIDTH * WIDTH,
    )
    cb = cot.astype(BF16)

    def around(array):
        near_y = swap(array, "blk", 2)
        return [array, swap(array, "blk", 1), near_y, swap(near_y, "blk", 1)]

    cbs = around(cb)
    h2s = around(h2)
    parts = len(w_parts)
    act, dhid, yo, *sums = call(
        functools.partial(ffn_kernel, w_plan),
        [sds((GROUP, QUART), BF16)] * 2
        + ([sds((ROWS, WIDTH), F32)] + [sds((ROWS, WIDTH), BF16)] * 3) * 2,
        [tab, *h2s, *cbs, vv, *w_parts],
        scratch=[
            pltpu.VMEM((WIDTH, QUART), BF16),
            pltpu.VMEM((WIDTH, QUART), BF16),
            pltpu.VMEM((GROUP, WIDTH), BF16),
            pltpu.VMEM((GROUP, WIDTH), BF16),
            pltpu.VMEM((1, QUART), F32),
            pltpu.VMEM((GROUP, WIDTH), F32),
            pltpu.VMEM((GROUP, WIDTH), F32),
            pltpu.SemaphoreType.DMA((2 * OWNERS,)),
        ],
        flops=8 * GROUP * WIDTH * QUART,
        in_any=range(10, 10 + parts),
    )
    ys, go, gs = sums[:3], sums[3], sums[4:]
    gs = [swap(g, "blk", k) for k, g in ((1, gs[0]), (2, gs[1]), (3, gs[2]))]
    ys = [swap(y, "blk", k) for k, y in ((1, ys[0]), (2, ys[1]), (3, ys[2]))]
    (output,) = call(output_kernel, [sds((ROWS, WIDTH), F32)], [tab, resid, yo, *ys, vv])

    dres, dmix, *dattn_slots, vs2 = call(
        back_mix_kernel,
        [sds((ROWS, WIDTH), F32), sds((ROWS, WIDTH), BF16)]
        + [sds((ROWS, HW), BF16)] * ULY
        + [sds((8, WIDTH), F32)],
        [tab, resid, cot, go, *gs, ow, vv],
        flops=2 * ROWS * WIDTH * WIDTH,
    )
    dattn = [dattn_slots[0]] + [swap(dattn_slots[k], "uly", k) for k in (1, 2, 3)]

    def panel_grad(rows, right):
        return call(
            ffn_grad_kernel,
            [sds((BLK, OWN, QUART), BF16)] * 2,
            [tab, *rows, right],
            scratch=[pltpu.VMEM((WIDTH, GROUP), BF16)],
            flops=2 * GROUP * WIDTH * QUART,
        )

    ukeep, usend = panel_grad(h2s, dhid)
    dkeep, dsend = panel_grad(cbs, act)
    okeep, osend = call(
        out_grad_kernel,
        [sds((4, PANEL, WIDTH), BF16)] * 2,
        [tab, *attn, dmix, vs2, dhid, cb],
        scratch=[pltpu.VMEM((WIDTH, ROWS), BF16), pltpu.VMEM((OWNERS, 16, WIDTH), BF16)],
        flops=2 * ROWS * WIDTH * WIDTH,
    )

    dq, keep_kv, send_kv = call(
        back_attend_kernel,
        [sds((GROUP, HW), BF16), sds((2, GROUP, 2 * HW), BF16), sds((2, GROUP, 2 * HW), BF16)],
        [tab, q, *kvs, *dattn, attn_all, lse, qcodes, kcode[:, None]],
        scratch=[pltpu.VMEM((BLK, GROUP, 2 * HW), F32), pltpu.VMEM((GROUP, HW), BF16)],
        flops=10 * GROUP * KEYS * HW,
    )
    got = swap(send_kv, "blk", 1)
    kv_keep = add_low(keep_kv[0], got[0])
    kv_got = swap(add_low(keep_kv[1], got[1]), "blk", 2)
    dproj, g0, g1, g2, g3, vs1 = call(
        back_proj_kernel,
        [sds((GROUP, 3 * HW), BF16), sds((ROWS, WIDTH), F32)]
        + [sds((ROWS, WIDTH), BF16)] * 3
        + [sds((8, WIDTH), F32)],
        [tab, dq, kv_keep, kv_got, w_qkv, n0, n1, n2, n3],
        flops=2 * GROUP * WIDTH * 3 * HW,
    )
    qkeep, qsend = call(
        qkv_grad_kernel,
        [sds((4, PANEL, 3 * HW), BF16)] * 2,
        [tab, h1, dproj, vs1],
        scratch=[pltpu.VMEM((WIDTH, GROUP), BF16), pltpu.VMEM((OWNERS, 16, 3 * HW), BF16)],
        flops=2 * GROUP * WIDTH * 3 * HW,
    )
    g1, g2, g3 = (swap(g, "uly", k) for k, g in ((1, g1), (2, g2), (3, g3)))
    (grad_inputs,) = call(
        back_norm_kernel, [sds((ROWS, WIDTH), F32)], [tab, x, dres, g0, g1, g2, g3, vv]
    )

    if near:
        def owned_panel(keep, send, first, second, final, shape):
            got = swap(send, "dp", 1)
            there = add_low(keep[2:], got[2:])
            here = add_low(keep[:2], got[:2])
            there = swap(there, "blk", 2)
            pieces = [here, swap(here, "blk", 1), there, swap(there, "blk", 1)]
            pair = sds((2, OWN, QUART), BF16)
            one = sds((OWN, QUART), BF16)
            steps = {1: 4, 2: 5}
            kept, sent = call(
                functools.partial(split_kernel, steps[first]), [pair] * 2, [tab, *pieces]
            )
            kept, sent = call(
                functools.partial(merge_kernel, steps[second]),
                [one] * 2,
                [tab, kept, swap(sent, "uly", first)],
            )
            total = add_low(kept, swap(sent, "uly", second))
            two = swap(total, "uly", 2)
            sums = [total, swap(total, "uly", 1), two, swap(two, "uly", 1)]
            return call(final, [sds(shape, F32)], [tab, *sums])[0]

        grad_up = owned_panel(ukeep, usend, 1, 2, up_final_kernel, (OWN, FF))
        grad_down = owned_panel(dkeep, dsend, 2, 1, down_final_kernel, (FF, OWN))

        o1 = add_low(okeep, swap(osend, "blk", 1))
        o2 = add_low(o1[:2], swap(o1[2:], "blk", 2))
        o3 = add_low(o2[0], swap(o2[1], "dp", 1))
        o4 = add_low(o3, swap(o3, "uly", 1))
        o5 = o4.astype(F32) + swap(o4, "uly", 2).astype(F32)
        grad_ow = o5[:OWN]
        grad_obias, grad_gain2, grad_shift2 = (o5[OWN, k * OWN : (k + 1) * OWN] for k in range(3))
        grad_ubias, grad_dbias = o5[OWN, 288:672], o5[OWN, 672:768]

        q1 = add_low(qkeep, swap(qsend, "blk", 1))
        q2 = add_low(q1[:2], swap(q1[2:], "blk", 2))
        q3 = add_low(q2[0], swap(q2[1], "dp", 1))
        grad_qkv, qvec = call(
            qkv_final_kernel,
            [sds((OWN, 3 * WIDTH), F32), sds((8, 3 * HW), F32)],
            [tab, q3] + [swap(q3, "uly", k) for k in (1, 2, 3)],
        )
        grad_gain1, grad_shift1, grad_qbias, grad_vbias = (
            qvec[0, k * OWN : (k + 1) * OWN] for k in range(4)
        )
    else:

        def owned(array):
            shard = lax.psum_scatter(
                array.astype(F32), axes, scatter_dimension=0, tiled=True
            )
            return lax.psum(shard.astype(BF16), "uly").astype(F32)

        def by_owner(keep, send, order):
            both = jnp.concatenate([keep, send], axis=0)
            return both[jnp.array(order)]

        o8 = by_owner(okeep, osend, [0, 4, 2, 6, 1, 5, 3, 7])
        q8 = by_owner(qkeep, qsend, [0, 4, 2, 6, 1, 5, 3, 7])

        def widen(keep, send):
            flat = jnp.concatenate([keep, send], axis=0).reshape(WIDTH, 1, QUART)
            place = (jnp.arange(BLK) == b)[None, :, None]
            return jnp.where(place, flat, jnp.zeros_like(flat)).reshape(WIDTH, FF)

        grad_up = owned(widen(ukeep, usend))
        grad_down = owned(widen(dkeep, dsend)).T
        grad_ubias = owned(o8[:, OWN, 288:672].reshape(FF))
        grad_dbias = owned(o8[:, OWN, 672:768].reshape(WIDTH))
        grad_ow = owned(o8[:, :OWN].reshape(WIDTH, WIDTH))
        grad_obias, grad_gain2, grad_shift2 = (
            owned(o8[:, OWN, k * OWN : (k + 1) * OWN].reshape(WIDTH)) for k in range(3)
        )
        mine = q8[:, :OWN].reshape(WIDTH, 3, 1, HW)
        spread = jnp.where(
            (jnp.arange(ULY) == z)[None, None, :, None], mine, jnp.zeros_like(mine)
        )
        grad_qkv = owned(spread.reshape(WIDTH, 3 * WIDTH))
        grad_gain1, grad_shift1, grad_qbias, grad_vbias = (
            owned(q8[:, OWN, k * OWN : (k + 1) * OWN].reshape(WIDTH)) for k in range(4)
        )

    return (
        output.reshape(inputs.shape),
        grad_inputs.reshape(inputs.shape),
        grad_qkv,
        grad_qbias,
        grad_vbias,
        grad_ow,
        grad_obias,
        grad_gain1,
        grad_shift1,
        grad_gain2,
        grad_shift2,
        grad_up,
        grad_ubias,
        grad_down,
        grad_dbias,
    )


def solution(mesh):
    rows = P(None, ("dp", "uly", "blk"), None)
    first = P(("dp", "blk"), None)
    flat = P(("dp", "blk"))
    second = P(None, ("dp", "blk"))
    return jax.shard_map(
        body,
        mesh=mesh,
        in_specs=(
            rows,
            rows,
            first,
            flat,
            flat,
            first,
            flat,
            flat,
            flat,
            flat,
            flat,
            first,
            flat,
            second,
            flat,
            P(None, "dp", None),
            P(None, "dp"),
        ),
        out_specs=(
            rows,
            rows,
            first,
            flat,
            flat,
            first,
            flat,
            flat,
            flat,
            flat,
            flat,
            first,
            flat,
            second,
            flat,
        ),
        check_vma=False,
    )
```

```python
import functools

import jax
import jax.numpy as jnp
from jax import lax
from jax.experimental import pallas as pl
from jax.experimental.pallas import tpu as pltpu
from jax.sharding import PartitionSpec as P

HEADS = 12
HEAD_DIM = 64
FF = 3072
F32 = jnp.float32
BF16 = jnp.bfloat16
NEG = -1e30
VMEM_LIMIT = 60 * 1024 * 1024

ROWS = 128
ULY = 4
BLK = 4
GROUP = ROWS * ULY
KEYS = GROUP * BLK
WIDTH = HEADS * HEAD_DIM
HW = WIDTH // ULY
LOCAL_HEADS = HEADS // ULY
OWNERS = 8
OWN = WIDTH // OWNERS
PANEL = OWN + 16
QUART = FF // BLK


def swap(array, axis, by):
    peers = lax.axis_size(axis)
    return lax.ppermute(array, axis, [(i, i ^ by) for i in range(peers)])


def cross(array, by):
    peers = lax.axis_size("dp") * lax.axis_size("blk")
    return lax.ppermute(array, ("dp", "blk"), [(i, i ^ by) for i in range(peers)])


def after(array, *others):
    return lax.optimization_barrier((array, *others))[0]


def vm():
    return pl.BlockSpec(memory_space=pltpu.VMEM)


def anyspace():
    return pl.BlockSpec(memory_space=pl.ANY)


def smem():
    return pl.BlockSpec(memory_space=pltpu.SMEM)


def call(kernel, outs, args, scratch=(), flops=0, in_any=()):
    specs = [smem()] + [anyspace() if i in in_any else vm() for i in range(1, len(args))]
    nbytes = sum(a.size * a.dtype.itemsize for a in args) + sum(
        o.size * o.dtype.itemsize for o in outs
    )
    nbytes = nbytes if flops else 1
    return pl.pallas_call(
        kernel,
        name=getattr(kernel, "func", kernel).__name__,
        out_shape=outs,
        in_specs=specs,
        out_specs=[vm() for _ in outs],
        scratch_shapes=list(scratch),
        cost_estimate=pl.CostEstimate(
            flops=flops, bytes_accessed=nbytes, transcendentals=0
        ),
        compiler_params=pltpu.CompilerParams(vmem_limit_bytes=VMEM_LIMIT),
    )(*args)


def sds(shape, dtype):
    return jax.ShapeDtypeStruct(shape, dtype)


def nn(a, b):
    return lax.dot_general(a, b, (((1,), (0,)), ((), ())), preferred_element_type=F32)


def nt(a, b):
    return lax.dot_general(a, b, (((1,), (1,)), ((), ())), preferred_element_type=F32)


def tn(a, b):
    return lax.dot_general(a, b, (((0,), (0,)), ((), ())), preferred_element_type=F32)


def rows_at(index, size):
    return pl.ds(pl.multiple_of(index * size, 32), size)


def vec(vv_ref, row, lane):
    return jnp.concatenate(
        [vv_ref[o].astype(F32)[row : row + 1, lane : lane + OWN] for o in range(OWNERS)], axis=1
    )


def norm_stats(v):
    mean = jnp.mean(v, axis=-1, keepdims=True)
    cen = v - mean
    var = jnp.mean(cen * cen, axis=-1, keepdims=True)
    r = lax.rsqrt(var + 1e-12)
    return cen * r, r


def norm_kernel(tab, x_ref, n_ref):
    n_ref[...] = norm_stats(x_ref[...])[0].astype(BF16)


def prep_kernel(tab, x_ref, w_ref, *rest):
    vectors, (n_ref, panel_ref) = rest[:9], rest[9:]
    z = tab[1]
    rows = [v[...].astype(F32).reshape(1, v.shape[0]) for v in vectors]
    panel_ref[OWN:, :] = jnp.concatenate(
        [
            jnp.concatenate(rows[:6], axis=1),
            jnp.concatenate(rows[6:], axis=1),
            jnp.zeros((14, 3 * HW), F32),
        ],
        axis=0,
    ).astype(BF16)
    for k in range(ULY):

        @pl.when(z == k)
        def _():
            parts = [w_ref[:, p * WIDTH + k * HW : p * WIDTH + (k + 1) * HW] for p in range(3)]
            panel_ref[:OWN, :] = jnp.concatenate(parts, axis=1)

    n_ref[...] = norm_stats(x_ref[...])[0].astype(BF16)


def quarter(index):
    return pl.ds(pl.multiple_of(index * QUART, 128), QUART)


def ffn_prep_kernel(tab, u_ref, d_ref, *outs):
    b = tab[3]
    for s, ref in enumerate(outs):
        q = quarter(jnp.bitwise_xor(b, s))
        ref[0] = u_ref[:, q]
        ref[1] = d_ref[:, q]


def qkv_kernel(owner_bits, tab, n0, n1, n2, n3, *rest):
    arrays = rest[: len(owner_bits)]
    q_ref, kv_ref, h_ref, w_ref, vv_ref = rest[len(owner_bits) :]
    me, z = tab[0], tab[1]
    for ref, bits in zip(arrays, owner_bits):
        for i, bit in enumerate(bits):
            o = jnp.bitwise_xor(me, bit)
            w_ref[rows_at(o, OWN), :] = ref[i, :OWN, :]
            vv_ref[o] = ref[i, OWN:PANEL, :]
    gain = vec(vv_ref, 0, 0)
    shift = vec(vv_ref, 0, OWN)
    lo = vv_ref[2 * z].astype(F32)
    hi = vv_ref[2 * z + 1].astype(F32)
    zero = jnp.zeros((1, HW), F32)
    bias = jnp.concatenate(
        [
            lo[0:1, 2 * OWN : 3 * OWN],
            hi[0:1, 2 * OWN : 3 * OWN],
            zero,
            lo[0:1, 3 * OWN : 4 * OWN],
            hi[0:1, 3 * OWN : 4 * OWN],
        ],
        axis=1,
    )
    for i, ref in enumerate((n0, n1, n2, n3)):
        rows = slice(i * ROWS, (i + 1) * ROWS)
        h = (ref[...].astype(F32) * gain + shift).astype(BF16)
        h_ref[rows, :] = h
        proj = (nn(h, w_ref[...]) + bias).astype(BF16)
        q_ref[rows, :] = proj[:, :HW] * jnp.asarray(HEAD_DIM ** (-0.5), BF16)
        kv_ref[rows, :] = proj[:, HW:]


def placed(piece, upper):
    zero = jnp.zeros_like(piece)
    return jnp.concatenate([zero, piece] if upper else [piece, zero], axis=1)


def head_cols(h):
    return slice(h * HEAD_DIM, (h + 1) * HEAD_DIM)


def window(index):
    lane = index * HEAD_DIM
    start = lane // 128 * 128
    return slice(start, start + 128), (lane % 128) >= 64


def attend_kernel(tab, q_ref, k0, k1, k2, k3, qc_ref, kc_ref, o0, o1, o2, o3, all_ref, lse_ref):
    kvs = (k0, k1, k2, k3)
    outs = (o0, o1, o2, o3)

    lane = lax.broadcasted_iota(jnp.int32, (ROWS, 128), 1)

    def step(i, carry):
        rows = rows_at(i, ROWS)
        code1 = qc_ref[rows, 0:1]
        code2 = qc_ref[rows, 1:2]
        masks = []
        for j in range(BLK):
            kc = kc_ref[0:1, j * GROUP : (j + 1) * GROUP]
            masks.append((kc == code1) | (kc == code2))
        heads = []
        lse = jnp.zeros((ROWS, 128), F32)
        for h in range(LOCAL_HEADS):
            kwin, kup = window(h)
            vwin, vup = window(LOCAL_HEADS + h)
            qp = placed(q_ref[rows, head_cols(h)], kup)
            scores = [
                jnp.where(masks[j], nt(qp, kvs[j][:, kwin]), NEG) for j in range(BLK)
            ]
            top = functools.reduce(jnp.maximum, [jnp.max(s, axis=1, keepdims=True) for s in scores])
            total = jnp.zeros((ROWS, 1), F32)
            acc = jnp.zeros((ROWS, 128), F32)
            for j in range(BLK):
                e = jnp.exp(scores[j] - top)
                total = total + jnp.sum(e, axis=1, keepdims=True)
                acc = acc + nn(e.astype(BF16), kvs[j][:, vwin])
            acc = acc[:, 64:] if vup else acc[:, :64]
            heads.append((acc / total).astype(BF16))
            lse = jnp.where(lane == h, top + jnp.log(total), lse)
        all_ref[rows, :] = jnp.concatenate(heads, axis=1)
        lse_ref[rows, :] = lse
        return carry

    lax.fori_loop(0, ULY, step, 0)
    for i in range(ULY):
        outs[i][...] = all_ref[i * ROWS : (i + 1) * ROWS, :]


def mix_kernel(plan, tab, a0, a1, a2, a3, x_ref, vv_ref, *rest):
    parts, (resid_ref, h_ref, ow_ref, sems) = rest[:-4], rest[-4:]
    me, z = tab[0], tab[1]
    copies = []
    for index, place, bit in plan:
        copy = pltpu.make_async_copy(
            parts[index].at[place],
            ow_ref.at[rows_at(jnp.bitwise_xor(me, bit), OWN), :],
            sems.at[len(copies)],
        )
        copy.start()
        copies.append(copy)
    acc = x_ref[...] + vec(vv_ref, 0, 4 * OWN)
    for copy in copies:
        copy.wait()
    for j, ref in enumerate((a0, a1, a2, a3)):
        acc = acc + nn(ref[...], ow_ref[rows_at(jnp.bitwise_xor(z, j), HW), :])
    resid_ref[...] = acc
    n, _ = norm_stats(acc)
    h_ref[...] = (n * vec(vv_ref, 0, 5 * OWN) + vec(vv_ref, 1, 0)).astype(BF16)


CHUNK = 256


def ffn_kernel(plan, tab, h0, h1, h2, h3, c0, c1, c2, c3, vv_ref, *rest):
    count = len(rest) - 16
    parts = rest[:count]
    act_ref, dhid_ref, ykeep, ysend, go_ref, g1, g2, g3 = rest[count : count + 8]
    u_ref, d_ref, hall, call_ref, bias_ref, yacc, gacc, sems = rest[count + 8 :]
    me, b = tab[0], tab[3]
    copies = []
    for u_place, d_place, bit in plan:
        rows = rows_at(jnp.bitwise_xor(me, bit), OWN)
        for (index, slot), target in ((u_place, u_ref), (d_place, d_ref)):
            copy = pltpu.make_async_copy(
                parts[index].at[slot], target.at[rows, :], sems.at[len(copies)]
            )
            copy.start()
            copies.append(copy)
    for i, (h_ref, c_ref) in enumerate(((h0, c0), (h1, c1), (h2, c2), (h3, c3))):
        rows = slice(i * ROWS, (i + 1) * ROWS)
        hall[rows, :] = h_ref[...]
        call_ref[rows, :] = c_ref[...]
    for k in range(2):
        bias_ref[:, k * 384 : (k + 1) * 384] = vv_ref[2 * b + k].astype(F32)[1:2, 192:576]
    yacc[...] = jnp.zeros_like(yacc)
    gacc[...] = jnp.zeros_like(gacc)
    for copy in copies:
        copy.wait()

    def step(k, carry):
        cols = pl.ds(pl.multiple_of(k * CHUNK, CHUNK), CHUNK)
        hid = nn(hall[...], u_ref[:, cols]) + bias_ref[:, cols]
        dact = nn(call_ref[...], d_ref[:, cols])
        cdf = 0.5 * (1.0 + lax.erf(hid * 0.7071067811865476))
        act = (hid * cdf).astype(BF16)
        pdf = jnp.exp(-0.5 * hid * hid) * 0.3989422804014327
        dhid = (dact * (cdf + hid * pdf)).astype(BF16)
        act_ref[:, cols] = act
        dhid_ref[:, cols] = dhid
        yacc[...] += nt(act, d_ref[:, cols])
        gacc[...] += nt(dhid, u_ref[:, cols])
        return carry

    lax.fori_loop(0, QUART // CHUNK, step, 0)
    for i, y_ref in enumerate((ykeep, ysend, ykeep, ysend)):
        y_ref[i // 2] = yacc[i * ROWS : (i + 1) * ROWS, :].astype(y_ref.dtype)
    for i, g_ref in enumerate((go_ref, g1, g2, g3)):
        g_ref[...] = gacc[i * ROWS : (i + 1) * ROWS, :].astype(g_ref.dtype)


def ffn_grad_kernel(tab, *refs):
    me = tab[0]
    h_refs, c_refs = refs[:4], refs[4:8]
    dhid_ref, act_ref, usend, ukeep, dthere, dhere, left, left2 = refs[8:]
    for i in range(BLK):
        left[:, i * ROWS : (i + 1) * ROWS] = h_refs[i][...].T
        left2[:, i * ROWS : (i + 1) * ROWS] = c_refs[i][...].T
    for source, right_ref, ref, bits in (
        (left, dhid_ref, usend, (4, 5, 6, 7)),
        (left, dhid_ref, ukeep, (0, 1, 2, 3)),
        (left2, act_ref, dthere, (2, 6, 3, 7)),
        (left2, act_ref, dhere, (0, 4, 1, 5)),
    ):
        for s, bit in enumerate(bits):
            o = jnp.bitwise_xor(me, bit)
            ref[s] = nn(source[rows_at(o, OWN), :], right_ref[...]).astype(BF16)


def back_mix_kernel(
    tab, resid_ref, cot_ref, go_ref, g1, g2, g3, ow_ref, vv_ref, dres_ref, dmix_ref, d0, d1, d2, d3, vs_ref
):
    z = tab[1]
    grad = go_ref[...] + g1[...].astype(F32) + g2[...].astype(F32) + g3[...].astype(F32)
    n, r = norm_stats(resid_ref[...])
    dn = grad * vec(vv_ref, 0, 5 * OWN)
    dres = cot_ref[...] + r * (
        dn
        - jnp.mean(dn, axis=-1, keepdims=True)
        - n * jnp.mean(dn * n, axis=-1, keepdims=True)
    )
    dres_ref[...] = dres
    dmix = dres.astype(BF16)
    dmix_ref[...] = dmix
    for j, ref in enumerate((d0, d1, d2, d3)):
        ref[...] = nt(dmix, ow_ref[rows_at(jnp.bitwise_xor(z, j), HW), :]).astype(BF16)
    vs_ref[0:1, :] = jnp.sum(dmix.astype(F32), axis=0, keepdims=True)
    vs_ref[1:2, :] = jnp.sum(grad * n, axis=0, keepdims=True)
    vs_ref[2:3, :] = jnp.sum(grad, axis=0, keepdims=True)
    vs_ref[3:8, :] = jnp.zeros((5, WIDTH), F32)


def out_grad_kernel(tab, a0, a1, a2, a3, dmix_ref, vs_ref, dhid_ref, c_ref, keep, send, left, vrow):
    me, z, b = tab[0], tab[1], tab[3]
    for j, ref in enumerate((a0, a1, a2, a3)):
        left[rows_at(jnp.bitwise_xor(z, j), HW), :] = ref[...].astype(F32).T.astype(BF16)
    vs = vs_ref[...]
    usum = jnp.sum(dhid_ref[...].astype(F32), axis=0, keepdims=True)
    csum = jnp.sum(c_ref[...].astype(F32), axis=0, keepdims=True)
    for o in range(OWNERS):
        part = usum[:, (o % 2) * 384 : (o % 2 + 1) * 384]
        row = jnp.concatenate(
            [vs[k : k + 1, o * OWN : (o + 1) * OWN] for k in range(3)]
            + [jnp.where(b == o // 2, part, 0.0), csum[:, o * OWN : (o + 1) * OWN]],
            axis=1,
        )
        vrow[o] = jnp.broadcast_to(row, (16, WIDTH)).astype(BF16)
    for ref, base in ((send, 1), (keep, 0)):
        for s in range(4):
            o = jnp.bitwise_xor(me, base + (s // 2) * 2 + (s % 2) * 4)
            ref[s, :OWN, :] = nn(left[rows_at(o, OWN), :], dmix_ref[...]).astype(BF16)
            ref[s, OWN:, :] = vrow[o]


def back_attend_kernel(
    tab,
    q_ref,
    k0,
    k1,
    k2,
    k3,
    g0,
    g1,
    g2,
    g3,
    all_ref,
    lse_ref,
    qr_ref,
    kcol_ref,
    dq_ref,
    keep,
    send,
    acc,
    gall,
):
    kvs = (k0, k1, k2, k3)
    acc[...] = jnp.zeros_like(acc)
    for i, g_ref in enumerate((g0, g1, g2, g3)):
        gall[i * ROWS : (i + 1) * ROWS, :] = g_ref[...]
    lane = lax.broadcasted_iota(jnp.int32, (ROWS, 128), 1)

    def step(i, carry):
        rows = rows_at(i, ROWS)
        prod = gall[rows, :].astype(F32) * all_ref[rows, :].astype(F32)
        stat = jnp.zeros((ROWS, 128), F32)
        for h in range(LOCAL_HEADS):
            stat = jnp.where(
                lane == h, jnp.sum(prod[:, head_cols(h)], axis=1, keepdims=True), stat
            )
        rowdot = stat.T
        lse = lse_ref[rows, :].T
        code1 = qr_ref[0:1, rows]
        code2 = qr_ref[1:2, rows]
        dq = [jnp.zeros((ROWS, 128), F32) for _ in range(LOCAL_HEADS)]
        for j in range(BLK):
            kc = kcol_ref[j * GROUP : (j + 1) * GROUP, :]
            mask = (kc == code1) | (kc == code2)
            for h in range(LOCAL_HEADS):
                kwin, kup = window(h)
                vwin, vup = window(LOCAL_HEADS + h)
                qp = placed(q_ref[rows, head_cols(h)], kup)
                gp = placed(gall[rows, head_cols(h)], vup)
                kk = kvs[j][:, kwin]
                scores = nt(kk, qp)
                p = jnp.where(mask, jnp.exp(scores - lse[h : h + 1, :]), 0.0)
                dp = nt(kvs[j][:, vwin], gp)
                ds = (p * (dp - rowdot[h : h + 1, :])).astype(BF16)
                acc[j, :, vwin] += nn(p.astype(BF16), gp)
                acc[j, :, kwin] += nn(ds, qp)
                dq[h] = dq[h] + tn(ds, kk)
        parts = []
        for h in range(LOCAL_HEADS):
            _, kup = window(h)
            parts.append(dq[h][:, 64:] if kup else dq[h][:, :64])
        dq_ref[rows, :] = (jnp.concatenate(parts, axis=1) * HEAD_DIM ** (-0.5)).astype(BF16)
        return carry

    lax.fori_loop(0, ULY, step, 0)
    keep[0] = acc[0].astype(BF16)
    keep[1] = acc[2].astype(BF16)
    send[0] = acc[1].astype(BF16)
    send[1] = acc[3].astype(BF16)


def back_proj_kernel(
    tab, dq_ref, keep, got, recv, w_ref, n0, n1, n2, n3, dproj_ref, h0, h1, send, vs_ref
):
    dproj_ref[:, :HW] = dq_ref[...]
    total = keep[0].astype(F32) + got[0].astype(F32) + recv[...].astype(F32)
    dproj_ref[:, HW:] = total.astype(BF16)
    gain = jnp.zeros((1, WIDTH), F32)
    shift = jnp.zeros((1, WIDTH), F32)
    outs = (h0, h1, send.at[0], send.at[1])
    for i, (n_ref, out) in enumerate(zip((n0, n1, n2, n3), outs)):
        rows = slice(i * ROWS, (i + 1) * ROWS)
        grad = nt(dproj_ref[rows, :], w_ref[...])
        out[...] = grad.astype(out.dtype)
        gain = gain + jnp.sum(grad * n_ref[...].astype(F32), axis=0, keepdims=True)
        shift = shift + jnp.sum(grad, axis=0, keepdims=True)
    vs_ref[0:1, :] = gain
    vs_ref[1:2, :] = shift
    cols = jnp.sum(dproj_ref[...].astype(F32), axis=0, keepdims=True)
    vs_ref[2:3, :] = jnp.concatenate([cols, jnp.zeros((1, WIDTH - 3 * HW), F32)], axis=1)
    vs_ref[3:8, :] = jnp.zeros((5, WIDTH), F32)


def qkv_grad_kernel(tab, h_ref, dproj_ref, vs_ref, keep, send, left, vrow):
    me, z = tab[0], tab[1]
    vs = vs_ref[...]
    for o in range(OWNERS):
        row = [vs[k : k + 1, o * OWN : (o + 1) * OWN] for k in range(2)]
        for lane in (0, 2 * HW):
            lane = lane + (o % 2) * OWN
            row.append(jnp.where(z == o // 2, vs[2:3, lane : lane + OWN], 0.0))
        row.append(jnp.zeros((1, 3 * HW - 4 * OWN), F32))
        vrow[o] = jnp.broadcast_to(jnp.concatenate(row, axis=1), (16, 3 * HW)).astype(BF16)
    for i in range(ULY):
        rows = slice(i * ROWS, (i + 1) * ROWS)
        left[:, rows] = h_ref[rows, :].T
    for ref, base in ((keep, 0), (send, 1)):
        for s in range(4):
            o = jnp.bitwise_xor(me, base + (s // 2) * 2 + (s % 2) * 4)
            ref[s, :OWN, :] = nn(left[rows_at(o, OWN), :], dproj_ref[...]).astype(BF16)
            ref[s, OWN:, :] = vrow[o]


def back_norm_kernel(tab, x_ref, dres_ref, h0, got2, got1, vv_ref, out_ref):
    grad = h0[...] + got2[0].astype(F32) + got1[...].astype(F32)
    n, r = norm_stats(x_ref[...])
    dn = grad * vec(vv_ref, 0, 0)
    out_ref[...] = dres_ref[...] + r * (
        dn
        - jnp.mean(dn, axis=-1, keepdims=True)
        - n * jnp.mean(dn * n, axis=-1, keepdims=True)
    )


def output_kernel(tab, resid_ref, keep, got, last, vv_ref, out_ref):
    out_ref[...] = (
        resid_ref[...]
        + keep[0]
        + got[0].astype(F32)
        + last[...].astype(F32)
        + vec(vv_ref, 1, OWN)
    )


def low_sum(a, b):
    return (a.astype(F32) + b.astype(F32)).astype(BF16)


def split_kernel(bit, tab, a_ref, ac_ref, by_ref, byc_ref, keep, send):
    for value, low_out, high_out in ((0, keep, send), (1, send, keep)):

        @pl.when(tab[bit] == value)
        def _():
            low_out[0] = a_ref[0]
            low_out[1] = ac_ref[1]
            high_out[0] = by_ref[0]
            high_out[1] = byc_ref[1]


def pack_kernel(tab, a_ref, ac_ref, by_ref, byc_ref, out_ref):
    for s, (ref, place) in enumerate(((a_ref, 1), (ac_ref, 3), (by_ref, 1), (byc_ref, 3))):
        out_ref[s] = ref[place]


def split_add_kernel(bit, tab, a_ref, ac_ref, by_ref, byc_ref, got, keep, send):
    refs = ((a_ref, 0), (ac_ref, 2), (by_ref, 0), (byc_ref, 2))
    for value, low_out, high_out in ((0, keep, send), (1, send, keep)):

        @pl.when(tab[bit] == value)
        def _():
            for s, (ref, place) in enumerate(refs):
                (low_out, high_out)[s // 2][s % 2] = low_sum(ref[place], got[s])


def merge_kernel(bit, tab, a_ref, b_ref, keep, send):
    for value, low_out, high_out in ((0, keep, send), (1, send, keep)):

        @pl.when(tab[bit] == value)
        def _():
            low_out[...] = low_sum(a_ref[0], b_ref[0])
            high_out[...] = low_sum(a_ref[1], b_ref[1])


def final_kernel(tab, pair, got, out_ref):
    b, odd, high = tab[3], tab[4], tab[5]
    for flip, ref in ((0, pair.at[0]), (1, pair.at[1]), (2, got.at[0]), (3, got.at[1])):
        q = jnp.bitwise_xor(jnp.bitwise_xor(b, 2 * odd + high), flip)
        out_ref[:, quarter(q)] = ref[...].astype(F32)


def qkv_final_kernel(tab, pair, got, out_ref, vec_ref):
    z = tab[1]
    refs = (pair.at[0], pair.at[1], got.at[0], got.at[1])
    for k in range(ULY):

        @pl.when(z == k)
        def _():
            for p in range(3):
                cols = [
                    refs[t ^ k][:OWN, p * HW : (p + 1) * HW].astype(F32) for t in range(ULY)
                ]
                out_ref[:, p * WIDTH : (p + 1) * WIDTH] = jnp.concatenate(cols, axis=1)

    total = jnp.zeros((16, 3 * HW), F32)
    for ref in refs:
        total = total + ref[OWN:, :].astype(F32)
    vec_ref[...] = total[:8, :]


def add_low(a, b):
    return (a.astype(F32) + b.astype(F32)).astype(BF16)


def xor_order(array, axis, index):
    shape = array.shape
    two = array.reshape(shape[:axis] + (2, 2) + shape[axis + 1 :])
    two = jnp.where((index & 1) == 1, jnp.flip(two, axis + 1), two)
    two = jnp.where((index & 2) == 2, jnp.flip(two, axis), two)
    return two.reshape(shape)


def body(
    inputs,
    cotangent,
    qkv_weight,
    query_bias,
    value_bias,
    out_weight,
    out_bias,
    norm1_gain,
    norm1_bias,
    norm2_gain,
    norm2_bias,
    up_weight,
    up_bias,
    down_weight,
    down_bias,
    doc_lengths,
    pad_mask,
):
    dp_count = lax.axis_size("dp")
    near = dp_count == 2
    dp = lax.axis_index("dp")
    z = lax.axis_index("uly")
    b = lax.axis_index("blk")
    core = b & 1
    rank = dp * BLK + b
    me = rank if near else jnp.int32(0)
    tab = jnp.stack([me, z, core, b, z & 1, z >> 1]).astype(jnp.int32)
    own_rows = WIDTH // (dp_count * BLK)
    axes = ("dp", "blk")

    x = inputs.reshape(ROWS, WIDTH)
    cot = cotangent.reshape(ROWS, WIDTH)

    if near:
        vectors = [norm1_gain, norm1_bias, query_bias, value_bias, out_bias, norm2_gain]
        vectors += [norm2_bias, down_bias, up_bias]
        n0, panel = call(
            prep_kernel,
            [sds((ROWS, WIDTH), BF16), sds((PANEL, 3 * HW), BF16)],
            [tab, x, qkv_weight, *vectors],
        )
        n1, n2, n3 = (swap(n0, "uly", k) for k in (1, 2, 3))
        a_0 = jnp.stack([panel, swap(panel, "dp", 1)])
        a_2 = swap(a_0, "blk", 2)
        four_bits = [[0, 4], [2, 6], [1, 5], [3, 7]]
        w_mine = call(
            ffn_prep_kernel,
            [sds((2, OWN, QUART), BF16)] * BLK,
            [tab, up_weight, down_weight.T],
        )
        n1 = after(n1, w_mine[0])
        a_2c = swap(a_2, "blk", 1)
        a_0c = swap(after(a_0, a_2c), "blk", 1)
        a_parts = [a_0, a_2, a_0c, a_2c]
        w_parts = [w_mine[0], None, cross(after(w_mine[2], a_0c), 2)] + [None] * 5
        w_plan = [((i, 0), (i, 1), i) for i in range(OWNERS)]
        o_plan = [
            (i, k, bit) for i, bits in enumerate(four_bits) for k, bit in enumerate(bits)
        ]
    else:
        (n0,) = call(norm_kernel, [sds((ROWS, WIDTH), BF16)], [tab, x])
        n1, n2, n3 = (swap(n0, "uly", k) for k in (1, 2, 3))
        qkv_cols = lax.dynamic_index_in_dim(
            qkv_weight.reshape(own_rows, 3, ULY, HW), z, axis=2, keepdims=False
        ).reshape(own_rows, 3 * HW)

        def full(array):
            return lax.all_gather(array, axes, axis=0, tiled=True)

        def eight(vector):
            return full(vector).reshape(OWNERS, 1, -1)

        def mine(array):
            cols = full(array).reshape(WIDTH, BLK, QUART)
            return lax.dynamic_index_in_dim(cols, b, 1, False).reshape(OWNERS, OWN, QUART)

        row0 = jnp.concatenate(
            [
                eight(v)
                for v in (norm1_gain, norm1_bias, query_bias, value_bias, out_bias, norm2_gain)
            ],
            axis=2,
        )
        row1 = jnp.concatenate([eight(v) for v in (norm2_bias, down_bias, up_bias)], axis=2)
        a_parts = [
            jnp.concatenate(
                [
                    full(qkv_cols).reshape(OWNERS, OWN, 3 * HW),
                    row0,
                    row1,
                    jnp.zeros((OWNERS, 14, 3 * HW), BF16),
                ],
                axis=1,
            )
        ]
        four_bits = [list(range(OWNERS))]
        o_parts = [full(out_weight).reshape(OWNERS, OWN, WIDTH)]
        w_parts = [mine(up_weight), mine(down_weight.T)]
        w_plan = [((0, o), (1, o), o) for o in range(OWNERS)]
        o_plan = [(0, o, o) for o in range(OWNERS)]

    ends = jnp.cumsum(doc_lengths.reshape(-1), dtype=jnp.int32)
    zs = jnp.arange(ULY, dtype=jnp.int32) ^ z
    bs = jnp.arange(BLK, dtype=jnp.int32) ^ b
    within = jnp.arange(ROWS, dtype=jnp.int32)
    kplace = ((zs[None, :, None] * BLK + bs[:, None, None]) * ROWS + within).reshape(KEYS)
    kseg = jnp.sum((kplace[:, None] >= ends[None, :]).astype(jnp.int32), axis=1)
    valid = pad_mask.reshape(ULY, BLK, ROWS)
    valid = xor_order(xor_order(valid, 0, z), 1, b).transpose(1, 0, 2).reshape(KEYS)
    kcode = jnp.where(valid > 0, kseg, kplace + 64)
    qcodes = jnp.stack([kseg[:GROUP], kplace[:GROUP] + 64])

    n1, q_cols, q_rows, k_cols, k_rows = lax.optimization_barrier(
        (n1, qcodes.T, qcodes, kcode[:, None], kcode[None, :])
    )
    q, kv, h1, w_qkv, vv = call(
        functools.partial(qkv_kernel, four_bits),
        [
            sds((GROUP, HW), BF16),
            sds((GROUP, 2 * HW), BF16),
            sds((GROUP, WIDTH), BF16),
            sds((WIDTH, 3 * HW), BF16),
            sds((OWNERS, 16, 3 * HW), BF16),
        ],
        [tab, n0, n1, n2, n3, *a_parts],
        flops=2 * GROUP * WIDTH * 3 * HW,
    )
    cb = cot.astype(BF16)
    if near:
        kv_y = swap(after(kv, w_parts[2]), "blk", 2)
        cb_y = swap(after(cb, kv_y), "blk", 2)
        w_parts[4] = cross(after(w_mine[0], kv), 4)
        w_parts[5] = cross(after(w_mine[1], kv), 5)
        o_0 = jnp.stack([out_weight, swap(after(out_weight, kv), "dp", 1)])
        o_0c = swap(o_0, "blk", 1)
        o_2 = swap(after(o_0, kv_y), "blk", 2)
    else:
        kv_y = swap(kv, "blk", 2)
    kv_c = swap(kv, "blk", 1)
    kv_yc = swap(kv_y, "blk", 1)
    if near:
        cb_c = swap(after(cb, kv), "blk", 1)
        w_parts[1] = cross(after(w_mine[1], kv), 1)
        kv_yc = after(kv_yc, o_0c, w_parts[1], cb_c)
    kvs = [kv, kv_c, kv_y, kv_yc]

    def around(array):
        near_y = swap(array, "blk", 2)
        return [array, swap(array, "blk", 1), near_y, swap(near_y, "blk", 1)]

    if near:
        w_parts[3] = cross(after(w_mine[3], kv_y), 3)
    else:
        cbs = around(cb)

    *attn_slots, attn_all, lse = call(
        attend_kernel,
        [sds((ROWS, HW), BF16)] * ULY + [sds((GROUP, HW), BF16), sds((GROUP, 128), F32)],
        [tab, q, *kvs, q_cols, k_rows],
        flops=4 * GROUP * KEYS * HW,
    )
    if near:
        attn_slots = after(attn_slots, w_parts[4], w_parts[5], o_2)
        o_2c = swap(after(o_2, attn_slots[0]), "blk", 1)
        o_parts = [o_0, o_2, o_0c, o_2c]
    attn = [attn_slots[0]] + [swap(attn_slots[k], "uly", k) for k in (1, 2, 3)]
    resid, h2, ow = call(
        functools.partial(mix_kernel, o_plan),
        [sds((ROWS, WIDTH), F32), sds((ROWS, WIDTH), BF16), sds((WIDTH, WIDTH), BF16)],
        [tab, *attn, x, vv, *o_parts],
        scratch=[pltpu.SemaphoreType.DMA((OWNERS,))],
        flops=2 * ROWS * WIDTH * WIDTH,
        in_any=range(7, 7 + len(o_parts)),
    )

    if near:
        w_parts[6] = cross(after(w_mine[2], attn[1]), 6)
        w_parts[7] = cross(after(w_mine[3], attn[2], cb_y, w_parts[3]), 7)
        h2 = after(h2, w_parts[6], w_parts[7])
        cbs = [cb, cb_c, cb_y, swap(after(cb_y, h2), "blk", 1)]
    h2s = around(h2)
    parts = len(w_parts)
    act, dhid, y_keep, y_send, go, *gs = call(
        functools.partial(ffn_kernel, w_plan),
        [sds((GROUP, QUART), BF16)] * 2
        + [sds((2, ROWS, WIDTH), F32), sds((2, ROWS, WIDTH), BF16), sds((ROWS, WIDTH), F32)]
        + [sds((ROWS, WIDTH), BF16)] * 3,
        [tab, *h2s, *cbs, vv, *w_parts],
        scratch=[
            pltpu.VMEM((WIDTH, QUART), BF16),
            pltpu.VMEM((WIDTH, QUART), BF16),
            pltpu.VMEM((GROUP, WIDTH), BF16),
            pltpu.VMEM((GROUP, WIDTH), BF16),
            pltpu.VMEM((1, QUART), F32),
            pltpu.VMEM((GROUP, WIDTH), F32),
            pltpu.VMEM((GROUP, WIDTH), F32),
            pltpu.SemaphoreType.DMA((2 * OWNERS,)),
        ],
        flops=8 * GROUP * WIDTH * QUART,
        in_any=range(10, 10 + parts),
    )
    gs = [swap(g, "blk", k) for k, g in enumerate(gs, 1)]

    y_got = swap(y_send, "blk", 1)
    y_part = (y_keep[1] + y_got[1].astype(F32)).astype(BF16)
    usend, ukeep, dthere, dhere = call(
        ffn_grad_kernel,
        [sds((BLK, OWN, QUART), BF16)] * 4,
        [tab, *h2s, *cbs, dhid, act],
        scratch=[pltpu.VMEM((WIDTH, GROUP), BF16)] * 2,
    )
    go = after(go, usend, dthere, y_part)

    dres, dmix, *dattn_slots, vs2 = call(
        back_mix_kernel,
        [sds((ROWS, WIDTH), F32), sds((ROWS, WIDTH), BF16)]
        + [sds((ROWS, HW), BF16)] * ULY
        + [sds((8, WIDTH), F32)],
        [tab, resid, cot, go, *gs, ow, vv],
        flops=2 * ROWS * WIDTH * WIDTH,
    )
    pair = sds((2, OWN, QUART), BF16)
    one = sds((OWN, QUART), BF16)
    dattn = [dattn_slots[0]] + [swap(dattn_slots[k], "uly", k) for k in (1, 2, 3)]
    if near:
        u_got = swap(usend, "dp", 1)
        d_there = swap(after(dthere, dmix), "blk", 2)
    y_last = swap(after(y_part, dattn[1]), "blk", 2)

    dq, keep_kv, send_kv = call(
        back_attend_kernel,
        [sds((GROUP, HW), BF16), sds((2, GROUP, 2 * HW), BF16), sds((2, GROUP, 2 * HW), BF16)],
        [tab, q, *kvs, *dattn, attn_all, lse, q_rows, k_cols],
        scratch=[pltpu.VMEM((BLK, GROUP, 2 * HW), F32), pltpu.VMEM((GROUP, HW), BF16)],
        flops=10 * GROUP * KEYS * HW,
    )
    if near:
        send_kv = after(send_kv, d_there, y_last)
    got = swap(send_kv, "blk", 1)
    kv_send = add_low(keep_kv[1], got[1])
    kv_got = swap(kv_send, "blk", 2)
    okeep, osend = call(
        out_grad_kernel,
        [sds((4, PANEL, WIDTH), BF16)] * 2,
        [tab, *attn, after(dmix, kv_send), vs2, dhid, cb],
        scratch=[pltpu.VMEM((WIDTH, ROWS), BF16), pltpu.VMEM((OWNERS, 16, WIDTH), BF16)],
    )

    if near:
        dhere, d_there = after(dhere, kv_send), after(d_there, kv_send)
        pieces = [dhere, swap(dhere, "blk", 1), d_there, swap(d_there, "blk", 1)]
        (d_send,) = call(pack_kernel, [sds((BLK, OWN, QUART), BF16)], [tab, *pieces])
        dq = after(dq, d_send, okeep)
    dproj, g_own, g_one, g_send, vs1 = call(
        back_proj_kernel,
        [sds((GROUP, 3 * HW), BF16)]
        + [sds((ROWS, WIDTH), F32)] * 2
        + [sds((2, ROWS, WIDTH), BF16), sds((8, WIDTH), F32)],
        [tab, dq, keep_kv, got, kv_got, w_qkv, n0, n1, n2, n3],
        flops=2 * GROUP * WIDTH * 3 * HW,
    )
    qkeep, qsend = call(
        qkv_grad_kernel,
        [sds((4, PANEL, 3 * HW), BF16)] * 2,
        [tab, h1, dproj, vs1],
        scratch=[pltpu.VMEM((WIDTH, GROUP), BF16), pltpu.VMEM((OWNERS, 16, 3 * HW), BF16)],
    )
    (output,) = call(
        output_kernel,
        [sds((ROWS, WIDTH), F32)],
        [tab, after(resid, dproj), y_keep, y_got, y_last, vv],
    )
    if near:
        o1 = add_low(okeep, swap(after(osend, dproj), "blk", 1))
        u_got = after(u_got, dproj)
        u_there = add_low(ukeep[2:], u_got[2:])
        u_here = add_low(ukeep[:2], u_got[:2])
        q1 = add_low(qkeep, swap(qsend, "blk", 1))
        u_there = swap(u_there, "blk", 2)
        upieces = [u_here, swap(u_here, "blk", 1), u_there, swap(u_there, "blk", 1)]
        ukept, usent = call(functools.partial(split_kernel, 4), [pair] * 2, [tab, *upieces])
        dkept, dsent = call(
            functools.partial(split_add_kernel, 4),
            [pair] * 2,
            [tab, *pieces, after(swap(d_send, "dp", 1), dproj)],
        )
        gates = [q1, dsent, usent]
    else:
        gates = []
    g_got = after(swap(g_send, "uly", 2), *gates)
    g_last = swap((g_one + g_got[1].astype(F32)).astype(BF16), "uly", 1)
    if near:

        def over_uly(kept, sent):
            return call(
                functools.partial(merge_kernel, 5),
                [one] * 2,
                [tab, kept, after(swap(sent, "uly", 1), g_got)],
            )

        def share(total):
            pair = jnp.stack([total, swap(total, "uly", 2)])
            return call(
                final_kernel, [sds((OWN, FF), F32)], [tab, pair, swap(pair, "uly", 1)]
            )[0]

        dkept, dsent = over_uly(dkept, dsent)
        ukept, usent = over_uly(ukept, usent)
        d_total = add_low(dkept, swap(dsent, "uly", 2))
        u_total = add_low(ukept, swap(usent, "uly", 2))
        g_last = after(g_last, d_total, usent, output)
        grad_down = share(d_total).T
        grad_up = share(u_total)

        o2 = add_low(o1[:2], swap(o1[2:], "blk", 2))
        o3 = add_low(o2[0], swap(o2[1], "dp", 1))
        o4 = add_low(o3, swap(after(o3, d_total), "uly", 1))
        o5 = o4.astype(F32) + swap(o4, "uly", 2).astype(F32)
        grad_ow = o5[:OWN]
        grad_obias, grad_gain2, grad_shift2 = (o5[OWN, k * OWN : (k + 1) * OWN] for k in range(3))
        grad_ubias, grad_dbias = o5[OWN, 288:672], o5[OWN, 672:768]

        q2 = add_low(q1[:2], swap(q1[2:], "blk", 2))
        q3 = add_low(q2[0], swap(q2[1], "dp", 1))
        q_pair = jnp.stack([q3, swap(q3, "uly", 1)])
        grad_qkv, qvec = call(
            qkv_final_kernel,
            [sds((OWN, 3 * WIDTH), F32), sds((8, 3 * HW), F32)],
            [tab, q_pair, swap(q_pair, "uly", 2)],
        )
        grad_gain1, grad_shift1, grad_qbias, grad_vbias = (
            qvec[0, k * OWN : (k + 1) * OWN] for k in range(4)
        )
    else:

        def owned(array):
            shard = lax.psum_scatter(
                array.astype(F32), axes, scatter_dimension=0, tiled=True
            )
            return lax.psum(shard.astype(BF16), "uly").astype(F32)

        def by_owner(keep, send, order):
            both = jnp.concatenate([keep, send], axis=0)
            return both[jnp.array(order)]

        o8 = by_owner(okeep, osend, [0, 4, 2, 6, 1, 5, 3, 7])
        q8 = by_owner(qkeep, qsend, [0, 4, 2, 6, 1, 5, 3, 7])

        def widen(keep, send, order):
            flat = jnp.concatenate([keep, send], axis=0)[jnp.array(order)]
            flat = flat.reshape(WIDTH, 1, QUART)
            place = (jnp.arange(BLK) == b)[None, :, None]
            return jnp.where(place, flat, jnp.zeros_like(flat)).reshape(WIDTH, FF)

        grad_up = owned(widen(ukeep, usend, range(OWNERS)))
        grad_down = owned(widen(dhere, dthere, [0, 2, 4, 6, 1, 3, 5, 7])).T
        grad_ubias = owned(o8[:, OWN, 288:672].reshape(FF))
        grad_dbias = owned(o8[:, OWN, 672:768].reshape(WIDTH))
        grad_ow = owned(o8[:, :OWN].reshape(WIDTH, WIDTH))
        grad_obias, grad_gain2, grad_shift2 = (
            owned(o8[:, OWN, k * OWN : (k + 1) * OWN].reshape(WIDTH)) for k in range(3)
        )
        mine = q8[:, :OWN].reshape(WIDTH, 3, 1, HW)
        spread = jnp.where(
            (jnp.arange(ULY) == z)[None, None, :, None], mine, jnp.zeros_like(mine)
        )
        grad_qkv = owned(spread.reshape(WIDTH, 3 * WIDTH))
        grad_gain1, grad_shift1, grad_qbias, grad_vbias = (
            owned(q8[:, OWN, k * OWN : (k + 1) * OWN].reshape(WIDTH)) for k in range(4)
        )

    (grad_inputs,) = call(
        back_norm_kernel, [sds((ROWS, WIDTH), F32)], [tab, x, dres, g_own, g_got, g_last, vv]
    )
    return (
        output.reshape(inputs.shape),
        grad_inputs.reshape(inputs.shape),
        grad_qkv,
        grad_qbias,
        grad_vbias,
        grad_ow,
        grad_obias,
        grad_gain1,
        grad_shift1,
        grad_gain2,
        grad_shift2,
        grad_up,
        grad_ubias,
        grad_down,
        grad_dbias,
    )


def solution(mesh):
    rows = P(None, ("dp", "uly", "blk"), None)
    first = P(("dp", "blk"), None)
    flat = P(("dp", "blk"))
    second = P(None, ("dp", "blk"))
    return jax.shard_map(
        body,
        mesh=mesh,
        in_specs=(
            rows,
            rows,
            first,
            flat,
            flat,
            first,
            flat,
            flat,
            flat,
            flat,
            flat,
            first,
            flat,
            second,
            flat,
            P(None, "dp", None),
            P(None, "dp"),
        ),
        out_specs=(
            rows,
            rows,
            first,
            flat,
            flat,
            first,
            flat,
            flat,
            flat,
            flat,
            flat,
            first,
            flat,
            second,
            flat,
        ),
        check_vma=False,
    )
```

```python
import functools

import jax
import jax.numpy as jnp
from jax import lax
from jax.experimental import pallas as pl
from jax.experimental.pallas import tpu as pltpu
from jax.sharding import PartitionSpec as P

HEADS = 12
HEAD_DIM = 64
FF = 3072
F32 = jnp.float32
BF16 = jnp.bfloat16
NEG = -1e30
VMEM_LIMIT = 60 * 1024 * 1024

ROWS = 128
ULY = 4
BLK = 4
GROUP = ROWS * ULY
KEYS = GROUP * BLK
WIDTH = HEADS * HEAD_DIM
HW = WIDTH // ULY
LOCAL_HEADS = HEADS // ULY
OWNERS = 8
OWN = WIDTH // OWNERS
PANEL = OWN + 16
QUART = FF // BLK
STEP = 256
BACK_STEP = 512


def swap(array, axis, by):
    peers = lax.axis_size(axis)
    return lax.ppermute(array, axis, [(i, i ^ by) for i in range(peers)])


def cross(array, by):
    peers = lax.axis_size("dp") * lax.axis_size("blk")
    return lax.ppermute(array, ("dp", "blk"), [(i, i ^ by) for i in range(peers)])


def after(array, *others):
    return lax.optimization_barrier((array, *others))[0]


def vm():
    return pl.BlockSpec(memory_space=pltpu.VMEM)


def anyspace():
    return pl.BlockSpec(memory_space=pl.ANY)


def smem():
    return pl.BlockSpec(memory_space=pltpu.SMEM)


def call(kernel, outs, args, scratch=(), flops=0, in_any=()):
    specs = [smem()] + [anyspace() if i in in_any else vm() for i in range(1, len(args))]
    nbytes = sum(a.size * a.dtype.itemsize for a in args) + sum(
        o.size * o.dtype.itemsize for o in outs
    )
    nbytes = nbytes if flops else 1
    return pl.pallas_call(
        kernel,
        name=getattr(kernel, "func", kernel).__name__,
        out_shape=outs,
        in_specs=specs,
        out_specs=[vm() for _ in outs],
        scratch_shapes=list(scratch),
        cost_estimate=pl.CostEstimate(
            flops=flops, bytes_accessed=nbytes, transcendentals=0
        ),
        compiler_params=pltpu.CompilerParams(vmem_limit_bytes=VMEM_LIMIT),
    )(*args)


def sds(shape, dtype):
    return jax.ShapeDtypeStruct(shape, dtype)


def nn(a, b):
    return lax.dot_general(a, b, (((1,), (0,)), ((), ())), preferred_element_type=F32)


def nt(a, b):
    return lax.dot_general(a, b, (((1,), (1,)), ((), ())), preferred_element_type=F32)


def tn(a, b):
    return lax.dot_general(a, b, (((0,), (0,)), ((), ())), preferred_element_type=F32)


def rows_at(index, size):
    return pl.ds(pl.multiple_of(index * size, 32), size)


def vec(vv_ref, row, lane):
    return jnp.concatenate(
        [vv_ref[o].astype(F32)[row : row + 1, lane : lane + OWN] for o in range(OWNERS)], axis=1
    )


def norm_stats(v):
    mean = jnp.mean(v, axis=-1, keepdims=True)
    cen = v - mean
    var = jnp.mean(cen * cen, axis=-1, keepdims=True)
    r = lax.rsqrt(var + 1e-12)
    return cen * r, r


def norm_kernel(tab, x_ref, n_ref):
    n_ref[...] = norm_stats(x_ref[...])[0].astype(BF16)


def prep_kernel(tab, x_ref, w_ref, *rest):
    vectors, (n_ref, panel_ref) = rest[:9], rest[9:]
    z = tab[1]
    rows = [v[...].astype(F32).reshape(1, v.shape[0]) for v in vectors]
    panel_ref[OWN:, :] = jnp.concatenate(
        [
            jnp.concatenate(rows[:6], axis=1),
            jnp.concatenate(rows[6:], axis=1),
            jnp.zeros((14, 3 * HW), F32),
        ],
        axis=0,
    ).astype(BF16)
    for k in range(ULY):

        @pl.when(z == k)
        def _():
            parts = [w_ref[:, p * WIDTH + k * HW : p * WIDTH + (k + 1) * HW] for p in range(3)]
            panel_ref[:OWN, :] = jnp.concatenate(parts, axis=1)

    n_ref[...] = norm_stats(x_ref[...])[0].astype(BF16)


def quarter(index):
    return pl.ds(pl.multiple_of(index * QUART, 128), QUART)


def ffn_prep_kernel(tab, u_ref, d_ref, *outs):
    b = tab[3]
    for s, ref in enumerate(outs):
        q = quarter(jnp.bitwise_xor(b, s))
        ref[0] = u_ref[:, q]
        ref[1] = d_ref[:, q]


def qkv_kernel(owner_bits, tab, n0, n1, n2, n3, *rest):
    arrays = rest[: len(owner_bits)]
    q_ref, kv_ref, h_ref, w_ref, vv_ref = rest[len(owner_bits) :]
    me, z = tab[0], tab[1]
    for ref, bits in zip(arrays, owner_bits):
        for i, bit in enumerate(bits):
            o = jnp.bitwise_xor(me, bit)
            w_ref[rows_at(o, OWN), :] = ref[i, :OWN, :]
            vv_ref[o] = ref[i, OWN:PANEL, :]
    gain = vec(vv_ref, 0, 0)
    shift = vec(vv_ref, 0, OWN)
    lo = vv_ref[2 * z].astype(F32)
    hi = vv_ref[2 * z + 1].astype(F32)
    zero = jnp.zeros((1, HW), F32)
    bias = jnp.concatenate(
        [
            lo[0:1, 2 * OWN : 3 * OWN],
            hi[0:1, 2 * OWN : 3 * OWN],
            zero,
            lo[0:1, 3 * OWN : 4 * OWN],
            hi[0:1, 3 * OWN : 4 * OWN],
        ],
        axis=1,
    )
    for i, ref in enumerate((n0, n1, n2, n3)):
        rows = slice(i * ROWS, (i + 1) * ROWS)
        h = (ref[...].astype(F32) * gain + shift).astype(BF16)
        h_ref[rows, :] = h
        proj = (nn(h, w_ref[...]) + bias).astype(BF16)
        q_ref[rows, :] = proj[:, :HW] * jnp.asarray(HEAD_DIM ** (-0.5), BF16)
        kv_ref[rows, :] = proj[:, HW:]


def placed(piece, upper):
    zero = jnp.zeros_like(piece)
    return jnp.concatenate([zero, piece] if upper else [piece, zero], axis=1)


def head_cols(h):
    return slice(h * HEAD_DIM, (h + 1) * HEAD_DIM)


def window(index):
    lane = index * HEAD_DIM
    start = lane // 128 * 128
    return slice(start, start + 128), (lane % 128) >= 64


def attend_kernel(tab, q_ref, k0, k1, k2, k3, qc_ref, kc_ref, o0, o1, o2, o3, all_ref, lse_ref):
    kvs = (k0, k1, k2, k3)
    outs = (o0, o1, o2, o3)

    lane = lax.broadcasted_iota(jnp.int32, (STEP, 128), 1)

    def step(i, carry):
        rows = rows_at(i, STEP)
        code1 = qc_ref[rows, 0:1]
        code2 = qc_ref[rows, 1:2]
        masks = []
        for j in range(BLK):
            kc = kc_ref[0:1, j * GROUP : (j + 1) * GROUP]
            masks.append((kc == code1) | (kc == code2))
        heads = []
        lse = jnp.zeros((STEP, 128), F32)
        for h in range(LOCAL_HEADS):
            kwin, kup = window(h)
            vwin, vup = window(LOCAL_HEADS + h)
            qp = placed(q_ref[rows, head_cols(h)], kup)
            scores = [
                jnp.where(masks[j], nt(qp, kvs[j][:, kwin]), NEG) for j in range(BLK)
            ]
            top = functools.reduce(jnp.maximum, [jnp.max(s, axis=1, keepdims=True) for s in scores])
            total = jnp.zeros((STEP, 1), F32)
            acc = jnp.zeros((STEP, 128), F32)
            for j in range(BLK):
                e = jnp.exp(scores[j] - top)
                total = total + jnp.sum(e, axis=1, keepdims=True)
                acc = acc + nn(e.astype(BF16), kvs[j][:, vwin])
            acc = acc[:, 64:] if vup else acc[:, :64]
            heads.append((acc / total).astype(BF16))
            lse = jnp.where(lane == h, top + jnp.log(total), lse)
        all_ref[rows, :] = jnp.concatenate(heads, axis=1)
        lse_ref[rows, :] = lse
        return carry

    lax.fori_loop(0, GROUP // STEP, step, 0)
    for i in range(ULY):
        outs[i][...] = all_ref[i * ROWS : (i + 1) * ROWS, :]


def mix_kernel(plan, tab, a0, a1, a2, a3, x_ref, vv_ref, *rest):
    parts, (resid_ref, h_ref, ow_ref, sems) = rest[:-4], rest[-4:]
    me, z = tab[0], tab[1]
    copies = []
    for index, place, bit in plan:
        copy = pltpu.make_async_copy(
            parts[index].at[place],
            ow_ref.at[rows_at(jnp.bitwise_xor(me, bit), OWN), :],
            sems.at[len(copies)],
        )
        copy.start()
        copies.append(copy)
    acc = x_ref[...] + vec(vv_ref, 0, 4 * OWN)
    for copy in copies:
        copy.wait()
    for j, ref in enumerate((a0, a1, a2, a3)):
        acc = acc + nn(ref[...], ow_ref[rows_at(jnp.bitwise_xor(z, j), HW), :])
    resid_ref[...] = acc
    n, _ = norm_stats(acc)
    h_ref[...] = (n * vec(vv_ref, 0, 5 * OWN) + vec(vv_ref, 1, 0)).astype(BF16)


CHUNK = 256


def ffn_kernel(plan, tab, h0, h1, h2, h3, c0, c1, c2, c3, vv_ref, *rest):
    count = len(rest) - 16
    parts = rest[:count]
    act_ref, dhid_ref, ykeep, ysend, go_ref, g1, g2, g3 = rest[count : count + 8]
    u_ref, d_ref, hall, call_ref, bias_ref, yacc, gacc, sems = rest[count + 8 :]
    me, b = tab[0], tab[3]
    copies = []
    for u_place, d_place, bit in plan:
        rows = rows_at(jnp.bitwise_xor(me, bit), OWN)
        for (index, slot), target in ((u_place, u_ref), (d_place, d_ref)):
            copy = pltpu.make_async_copy(
                parts[index].at[slot], target.at[rows, :], sems.at[len(copies)]
            )
            copy.start()
            copies.append(copy)
    for i, (h_ref, c_ref) in enumerate(((h0, c0), (h1, c1), (h2, c2), (h3, c3))):
        rows = slice(i * ROWS, (i + 1) * ROWS)
        hall[rows, :] = h_ref[...]
        call_ref[rows, :] = c_ref[...]
    for k in range(2):
        bias_ref[:, k * 384 : (k + 1) * 384] = vv_ref[2 * b + k].astype(F32)[1:2, 192:576]
    yacc[...] = jnp.zeros_like(yacc)
    gacc[...] = jnp.zeros_like(gacc)
    for copy in copies:
        copy.wait()

    def step(k, carry):
        cols = pl.ds(pl.multiple_of(k * CHUNK, CHUNK), CHUNK)
        hid = nn(hall[...], u_ref[:, cols]) + bias_ref[:, cols]
        dact = nn(call_ref[...], d_ref[:, cols])
        cdf = 0.5 * (1.0 + lax.erf(hid * 0.7071067811865476))
        act = (hid * cdf).astype(BF16)
        pdf = jnp.exp(-0.5 * hid * hid) * 0.3989422804014327
        dhid = (dact * (cdf + hid * pdf)).astype(BF16)
        act_ref[:, cols] = act
        dhid_ref[:, cols] = dhid
        yacc[...] += nt(act, d_ref[:, cols])
        gacc[...] += nt(dhid, u_ref[:, cols])
        return carry

    lax.fori_loop(0, QUART // CHUNK, step, 0)
    for i, y_ref in enumerate((ykeep, ysend, ykeep, ysend)):
        y_ref[i // 2] = yacc[i * ROWS : (i + 1) * ROWS, :].astype(y_ref.dtype)
    for i, g_ref in enumerate((go_ref, g1, g2, g3)):
        g_ref[...] = gacc[i * ROWS : (i + 1) * ROWS, :].astype(g_ref.dtype)


def ffn_grad_kernel(tab, *refs):
    me = tab[0]
    h_refs, c_refs = refs[:4], refs[4:8]
    dhid_ref, act_ref, usend, ukeep, dthere, dhere, left, left2 = refs[8:]
    for i in range(BLK):
        left[:, i * ROWS : (i + 1) * ROWS] = h_refs[i][...].T
        left2[:, i * ROWS : (i + 1) * ROWS] = c_refs[i][...].T
    for source, right_ref, ref, bits in (
        (left, dhid_ref, usend, (4, 5, 6, 7)),
        (left, dhid_ref, ukeep, (0, 1, 2, 3)),
        (left2, act_ref, dthere, (2, 6, 3, 7)),
        (left2, act_ref, dhere, (0, 4, 1, 5)),
    ):
        for s, bit in enumerate(bits):
            o = jnp.bitwise_xor(me, bit)
            ref[s] = nn(source[rows_at(o, OWN), :], right_ref[...]).astype(BF16)


def back_mix_kernel(
    tab, resid_ref, cot_ref, go_ref, g1, g2, g3, ow_ref, vv_ref, dres_ref, dmix_ref, d0, d1, d2, d3, vs_ref
):
    z = tab[1]
    grad = go_ref[...] + g1[...].astype(F32) + g2[...].astype(F32) + g3[...].astype(F32)
    n, r = norm_stats(resid_ref[...])
    dn = grad * vec(vv_ref, 0, 5 * OWN)
    dres = cot_ref[...] + r * (
        dn
        - jnp.mean(dn, axis=-1, keepdims=True)
        - n * jnp.mean(dn * n, axis=-1, keepdims=True)
    )
    dres_ref[...] = dres
    dmix = dres.astype(BF16)
    dmix_ref[...] = dmix
    for j, ref in enumerate((d0, d1, d2, d3)):
        ref[...] = nt(dmix, ow_ref[rows_at(jnp.bitwise_xor(z, j), HW), :]).astype(BF16)
    vs_ref[0:1, :] = jnp.sum(dmix.astype(F32), axis=0, keepdims=True)
    vs_ref[1:2, :] = jnp.sum(grad * n, axis=0, keepdims=True)
    vs_ref[2:3, :] = jnp.sum(grad, axis=0, keepdims=True)
    vs_ref[3:8, :] = jnp.zeros((5, WIDTH), F32)


def out_grad_kernel(tab, a0, a1, a2, a3, dmix_ref, vs_ref, dhid_ref, c_ref, keep, send, left, vrow):
    me, z, b = tab[0], tab[1], tab[3]
    for j, ref in enumerate((a0, a1, a2, a3)):
        left[rows_at(jnp.bitwise_xor(z, j), HW), :] = ref[...].astype(F32).T.astype(BF16)
    vs = vs_ref[...]
    usum = jnp.sum(dhid_ref[...].astype(F32), axis=0, keepdims=True)
    csum = jnp.sum(c_ref[...].astype(F32), axis=0, keepdims=True)
    for o in range(OWNERS):
        part = usum[:, (o % 2) * 384 : (o % 2 + 1) * 384]
        row = jnp.concatenate(
            [vs[k : k + 1, o * OWN : (o + 1) * OWN] for k in range(3)]
            + [jnp.where(b == o // 2, part, 0.0), csum[:, o * OWN : (o + 1) * OWN]],
            axis=1,
        )
        vrow[o] = jnp.broadcast_to(row, (16, WIDTH)).astype(BF16)
    for ref, base in ((send, 1), (keep, 0)):
        for s in range(4):
            o = jnp.bitwise_xor(me, base + (s // 2) * 2 + (s % 2) * 4)
            ref[s, :OWN, :] = nn(left[rows_at(o, OWN), :], dmix_ref[...]).astype(BF16)
            ref[s, OWN:, :] = vrow[o]


def back_attend_kernel(
    tab,
    q_ref,
    k0,
    k1,
    k2,
    k3,
    g0,
    g1,
    g2,
    g3,
    all_ref,
    lse_ref,
    qr_ref,
    kcol_ref,
    dq_ref,
    keep,
    send,
    acc,
    gall,
):
    kvs = (k0, k1, k2, k3)
    acc[...] = jnp.zeros_like(acc)
    for i, g_ref in enumerate((g0, g1, g2, g3)):
        gall[i * ROWS : (i + 1) * ROWS, :] = g_ref[...]
    lane = lax.broadcasted_iota(jnp.int32, (BACK_STEP, 128), 1)

    def step(i, carry):
        rows = rows_at(i, BACK_STEP)
        prod = gall[rows, :].astype(F32) * all_ref[rows, :].astype(F32)
        stat = jnp.zeros((BACK_STEP, 128), F32)
        for h in range(LOCAL_HEADS):
            stat = jnp.where(
                lane == h, jnp.sum(prod[:, head_cols(h)], axis=1, keepdims=True), stat
            )
        rowdot = stat.T
        lse = lse_ref[rows, :].T
        code1 = qr_ref[0:1, rows]
        code2 = qr_ref[1:2, rows]
        dq = [jnp.zeros((BACK_STEP, 128), F32) for _ in range(LOCAL_HEADS)]
        for j in range(BLK):
            kc = kcol_ref[j * GROUP : (j + 1) * GROUP, :]
            mask = (kc == code1) | (kc == code2)
            for h in range(LOCAL_HEADS):
                kwin, kup = window(h)
                vwin, vup = window(LOCAL_HEADS + h)
                qp = placed(q_ref[rows, head_cols(h)], kup)
                gp = placed(gall[rows, head_cols(h)], vup)
                kk = kvs[j][:, kwin]
                scores = nt(kk, qp)
                p = jnp.where(mask, jnp.exp(scores - lse[h : h + 1, :]), 0.0)
                dp = nt(kvs[j][:, vwin], gp)
                ds = (p * (dp - rowdot[h : h + 1, :])).astype(BF16)
                acc[j, :, vwin] += nn(p.astype(BF16), gp)
                acc[j, :, kwin] += nn(ds, qp)
                dq[h] = dq[h] + tn(ds, kk)
        parts = []
        for h in range(LOCAL_HEADS):
            _, kup = window(h)
            parts.append(dq[h][:, 64:] if kup else dq[h][:, :64])
        dq_ref[rows, :] = (jnp.concatenate(parts, axis=1) * HEAD_DIM ** (-0.5)).astype(BF16)
        return carry

    lax.fori_loop(0, GROUP // BACK_STEP, step, 0)
    keep[0] = acc[0].astype(BF16)
    keep[1] = acc[2].astype(BF16)
    send[0] = acc[1].astype(BF16)
    send[1] = acc[3].astype(BF16)


def back_proj_kernel(
    tab, dq_ref, keep, got, recv, w_ref, n0, n1, n2, n3, dproj_ref, h0, h1, send, vs_ref
):
    dproj_ref[:, :HW] = dq_ref[...]
    total = keep[0].astype(F32) + got[0].astype(F32) + recv[...].astype(F32)
    dproj_ref[:, HW:] = total.astype(BF16)
    gain = jnp.zeros((1, WIDTH), F32)
    shift = jnp.zeros((1, WIDTH), F32)
    outs = (h0, h1, send.at[0], send.at[1])
    for i, (n_ref, out) in enumerate(zip((n0, n1, n2, n3), outs)):
        rows = slice(i * ROWS, (i + 1) * ROWS)
        grad = nt(dproj_ref[rows, :], w_ref[...])
        out[...] = grad.astype(out.dtype)
        gain = gain + jnp.sum(grad * n_ref[...].astype(F32), axis=0, keepdims=True)
        shift = shift + jnp.sum(grad, axis=0, keepdims=True)
    vs_ref[0:1, :] = gain
    vs_ref[1:2, :] = shift
    cols = jnp.sum(dproj_ref[...].astype(F32), axis=0, keepdims=True)
    vs_ref[2:3, :] = jnp.concatenate([cols, jnp.zeros((1, WIDTH - 3 * HW), F32)], axis=1)
    vs_ref[3:8, :] = jnp.zeros((5, WIDTH), F32)


def qkv_grad_kernel(tab, h_ref, dproj_ref, vs_ref, keep, send, left, vrow):
    me, z = tab[0], tab[1]
    vs = vs_ref[...]
    for o in range(OWNERS):
        row = [vs[k : k + 1, o * OWN : (o + 1) * OWN] for k in range(2)]
        for lane in (0, 2 * HW):
            lane = lane + (o % 2) * OWN
            row.append(jnp.where(z == o // 2, vs[2:3, lane : lane + OWN], 0.0))
        row.append(jnp.zeros((1, 3 * HW - 4 * OWN), F32))
        vrow[o] = jnp.broadcast_to(jnp.concatenate(row, axis=1), (16, 3 * HW)).astype(BF16)
    for i in range(ULY):
        rows = slice(i * ROWS, (i + 1) * ROWS)
        left[:, rows] = h_ref[rows, :].T
    for ref, base in ((keep, 0), (send, 1)):
        for s in range(4):
            o = jnp.bitwise_xor(me, base + (s // 2) * 2 + (s % 2) * 4)
            ref[s, :OWN, :] = nn(left[rows_at(o, OWN), :], dproj_ref[...]).astype(BF16)
            ref[s, OWN:, :] = vrow[o]


def back_norm_kernel(tab, x_ref, dres_ref, h0, got2, got1, vv_ref, out_ref):
    grad = h0[...] + got2[0].astype(F32) + got1[...].astype(F32)
    n, r = norm_stats(x_ref[...])
    dn = grad * vec(vv_ref, 0, 0)
    out_ref[...] = dres_ref[...] + r * (
        dn
        - jnp.mean(dn, axis=-1, keepdims=True)
        - n * jnp.mean(dn * n, axis=-1, keepdims=True)
    )


def output_kernel(tab, resid_ref, keep, got, last, vv_ref, out_ref):
    out_ref[...] = (
        resid_ref[...]
        + keep[0]
        + got[0].astype(F32)
        + last[...].astype(F32)
        + vec(vv_ref, 1, OWN)
    )


def low_sum(a, b):
    return (a.astype(F32) + b.astype(F32)).astype(BF16)


def split_kernel(bit, tab, a_ref, ac_ref, by_ref, byc_ref, keep, send):
    for value, low_out, high_out in ((0, keep, send), (1, send, keep)):

        @pl.when(tab[bit] == value)
        def _():
            low_out[0] = a_ref[0]
            low_out[1] = ac_ref[1]
            high_out[0] = by_ref[0]
            high_out[1] = byc_ref[1]


def pack_kernel(tab, a_ref, ac_ref, by_ref, byc_ref, out_ref):
    for s, (ref, place) in enumerate(((a_ref, 1), (ac_ref, 3), (by_ref, 1), (byc_ref, 3))):
        out_ref[s] = ref[place]


def split_add_kernel(bit, tab, a_ref, ac_ref, by_ref, byc_ref, got, keep, send):
    refs = ((a_ref, 0), (ac_ref, 2), (by_ref, 0), (byc_ref, 2))
    for value, low_out, high_out in ((0, keep, send), (1, send, keep)):

        @pl.when(tab[bit] == value)
        def _():
            for s, (ref, place) in enumerate(refs):
                (low_out, high_out)[s // 2][s % 2] = low_sum(ref[place], got[s])


def merge_kernel(bit, tab, a_ref, b_ref, keep, send):
    for value, low_out, high_out in ((0, keep, send), (1, send, keep)):

        @pl.when(tab[bit] == value)
        def _():
            low_out[...] = low_sum(a_ref[0], b_ref[0])
            high_out[...] = low_sum(a_ref[1], b_ref[1])


def final_kernel(tab, pair, got, out_ref):
    b, odd, high = tab[3], tab[4], tab[5]
    for flip, ref in ((0, pair.at[0]), (1, pair.at[1]), (2, got.at[0]), (3, got.at[1])):
        q = jnp.bitwise_xor(jnp.bitwise_xor(b, 2 * odd + high), flip)
        out_ref[:, quarter(q)] = ref[...].astype(F32)


def qkv_final_kernel(tab, pair, got, out_ref, vec_ref):
    z = tab[1]
    refs = (pair.at[0], pair.at[1], got.at[0], got.at[1])
    for k in range(ULY):

        @pl.when(z == k)
        def _():
            for p in range(3):
                cols = [
                    refs[t ^ k][:OWN, p * HW : (p + 1) * HW].astype(F32) for t in range(ULY)
                ]
                out_ref[:, p * WIDTH : (p + 1) * WIDTH] = jnp.concatenate(cols, axis=1)

    total = jnp.zeros((16, 3 * HW), F32)
    for ref in refs:
        total = total + ref[OWN:, :].astype(F32)
    vec_ref[...] = total[:8, :]


def add_low(a, b):
    return (a.astype(F32) + b.astype(F32)).astype(BF16)


def xor_order(array, axis, index):
    shape = array.shape
    two = array.reshape(shape[:axis] + (2, 2) + shape[axis + 1 :])
    two = jnp.where((index & 1) == 1, jnp.flip(two, axis + 1), two)
    two = jnp.where((index & 2) == 2, jnp.flip(two, axis), two)
    return two.reshape(shape)


def body(
    inputs,
    cotangent,
    qkv_weight,
    query_bias,
    value_bias,
    out_weight,
    out_bias,
    norm1_gain,
    norm1_bias,
    norm2_gain,
    norm2_bias,
    up_weight,
    up_bias,
    down_weight,
    down_bias,
    doc_lengths,
    pad_mask,
):
    dp_count = lax.axis_size("dp")
    near = dp_count == 2
    dp = lax.axis_index("dp")
    z = lax.axis_index("uly")
    b = lax.axis_index("blk")
    core = b & 1
    rank = dp * BLK + b
    me = rank if near else jnp.int32(0)
    tab = jnp.stack([me, z, core, b, z & 1, z >> 1]).astype(jnp.int32)
    own_rows = WIDTH // (dp_count * BLK)
    axes = ("dp", "blk")

    x = inputs.reshape(ROWS, WIDTH)
    cot = cotangent.reshape(ROWS, WIDTH)

    if near:
        vectors = [norm1_gain, norm1_bias, query_bias, value_bias, out_bias, norm2_gain]
        vectors += [norm2_bias, down_bias, up_bias]
        n0, panel = call(
            prep_kernel,
            [sds((ROWS, WIDTH), BF16), sds((PANEL, 3 * HW), BF16)],
            [tab, x, qkv_weight, *vectors],
        )
        n1, n2, n3 = (swap(n0, "uly", k) for k in (1, 2, 3))
        a_0 = jnp.stack([panel, swap(panel, "dp", 1)])
        a_2 = swap(a_0, "blk", 2)
        four_bits = [[0, 4], [2, 6], [1, 5], [3, 7]]
        w_mine = call(
            ffn_prep_kernel,
            [sds((2, OWN, QUART), BF16)] * BLK,
            [tab, up_weight, down_weight.T],
        )
        n1 = after(n1, w_mine[0])
        a_2c = swap(a_2, "blk", 1)
        a_0c = swap(after(a_0, a_2c), "blk", 1)
        a_parts = [a_0, a_2, a_0c, a_2c]
        w_parts = [w_mine[0], None, cross(after(w_mine[2], a_0c), 2)] + [None] * 5
        w_plan = [((i, 0), (i, 1), i) for i in range(OWNERS)]
        o_plan = [
            (i, k, bit) for i, bits in enumerate(four_bits) for k, bit in enumerate(bits)
        ]
    else:
        (n0,) = call(norm_kernel, [sds((ROWS, WIDTH), BF16)], [tab, x])
        n1, n2, n3 = (swap(n0, "uly", k) for k in (1, 2, 3))
        qkv_cols = lax.dynamic_index_in_dim(
            qkv_weight.reshape(own_rows, 3, ULY, HW), z, axis=2, keepdims=False
        ).reshape(own_rows, 3 * HW)

        def full(array):
            return lax.all_gather(array, axes, axis=0, tiled=True)

        def eight(vector):
            return full(vector).reshape(OWNERS, 1, -1)

        def mine(array):
            cols = full(array).reshape(WIDTH, BLK, QUART)
            return lax.dynamic_index_in_dim(cols, b, 1, False).reshape(OWNERS, OWN, QUART)

        row0 = jnp.concatenate(
            [
                eight(v)
                for v in (norm1_gain, norm1_bias, query_bias, value_bias, out_bias, norm2_gain)
            ],
            axis=2,
        )
        row1 = jnp.concatenate([eight(v) for v in (norm2_bias, down_bias, up_bias)], axis=2)
        a_parts = [
            jnp.concatenate(
                [
                    full(qkv_cols).reshape(OWNERS, OWN, 3 * HW),
                    row0,
                    row1,
                    jnp.zeros((OWNERS, 14, 3 * HW), BF16),
                ],
                axis=1,
            )
        ]
        four_bits = [list(range(OWNERS))]
        o_parts = [full(out_weight).reshape(OWNERS, OWN, WIDTH)]
        w_parts = [mine(up_weight), mine(down_weight.T)]
        w_plan = [((0, o), (1, o), o) for o in range(OWNERS)]
        o_plan = [(0, o, o) for o in range(OWNERS)]

    ends = jnp.cumsum(doc_lengths.reshape(-1), dtype=jnp.int32)
    zs = jnp.arange(ULY, dtype=jnp.int32) ^ z
    bs = jnp.arange(BLK, dtype=jnp.int32) ^ b
    within = jnp.arange(ROWS, dtype=jnp.int32)
    kplace = ((zs[None, :, None] * BLK + bs[:, None, None]) * ROWS + within).reshape(KEYS)
    kseg = jnp.sum((kplace[:, None] >= ends[None, :]).astype(jnp.int32), axis=1)
    valid = pad_mask.reshape(ULY, BLK, ROWS)
    valid = xor_order(xor_order(valid, 0, z), 1, b).transpose(1, 0, 2).reshape(KEYS)
    kcode = jnp.where(valid > 0, kseg, kplace + 64)
    qcodes = jnp.stack([kseg[:GROUP], kplace[:GROUP] + 64])

    n1, q_cols, q_rows, k_cols, k_rows = lax.optimization_barrier(
        (n1, qcodes.T, qcodes, kcode[:, None], kcode[None, :])
    )
    q, kv, h1, w_qkv, vv = call(
        functools.partial(qkv_kernel, four_bits),
        [
            sds((GROUP, HW), BF16),
            sds((GROUP, 2 * HW), BF16),
            sds((GROUP, WIDTH), BF16),
            sds((WIDTH, 3 * HW), BF16),
            sds((OWNERS, 16, 3 * HW), BF16),
        ],
        [tab, n0, n1, n2, n3, *a_parts],
        flops=2 * GROUP * WIDTH * 3 * HW,
    )
    cb = cot.astype(BF16)
    if near:
        kv_y = swap(after(kv, w_parts[2]), "blk", 2)
        cb_y = swap(after(cb, kv_y), "blk", 2)
        w_parts[4] = cross(after(w_mine[0], kv), 4)
        w_parts[5] = cross(after(w_mine[1], kv), 5)
        o_0 = jnp.stack([out_weight, swap(after(out_weight, kv), "dp", 1)])
        o_0c = swap(o_0, "blk", 1)
        o_2 = swap(after(o_0, kv_y), "blk", 2)
    else:
        kv_y = swap(kv, "blk", 2)
    kv_c = swap(kv, "blk", 1)
    kv_yc = swap(kv_y, "blk", 1)
    if near:
        cb_c = swap(after(cb, kv), "blk", 1)
        w_parts[1] = cross(after(w_mine[1], kv), 1)
        kv_yc = after(kv_yc, o_0c, w_parts[1], cb_c)
    kvs = [kv, kv_c, kv_y, kv_yc]

    def around(array):
        near_y = swap(array, "blk", 2)
        return [array, swap(array, "blk", 1), near_y, swap(near_y, "blk", 1)]

    if near:
        w_parts[3] = cross(after(w_mine[3], kv_y), 3)
    else:
        cbs = around(cb)

    *attn_slots, attn_all, lse = call(
        attend_kernel,
        [sds((ROWS, HW), BF16)] * ULY + [sds((GROUP, HW), BF16), sds((GROUP, 128), F32)],
        [tab, q, *kvs, q_cols, k_rows],
        flops=4 * GROUP * KEYS * HW,
    )
    if near:
        attn_slots = after(attn_slots, w_parts[4], w_parts[5], o_2)
        o_2c = swap(after(o_2, attn_slots[0]), "blk", 1)
        o_parts = [o_0, o_2, o_0c, o_2c]
    attn = [attn_slots[0]] + [swap(attn_slots[k], "uly", k) for k in (1, 2, 3)]
    resid, h2, ow = call(
        functools.partial(mix_kernel, o_plan),
        [sds((ROWS, WIDTH), F32), sds((ROWS, WIDTH), BF16), sds((WIDTH, WIDTH), BF16)],
        [tab, *attn, x, vv, *o_parts],
        scratch=[pltpu.SemaphoreType.DMA((OWNERS,))],
        flops=2 * ROWS * WIDTH * WIDTH,
        in_any=range(7, 7 + len(o_parts)),
    )

    if near:
        w_parts[6] = cross(after(w_mine[2], attn[1]), 6)
        w_parts[7] = cross(after(w_mine[3], attn[2], cb_y, w_parts[3]), 7)
        h2 = after(h2, w_parts[6], w_parts[7])
        cbs = [cb, cb_c, cb_y, swap(after(cb_y, h2), "blk", 1)]
    h2s = around(h2)
    parts = len(w_parts)
    act, dhid, y_keep, y_send, go, *gs = call(
        functools.partial(ffn_kernel, w_plan),
        [sds((GROUP, QUART), BF16)] * 2
        + [sds((2, ROWS, WIDTH), F32), sds((2, ROWS, WIDTH), BF16), sds((ROWS, WIDTH), F32)]
        + [sds((ROWS, WIDTH), BF16)] * 3,
        [tab, *h2s, *cbs, vv, *w_parts],
        scratch=[
            pltpu.VMEM((WIDTH, QUART), BF16),
            pltpu.VMEM((WIDTH, QUART), BF16),
            pltpu.VMEM((GROUP, WIDTH), BF16),
            pltpu.VMEM((GROUP, WIDTH), BF16),
            pltpu.VMEM((1, QUART), F32),
            pltpu.VMEM((GROUP, WIDTH), F32),
            pltpu.VMEM((GROUP, WIDTH), F32),
            pltpu.SemaphoreType.DMA((2 * OWNERS,)),
        ],
        flops=8 * GROUP * WIDTH * QUART,
        in_any=range(10, 10 + parts),
    )
    gs = [swap(g, "blk", k) for k, g in enumerate(gs, 1)]

    y_got = swap(y_send, "blk", 1)
    y_part = (y_keep[1] + y_got[1].astype(F32)).astype(BF16)
    usend, ukeep, dthere, dhere = call(
        ffn_grad_kernel,
        [sds((BLK, OWN, QUART), BF16)] * 4,
        [tab, *h2s, *cbs, dhid, act],
        scratch=[pltpu.VMEM((WIDTH, GROUP), BF16)] * 2,
    )
    go = after(go, usend, dthere, y_part)

    dres, dmix, *dattn_slots, vs2 = call(
        back_mix_kernel,
        [sds((ROWS, WIDTH), F32), sds((ROWS, WIDTH), BF16)]
        + [sds((ROWS, HW), BF16)] * ULY
        + [sds((8, WIDTH), F32)],
        [tab, resid, cot, go, *gs, ow, vv],
        flops=2 * ROWS * WIDTH * WIDTH,
    )
    pair = sds((2, OWN, QUART), BF16)
    one = sds((OWN, QUART), BF16)
    dattn = [dattn_slots[0]] + [swap(dattn_slots[k], "uly", k) for k in (1, 2, 3)]
    if near:
        u_got = swap(usend, "dp", 1)
        d_there = swap(after(dthere, dmix), "blk", 2)
    y_last = swap(after(y_part, dattn[1]), "blk", 2)

    dq, keep_kv, send_kv = call(
        back_attend_kernel,
        [sds((GROUP, HW), BF16), sds((2, GROUP, 2 * HW), BF16), sds((2, GROUP, 2 * HW), BF16)],
        [tab, q, *kvs, *dattn, attn_all, lse, q_rows, k_cols],
        scratch=[pltpu.VMEM((BLK, GROUP, 2 * HW), F32), pltpu.VMEM((GROUP, HW), BF16)],
        flops=10 * GROUP * KEYS * HW,
    )
    if near:
        send_kv = after(send_kv, d_there, y_last)
    got = swap(send_kv, "blk", 1)
    kv_send = add_low(keep_kv[1], got[1])
    kv_got = swap(kv_send, "blk", 2)
    okeep, osend = call(
        out_grad_kernel,
        [sds((4, PANEL, WIDTH), BF16)] * 2,
        [tab, *attn, after(dmix, kv_send), vs2, dhid, cb],
        scratch=[pltpu.VMEM((WIDTH, ROWS), BF16), pltpu.VMEM((OWNERS, 16, WIDTH), BF16)],
    )

    if near:
        dhere, d_there = after(dhere, kv_send), after(d_there, kv_send)
        pieces = [dhere, swap(dhere, "blk", 1), d_there, swap(d_there, "blk", 1)]
        (d_send,) = call(pack_kernel, [sds((BLK, OWN, QUART), BF16)], [tab, *pieces])
        dq = after(dq, d_send, okeep)
    dproj, g_own, g_one, g_send, vs1 = call(
        back_proj_kernel,
        [sds((GROUP, 3 * HW), BF16)]
        + [sds((ROWS, WIDTH), F32)] * 2
        + [sds((2, ROWS, WIDTH), BF16), sds((8, WIDTH), F32)],
        [tab, dq, keep_kv, got, kv_got, w_qkv, n0, n1, n2, n3],
        flops=2 * GROUP * WIDTH * 3 * HW,
    )
    qkeep, qsend = call(
        qkv_grad_kernel,
        [sds((4, PANEL, 3 * HW), BF16)] * 2,
        [tab, h1, dproj, vs1],
        scratch=[pltpu.VMEM((WIDTH, GROUP), BF16), pltpu.VMEM((OWNERS, 16, 3 * HW), BF16)],
    )
    (output,) = call(
        output_kernel,
        [sds((ROWS, WIDTH), F32)],
        [tab, after(resid, dproj), y_keep, y_got, y_last, vv],
    )
    if near:
        o1 = add_low(okeep, swap(after(osend, dproj), "blk", 1))
        u_got = after(u_got, dproj)
        u_there = add_low(ukeep[2:], u_got[2:])
        u_here = add_low(ukeep[:2], u_got[:2])
        q1 = add_low(qkeep, swap(qsend, "blk", 1))
        u_there = swap(u_there, "blk", 2)
        upieces = [u_here, swap(u_here, "blk", 1), u_there, swap(u_there, "blk", 1)]
        ukept, usent = call(functools.partial(split_kernel, 4), [pair] * 2, [tab, *upieces])
        dkept, dsent = call(
            functools.partial(split_add_kernel, 4),
            [pair] * 2,
            [tab, *pieces, after(swap(d_send, "dp", 1), dproj)],
        )
        gates = [q1, dsent, usent]
    else:
        gates = []
    g_got = after(swap(g_send, "uly", 2), *gates)
    g_last = swap((g_one + g_got[1].astype(F32)).astype(BF16), "uly", 1)
    if near:

        def over_uly(kept, sent):
            return call(
                functools.partial(merge_kernel, 5),
                [one] * 2,
                [tab, kept, after(swap(sent, "uly", 1), g_got)],
            )

        def share(total):
            pair = jnp.stack([total, swap(total, "uly", 2)])
            return call(
                final_kernel, [sds((OWN, FF), F32)], [tab, pair, swap(pair, "uly", 1)]
            )[0]

        dkept, dsent = over_uly(dkept, dsent)
        ukept, usent = over_uly(ukept, usent)
        d_total = add_low(dkept, swap(dsent, "uly", 2))
        u_mid = swap(usent, "uly", 2)
        g_last = after(g_last, d_total, usent, output)

        o2 = add_low(o1[:2], swap(o1[2:], "blk", 2))
        o3 = add_low(o2[0], swap(o2[1], "dp", 1))
        u_total = add_low(after(ukept, o3), u_mid)
        grad_down = share(d_total).T
        grad_up = share(u_total)
        o4 = add_low(o3, swap(after(o3, d_total), "uly", 1))
        o5 = o4.astype(F32) + swap(o4, "uly", 2).astype(F32)
        grad_ow = o5[:OWN]
        grad_obias, grad_gain2, grad_shift2 = (o5[OWN, k * OWN : (k + 1) * OWN] for k in range(3))
        grad_ubias, grad_dbias = o5[OWN, 288:672], o5[OWN, 672:768]

        q2 = add_low(q1[:2], swap(q1[2:], "blk", 2))
        q3 = add_low(q2[0], swap(q2[1], "dp", 1))
        q_pair = jnp.stack([q3, swap(q3, "uly", 1)])
        grad_qkv, qvec = call(
            qkv_final_kernel,
            [sds((OWN, 3 * WIDTH), F32), sds((8, 3 * HW), F32)],
            [tab, q_pair, swap(after(q_pair, u_total), "uly", 2)],
        )
        grad_gain1, grad_shift1, grad_qbias, grad_vbias = (
            qvec[0, k * OWN : (k + 1) * OWN] for k in range(4)
        )
    else:

        def owned(array):
            shard = lax.psum_scatter(
                array.astype(F32), axes, scatter_dimension=0, tiled=True
            )
            return lax.psum(shard.astype(BF16), "uly").astype(F32)

        def by_owner(keep, send, order):
            both = jnp.concatenate([keep, send], axis=0)
            return both[jnp.array(order)]

        o8 = by_owner(okeep, osend, [0, 4, 2, 6, 1, 5, 3, 7])
        q8 = by_owner(qkeep, qsend, [0, 4, 2, 6, 1, 5, 3, 7])

        def widen(keep, send, order):
            flat = jnp.concatenate([keep, send], axis=0)[jnp.array(order)]
            flat = flat.reshape(WIDTH, 1, QUART)
            place = (jnp.arange(BLK) == b)[None, :, None]
            return jnp.where(place, flat, jnp.zeros_like(flat)).reshape(WIDTH, FF)

        grad_up = owned(widen(ukeep, usend, range(OWNERS)))
        grad_down = owned(widen(dhere, dthere, [0, 2, 4, 6, 1, 3, 5, 7])).T
        grad_ubias = owned(o8[:, OWN, 288:672].reshape(FF))
        grad_dbias = owned(o8[:, OWN, 672:768].reshape(WIDTH))
        grad_ow = owned(o8[:, :OWN].reshape(WIDTH, WIDTH))
        grad_obias, grad_gain2, grad_shift2 = (
            owned(o8[:, OWN, k * OWN : (k + 1) * OWN].reshape(WIDTH)) for k in range(3)
        )
        mine = q8[:, :OWN].reshape(WIDTH, 3, 1, HW)
        spread = jnp.where(
            (jnp.arange(ULY) == z)[None, None, :, None], mine, jnp.zeros_like(mine)
        )
        grad_qkv = owned(spread.reshape(WIDTH, 3 * WIDTH))
        grad_gain1, grad_shift1, grad_qbias, grad_vbias = (
            owned(q8[:, OWN, k * OWN : (k + 1) * OWN].reshape(WIDTH)) for k in range(4)
        )

    (grad_inputs,) = call(
        back_norm_kernel, [sds((ROWS, WIDTH), F32)], [tab, x, dres, g_own, g_got, g_last, vv]
    )
    return (
        output.reshape(inputs.shape),
        grad_inputs.reshape(inputs.shape),
        grad_qkv,
        grad_qbias,
        grad_vbias,
        grad_ow,
        grad_obias,
        grad_gain1,
        grad_shift1,
        grad_gain2,
        grad_shift2,
        grad_up,
        grad_ubias,
        grad_down,
        grad_dbias,
    )


def solution(mesh):
    rows = P(None, ("dp", "uly", "blk"), None)
    first = P(("dp", "blk"), None)
    flat = P(("dp", "blk"))
    second = P(None, ("dp", "blk"))
    return jax.shard_map(
        body,
        mesh=mesh,
        in_specs=(
            rows,
            rows,
            first,
            flat,
            flat,
            first,
            flat,
            flat,
            flat,
            flat,
            flat,
            first,
            flat,
            second,
            flat,
            P(None, "dp", None),
            P(None, "dp"),
        ),
        out_specs=(
            rows,
            rows,
            first,
            flat,
            flat,
            first,
            flat,
            flat,
            flat,
            flat,
            flat,
            first,
            flat,
            second,
            flat,
        ),
        check_vma=False,
    )
```

```python
import functools

import jax
import jax.numpy as jnp
from jax import lax
from jax.experimental import pallas as pl
from jax.experimental.pallas import tpu as pltpu
from jax.sharding import PartitionSpec as P

HEADS = 12
HEAD_DIM = 64
FF = 3072
F32 = jnp.float32
BF16 = jnp.bfloat16
NEG = -1e30
VMEM_LIMIT = 60 * 1024 * 1024

ROWS = 128
ULY = 4
BLK = 4
GROUP = ROWS * ULY
KEYS = GROUP * BLK
WIDTH = HEADS * HEAD_DIM
HW = WIDTH // ULY
LOCAL_HEADS = HEADS // ULY
OWNERS = 8
OWN = WIDTH // OWNERS
PANEL = OWN + 16
QUART = FF // BLK
STEP = 512
BACK_STEP = 512


def swap(array, axis, by):
    peers = lax.axis_size(axis)
    return lax.ppermute(array, axis, [(i, i ^ by) for i in range(peers)])


def cross(array, by):
    peers = lax.axis_size("dp") * lax.axis_size("blk")
    return lax.ppermute(array, ("dp", "blk"), [(i, i ^ by) for i in range(peers)])


def after(array, *others):
    return lax.optimization_barrier((array, *others))[0]


def vm():
    return pl.BlockSpec(memory_space=pltpu.VMEM)


def anyspace():
    return pl.BlockSpec(memory_space=pl.ANY)


def smem():
    return pl.BlockSpec(memory_space=pltpu.SMEM)


def call(kernel, outs, args, scratch=(), flops=0, in_any=()):
    specs = [smem()] + [anyspace() if i in in_any else vm() for i in range(1, len(args))]
    nbytes = sum(a.size * a.dtype.itemsize for a in args) + sum(
        o.size * o.dtype.itemsize for o in outs
    )
    nbytes = nbytes if flops else 1
    return pl.pallas_call(
        kernel,
        name=getattr(kernel, "func", kernel).__name__,
        out_shape=outs,
        in_specs=specs,
        out_specs=[vm() for _ in outs],
        scratch_shapes=list(scratch),
        cost_estimate=pl.CostEstimate(
            flops=flops, bytes_accessed=nbytes, transcendentals=0
        ),
        compiler_params=pltpu.CompilerParams(vmem_limit_bytes=VMEM_LIMIT),
    )(*args)


def sds(shape, dtype):
    return jax.ShapeDtypeStruct(shape, dtype)


def nn(a, b):
    return lax.dot_general(a, b, (((1,), (0,)), ((), ())), preferred_element_type=F32)


def nt(a, b):
    return lax.dot_general(a, b, (((1,), (1,)), ((), ())), preferred_element_type=F32)


def tn(a, b):
    return lax.dot_general(a, b, (((0,), (0,)), ((), ())), preferred_element_type=F32)


def rows_at(index, size):
    return pl.ds(pl.multiple_of(index * size, 32), size)


def vec(vv_ref, row, lane):
    return jnp.concatenate(
        [vv_ref[o].astype(F32)[row : row + 1, lane : lane + OWN] for o in range(OWNERS)], axis=1
    )


def norm_stats(v):
    mean = jnp.mean(v, axis=-1, keepdims=True)
    cen = v - mean
    var = jnp.mean(cen * cen, axis=-1, keepdims=True)
    r = lax.rsqrt(var + 1e-12)
    return cen * r, r


def norm_kernel(tab, x_ref, n_ref):
    n_ref[...] = norm_stats(x_ref[...])[0].astype(BF16)


def prep_kernel(tab, x_ref, w_ref, *rest):
    vectors, (n_ref, panel_ref) = rest[:9], rest[9:]
    z = tab[1]
    rows = [v[...].astype(F32).reshape(1, v.shape[0]) for v in vectors]
    panel_ref[OWN:, :] = jnp.concatenate(
        [
            jnp.concatenate(rows[:6], axis=1),
            jnp.concatenate(rows[6:], axis=1),
            jnp.zeros((14, 3 * HW), F32),
        ],
        axis=0,
    ).astype(BF16)
    for k in range(ULY):

        @pl.when(z == k)
        def _():
            parts = [w_ref[:, p * WIDTH + k * HW : p * WIDTH + (k + 1) * HW] for p in range(3)]
            panel_ref[:OWN, :] = jnp.concatenate(parts, axis=1)

    n_ref[...] = norm_stats(x_ref[...])[0].astype(BF16)


def quarter(index):
    return pl.ds(pl.multiple_of(index * QUART, 128), QUART)


def ffn_prep_kernel(tab, u_ref, d_ref, *outs):
    b = tab[3]
    for s, ref in enumerate(outs):
        q = quarter(jnp.bitwise_xor(b, s))
        ref[0] = u_ref[:, q]
        ref[1] = d_ref[:, q]


def qkv_kernel(owner_bits, tab, n0, n1, n2, n3, *rest):
    arrays = rest[: len(owner_bits)]
    q_ref, kv_ref, h_ref, w_ref, vv_ref = rest[len(owner_bits) :]
    me, z = tab[0], tab[1]
    for ref, bits in zip(arrays, owner_bits):
        for i, bit in enumerate(bits):
            o = jnp.bitwise_xor(me, bit)
            w_ref[rows_at(o, OWN), :] = ref[i, :OWN, :]
            vv_ref[o] = ref[i, OWN:PANEL, :]
    gain = vec(vv_ref, 0, 0)
    shift = vec(vv_ref, 0, OWN)
    lo = vv_ref[2 * z].astype(F32)
    hi = vv_ref[2 * z + 1].astype(F32)
    zero = jnp.zeros((1, HW), F32)
    bias = jnp.concatenate(
        [
            lo[0:1, 2 * OWN : 3 * OWN],
            hi[0:1, 2 * OWN : 3 * OWN],
            zero,
            lo[0:1, 3 * OWN : 4 * OWN],
            hi[0:1, 3 * OWN : 4 * OWN],
        ],
        axis=1,
    )
    for i, ref in enumerate((n0, n1, n2, n3)):
        rows = slice(i * ROWS, (i + 1) * ROWS)
        h = (ref[...].astype(F32) * gain + shift).astype(BF16)
        h_ref[rows, :] = h
        proj = (nn(h, w_ref[...]) + bias).astype(BF16)
        q_ref[rows, :] = proj[:, :HW] * jnp.asarray(HEAD_DIM ** (-0.5), BF16)
        kv_ref[rows, :] = proj[:, HW:]


def placed(piece, upper):
    zero = jnp.zeros_like(piece)
    return jnp.concatenate([zero, piece] if upper else [piece, zero], axis=1)


def head_cols(h):
    return slice(h * HEAD_DIM, (h + 1) * HEAD_DIM)


def window(index):
    lane = index * HEAD_DIM
    start = lane // 128 * 128
    return slice(start, start + 128), (lane % 128) >= 64


def attend_kernel(tab, q_ref, k0, k1, k2, k3, qc_ref, kc_ref, o0, o1, o2, o3, all_ref, lse_ref):
    kvs = (k0, k1, k2, k3)
    outs = (o0, o1, o2, o3)

    lane = lax.broadcasted_iota(jnp.int32, (STEP, 128), 1)

    def step(i, carry):
        rows = rows_at(i, STEP)
        code1 = qc_ref[rows, 0:1]
        code2 = qc_ref[rows, 1:2]
        masks = []
        for j in range(BLK):
            kc = kc_ref[0:1, j * GROUP : (j + 1) * GROUP]
            masks.append((kc == code1) | (kc == code2))
        heads = []
        lse = jnp.zeros((STEP, 128), F32)
        for h in range(LOCAL_HEADS):
            kwin, kup = window(h)
            vwin, vup = window(LOCAL_HEADS + h)
            qp = placed(q_ref[rows, head_cols(h)], kup)
            scores = [
                jnp.where(masks[j], nt(qp, kvs[j][:, kwin]), NEG) for j in range(BLK)
            ]
            top = functools.reduce(jnp.maximum, [jnp.max(s, axis=1, keepdims=True) for s in scores])
            total = jnp.zeros((STEP, 1), F32)
            acc = jnp.zeros((STEP, 128), F32)
            for j in range(BLK):
                e = jnp.exp(scores[j] - top)
                total = total + jnp.sum(e, axis=1, keepdims=True)
                acc = acc + nn(e.astype(BF16), kvs[j][:, vwin])
            acc = acc[:, 64:] if vup else acc[:, :64]
            heads.append((acc / total).astype(BF16))
            lse = jnp.where(lane == h, top + jnp.log(total), lse)
        all_ref[rows, :] = jnp.concatenate(heads, axis=1)
        lse_ref[rows, :] = lse
        return carry

    lax.fori_loop(0, GROUP // STEP, step, 0)
    for i in range(ULY):
        outs[i][...] = all_ref[i * ROWS : (i + 1) * ROWS, :]


def mix_kernel(plan, tab, a0, a1, a2, a3, x_ref, vv_ref, *rest):
    parts, (resid_ref, h_ref, ow_ref, sems) = rest[:-4], rest[-4:]
    me, z = tab[0], tab[1]
    copies = []
    for index, place, bit in plan:
        copy = pltpu.make_async_copy(
            parts[index].at[place],
            ow_ref.at[rows_at(jnp.bitwise_xor(me, bit), OWN), :],
            sems.at[len(copies)],
        )
        copy.start()
        copies.append(copy)
    acc = x_ref[...] + vec(vv_ref, 0, 4 * OWN)
    for copy in copies:
        copy.wait()
    for j, ref in enumerate((a0, a1, a2, a3)):
        acc = acc + nn(ref[...], ow_ref[rows_at(jnp.bitwise_xor(z, j), HW), :])
    resid_ref[...] = acc
    n, _ = norm_stats(acc)
    h_ref[...] = (n * vec(vv_ref, 0, 5 * OWN) + vec(vv_ref, 1, 0)).astype(BF16)


CHUNK = 256


def ffn_kernel(plan, tab, h0, h1, h2, h3, c0, c1, c2, c3, vv_ref, *rest):
    count = len(rest) - 16
    parts = rest[:count]
    act_ref, dhid_ref, ykeep, ysend, go_ref, g1, g2, g3 = rest[count : count + 8]
    u_ref, d_ref, hall, call_ref, bias_ref, yacc, gacc, sems = rest[count + 8 :]
    me, b = tab[0], tab[3]
    copies = []
    for u_place, d_place, bit in plan:
        rows = rows_at(jnp.bitwise_xor(me, bit), OWN)
        for (index, slot), target in ((u_place, u_ref), (d_place, d_ref)):
            copy = pltpu.make_async_copy(
                parts[index].at[slot], target.at[rows, :], sems.at[len(copies)]
            )
            copy.start()
            copies.append(copy)
    for i, (h_ref, c_ref) in enumerate(((h0, c0), (h1, c1), (h2, c2), (h3, c3))):
        rows = slice(i * ROWS, (i + 1) * ROWS)
        hall[rows, :] = h_ref[...]
        call_ref[rows, :] = c_ref[...]
    for k in range(2):
        bias_ref[:, k * 384 : (k + 1) * 384] = vv_ref[2 * b + k].astype(F32)[1:2, 192:576]
    yacc[...] = jnp.zeros_like(yacc)
    gacc[...] = jnp.zeros_like(gacc)
    for copy in copies:
        copy.wait()

    def step(k, carry):
        cols = pl.ds(pl.multiple_of(k * CHUNK, CHUNK), CHUNK)
        hid = nn(hall[...], u_ref[:, cols]) + bias_ref[:, cols]
        dact = nn(call_ref[...], d_ref[:, cols])
        cdf = 0.5 * (1.0 + lax.erf(hid * 0.7071067811865476))
        act = (hid * cdf).astype(BF16)
        pdf = jnp.exp(-0.5 * hid * hid) * 0.3989422804014327
        dhid = (dact * (cdf + hid * pdf)).astype(BF16)
        act_ref[:, cols] = act
        dhid_ref[:, cols] = dhid
        yacc[...] += nt(act, d_ref[:, cols])
        gacc[...] += nt(dhid, u_ref[:, cols])
        return carry

    lax.fori_loop(0, QUART // CHUNK, step, 0)
    for i, y_ref in enumerate((ykeep, ysend, ykeep, ysend)):
        y_ref[i // 2] = yacc[i * ROWS : (i + 1) * ROWS, :].astype(y_ref.dtype)
    for i, g_ref in enumerate((go_ref, g1, g2, g3)):
        g_ref[...] = gacc[i * ROWS : (i + 1) * ROWS, :].astype(g_ref.dtype)


def ffn_grad_kernel(tab, *refs):
    me = tab[0]
    h_refs, c_refs = refs[:4], refs[4:8]
    dhid_ref, act_ref, usend, ukeep, dthere, dhere, left, left2 = refs[8:]
    for i in range(BLK):
        left[:, i * ROWS : (i + 1) * ROWS] = h_refs[i][...].T
        left2[:, i * ROWS : (i + 1) * ROWS] = c_refs[i][...].T
    for source, right_ref, ref, bits in (
        (left, dhid_ref, usend, (4, 5, 6, 7)),
        (left, dhid_ref, ukeep, (0, 1, 2, 3)),
        (left2, act_ref, dthere, (2, 6, 3, 7)),
        (left2, act_ref, dhere, (0, 4, 1, 5)),
    ):
        for s, bit in enumerate(bits):
            o = jnp.bitwise_xor(me, bit)
            ref[s] = nn(source[rows_at(o, OWN), :], right_ref[...]).astype(BF16)


def back_mix_kernel(
    tab, resid_ref, cot_ref, go_ref, g1, g2, g3, ow_ref, vv_ref, dres_ref, dmix_ref, d0, d1, d2, d3, vs_ref
):
    z = tab[1]
    grad = go_ref[...] + g1[...].astype(F32) + g2[...].astype(F32) + g3[...].astype(F32)
    n, r = norm_stats(resid_ref[...])
    dn = grad * vec(vv_ref, 0, 5 * OWN)
    dres = cot_ref[...] + r * (
        dn
        - jnp.mean(dn, axis=-1, keepdims=True)
        - n * jnp.mean(dn * n, axis=-1, keepdims=True)
    )
    dres_ref[...] = dres
    dmix = dres.astype(BF16)
    dmix_ref[...] = dmix
    for j, ref in enumerate((d0, d1, d2, d3)):
        ref[...] = nt(dmix, ow_ref[rows_at(jnp.bitwise_xor(z, j), HW), :]).astype(BF16)
    vs_ref[0:1, :] = jnp.sum(dmix.astype(F32), axis=0, keepdims=True)
    vs_ref[1:2, :] = jnp.sum(grad * n, axis=0, keepdims=True)
    vs_ref[2:3, :] = jnp.sum(grad, axis=0, keepdims=True)
    vs_ref[3:8, :] = jnp.zeros((5, WIDTH), F32)


def out_grad_kernel(tab, a0, a1, a2, a3, dmix_ref, vs_ref, dhid_ref, c_ref, keep, send, left, vrow):
    me, z, b = tab[0], tab[1], tab[3]
    for j, ref in enumerate((a0, a1, a2, a3)):
        left[rows_at(jnp.bitwise_xor(z, j), HW), :] = ref[...].astype(F32).T.astype(BF16)
    vs = vs_ref[...]
    usum = jnp.sum(dhid_ref[...].astype(F32), axis=0, keepdims=True)
    csum = jnp.sum(c_ref[...].astype(F32), axis=0, keepdims=True)
    for o in range(OWNERS):
        part = usum[:, (o % 2) * 384 : (o % 2 + 1) * 384]
        row = jnp.concatenate(
            [vs[k : k + 1, o * OWN : (o + 1) * OWN] for k in range(3)]
            + [jnp.where(b == o // 2, part, 0.0), csum[:, o * OWN : (o + 1) * OWN]],
            axis=1,
        )
        vrow[o] = jnp.broadcast_to(row, (16, WIDTH)).astype(BF16)
    for ref, base in ((send, 1), (keep, 0)):
        for s in range(4):
            o = jnp.bitwise_xor(me, base + (s // 2) * 2 + (s % 2) * 4)
            ref[s, :OWN, :] = nn(left[rows_at(o, OWN), :], dmix_ref[...]).astype(BF16)
            ref[s, OWN:, :] = vrow[o]


def back_attend_kernel(
    tab,
    q_ref,
    k0,
    k1,
    k2,
    k3,
    g0,
    g1,
    g2,
    g3,
    all_ref,
    lse_ref,
    qr_ref,
    kcol_ref,
    dq_ref,
    keep,
    send,
    acc,
    gall,
):
    kvs = (k0, k1, k2, k3)
    acc[...] = jnp.zeros_like(acc)
    for i, g_ref in enumerate((g0, g1, g2, g3)):
        gall[i * ROWS : (i + 1) * ROWS, :] = g_ref[...]
    lane = lax.broadcasted_iota(jnp.int32, (BACK_STEP, 128), 1)

    def step(i, carry):
        rows = rows_at(i, BACK_STEP)
        prod = gall[rows, :].astype(F32) * all_ref[rows, :].astype(F32)
        stat = jnp.zeros((BACK_STEP, 128), F32)
        for h in range(LOCAL_HEADS):
            stat = jnp.where(
                lane == h, jnp.sum(prod[:, head_cols(h)], axis=1, keepdims=True), stat
            )
        rowdot = stat.T
        lse = lse_ref[rows, :].T
        code1 = qr_ref[0:1, rows]
        code2 = qr_ref[1:2, rows]
        dq = [jnp.zeros((BACK_STEP, 128), F32) for _ in range(LOCAL_HEADS)]
        for j in range(BLK):
            kc = kcol_ref[j * GROUP : (j + 1) * GROUP, :]
            mask = (kc == code1) | (kc == code2)
            for h in range(LOCAL_HEADS):
                kwin, kup = window(h)
                vwin, vup = window(LOCAL_HEADS + h)
                qp = placed(q_ref[rows, head_cols(h)], kup)
                gp = placed(gall[rows, head_cols(h)], vup)
                kk = kvs[j][:, kwin]
                scores = nt(kk, qp)
                p = jnp.where(mask, jnp.exp(scores - lse[h : h + 1, :]), 0.0)
                dp = nt(kvs[j][:, vwin], gp)
                ds = (p * (dp - rowdot[h : h + 1, :])).astype(BF16)
                acc[j, :, vwin] += nn(p.astype(BF16), gp)
                acc[j, :, kwin] += nn(ds, qp)
                dq[h] = dq[h] + tn(ds, kk)
        parts = []
        for h in range(LOCAL_HEADS):
            _, kup = window(h)
            parts.append(dq[h][:, 64:] if kup else dq[h][:, :64])
        dq_ref[rows, :] = (jnp.concatenate(parts, axis=1) * HEAD_DIM ** (-0.5)).astype(BF16)
        return carry

    lax.fori_loop(0, GROUP // BACK_STEP, step, 0)
    keep[0] = acc[0].astype(BF16)
    keep[1] = acc[2].astype(BF16)
    send[0] = acc[1].astype(BF16)
    send[1] = acc[3].astype(BF16)


def back_proj_kernel(
    tab, dq_ref, keep, got, recv, w_ref, n0, n1, n2, n3, dproj_ref, h0, h1, send, vs_ref
):
    dproj_ref[:, :HW] = dq_ref[...]
    total = keep[0].astype(F32) + got[0].astype(F32) + recv[...].astype(F32)
    dproj_ref[:, HW:] = total.astype(BF16)
    gain = jnp.zeros((1, WIDTH), F32)
    shift = jnp.zeros((1, WIDTH), F32)
    outs = (h0, h1, send.at[0], send.at[1])
    for i, (n_ref, out) in enumerate(zip((n0, n1, n2, n3), outs)):
        rows = slice(i * ROWS, (i + 1) * ROWS)
        grad = nt(dproj_ref[rows, :], w_ref[...])
        out[...] = grad.astype(out.dtype)
        gain = gain + jnp.sum(grad * n_ref[...].astype(F32), axis=0, keepdims=True)
        shift = shift + jnp.sum(grad, axis=0, keepdims=True)
    vs_ref[0:1, :] = gain
    vs_ref[1:2, :] = shift
    cols = jnp.sum(dproj_ref[...].astype(F32), axis=0, keepdims=True)
    vs_ref[2:3, :] = jnp.concatenate([cols, jnp.zeros((1, WIDTH - 3 * HW), F32)], axis=1)
    vs_ref[3:8, :] = jnp.zeros((5, WIDTH), F32)


def qkv_grad_kernel(tab, h_ref, dproj_ref, vs_ref, keep, send, left, vrow):
    me, z = tab[0], tab[1]
    vs = vs_ref[...]
    for o in range(OWNERS):
        row = [vs[k : k + 1, o * OWN : (o + 1) * OWN] for k in range(2)]
        for lane in (0, 2 * HW):
            lane = lane + (o % 2) * OWN
            row.append(jnp.where(z == o // 2, vs[2:3, lane : lane + OWN], 0.0))
        row.append(jnp.zeros((1, 3 * HW - 4 * OWN), F32))
        vrow[o] = jnp.broadcast_to(jnp.concatenate(row, axis=1), (16, 3 * HW)).astype(BF16)
    for i in range(ULY):
        rows = slice(i * ROWS, (i + 1) * ROWS)
        left[:, rows] = h_ref[rows, :].T
    for ref, base in ((keep, 0), (send, 1)):
        for s in range(4):
            o = jnp.bitwise_xor(me, base + (s // 2) * 2 + (s % 2) * 4)
            ref[s, :OWN, :] = nn(left[rows_at(o, OWN), :], dproj_ref[...]).astype(BF16)
            ref[s, OWN:, :] = vrow[o]


def back_norm_kernel(tab, x_ref, dres_ref, h0, got2, got1, vv_ref, out_ref):
    grad = h0[...] + got2[0].astype(F32) + got1[...].astype(F32)
    n, r = norm_stats(x_ref[...])
    dn = grad * vec(vv_ref, 0, 0)
    out_ref[...] = dres_ref[...] + r * (
        dn
        - jnp.mean(dn, axis=-1, keepdims=True)
        - n * jnp.mean(dn * n, axis=-1, keepdims=True)
    )


def output_kernel(tab, resid_ref, keep, got, last, vv_ref, out_ref):
    out_ref[...] = (
        resid_ref[...]
        + keep[0]
        + got[0].astype(F32)
        + last[...].astype(F32)
        + vec(vv_ref, 1, OWN)
    )


def low_sum(a, b):
    return (a.astype(F32) + b.astype(F32)).astype(BF16)


def split_kernel(bit, tab, a_ref, ac_ref, by_ref, byc_ref, keep, send):
    for value, low_out, high_out in ((0, keep, send), (1, send, keep)):

        @pl.when(tab[bit] == value)
        def _():
            low_out[0] = a_ref[0]
            low_out[1] = ac_ref[1]
            high_out[0] = by_ref[0]
            high_out[1] = byc_ref[1]


def pack_kernel(tab, a_ref, ac_ref, by_ref, byc_ref, out_ref):
    for s, (ref, place) in enumerate(((a_ref, 1), (ac_ref, 3), (by_ref, 1), (byc_ref, 3))):
        out_ref[s] = ref[place]


def split_add_kernel(bit, tab, a_ref, ac_ref, by_ref, byc_ref, got, keep, send):
    refs = ((a_ref, 0), (ac_ref, 2), (by_ref, 0), (byc_ref, 2))
    for value, low_out, high_out in ((0, keep, send), (1, send, keep)):

        @pl.when(tab[bit] == value)
        def _():
            for s, (ref, place) in enumerate(refs):
                (low_out, high_out)[s // 2][s % 2] = low_sum(ref[place], got[s])


def merge_kernel(bit, tab, a_ref, b_ref, keep, send):
    for value, low_out, high_out in ((0, keep, send), (1, send, keep)):

        @pl.when(tab[bit] == value)
        def _():
            low_out[...] = low_sum(a_ref[0], b_ref[0])
            high_out[...] = low_sum(a_ref[1], b_ref[1])


def final_kernel(tab, pair, got, out_ref):
    b, odd, high = tab[3], tab[4], tab[5]
    for flip, ref in ((0, pair.at[0]), (1, pair.at[1]), (2, got.at[0]), (3, got.at[1])):
        q = jnp.bitwise_xor(jnp.bitwise_xor(b, 2 * odd + high), flip)
        out_ref[:, quarter(q)] = ref[...].astype(F32)


def qkv_final_kernel(tab, pair, got, out_ref, vec_ref):
    z = tab[1]
    refs = (pair.at[0], pair.at[1], got.at[0], got.at[1])
    for k in range(ULY):

        @pl.when(z == k)
        def _():
            for p in range(3):
                cols = [
                    refs[t ^ k][:OWN, p * HW : (p + 1) * HW].astype(F32) for t in range(ULY)
                ]
                out_ref[:, p * WIDTH : (p + 1) * WIDTH] = jnp.concatenate(cols, axis=1)

    total = jnp.zeros((16, 3 * HW), F32)
    for ref in refs:
        total = total + ref[OWN:, :].astype(F32)
    vec_ref[...] = total[:8, :]


def add_low(a, b):
    return (a.astype(F32) + b.astype(F32)).astype(BF16)


def xor_order(array, axis, index):
    shape = array.shape
    two = array.reshape(shape[:axis] + (2, 2) + shape[axis + 1 :])
    two = jnp.where((index & 1) == 1, jnp.flip(two, axis + 1), two)
    two = jnp.where((index & 2) == 2, jnp.flip(two, axis), two)
    return two.reshape(shape)


def body(
    inputs,
    cotangent,
    qkv_weight,
    query_bias,
    value_bias,
    out_weight,
    out_bias,
    norm1_gain,
    norm1_bias,
    norm2_gain,
    norm2_bias,
    up_weight,
    up_bias,
    down_weight,
    down_bias,
    doc_lengths,
    pad_mask,
):
    dp_count = lax.axis_size("dp")
    near = dp_count == 2
    dp = lax.axis_index("dp")
    z = lax.axis_index("uly")
    b = lax.axis_index("blk")
    core = b & 1
    rank = dp * BLK + b
    me = rank if near else jnp.int32(0)
    tab = jnp.stack([me, z, core, b, z & 1, z >> 1]).astype(jnp.int32)
    own_rows = WIDTH // (dp_count * BLK)
    axes = ("dp", "blk")

    x = inputs.reshape(ROWS, WIDTH)
    cot = cotangent.reshape(ROWS, WIDTH)

    if near:
        vectors = [norm1_gain, norm1_bias, query_bias, value_bias, out_bias, norm2_gain]
        vectors += [norm2_bias, down_bias, up_bias]
        n0, panel = call(
            prep_kernel,
            [sds((ROWS, WIDTH), BF16), sds((PANEL, 3 * HW), BF16)],
            [tab, x, qkv_weight, *vectors],
        )
        n1, n2, n3 = (swap(n0, "uly", k) for k in (1, 2, 3))
        a_0 = jnp.stack([panel, swap(panel, "dp", 1)])
        a_2 = swap(a_0, "blk", 2)
        four_bits = [[0, 4], [2, 6], [1, 5], [3, 7]]
        w_mine = call(
            ffn_prep_kernel,
            [sds((2, OWN, QUART), BF16)] * BLK,
            [tab, up_weight, down_weight.T],
        )
        n1 = after(n1, w_mine[0])
        a_2c = swap(a_2, "blk", 1)
        a_0c = swap(after(a_0, a_2c), "blk", 1)
        a_parts = [a_0, a_2, a_0c, a_2c]
        w_parts = [w_mine[0], None, cross(after(w_mine[2], a_0c), 2)] + [None] * 5
        w_plan = [((i, 0), (i, 1), i) for i in range(OWNERS)]
        o_plan = [
            (i, k, bit) for i, bits in enumerate(four_bits) for k, bit in enumerate(bits)
        ]
    else:
        (n0,) = call(norm_kernel, [sds((ROWS, WIDTH), BF16)], [tab, x])
        n1, n2, n3 = (swap(n0, "uly", k) for k in (1, 2, 3))
        qkv_cols = lax.dynamic_index_in_dim(
            qkv_weight.reshape(own_rows, 3, ULY, HW), z, axis=2, keepdims=False
        ).reshape(own_rows, 3 * HW)

        def full(array):
            return lax.all_gather(array, axes, axis=0, tiled=True)

        def eight(vector):
            return full(vector).reshape(OWNERS, 1, -1)

        def mine(array):
            cols = full(array).reshape(WIDTH, BLK, QUART)
            return lax.dynamic_index_in_dim(cols, b, 1, False).reshape(OWNERS, OWN, QUART)

        row0 = jnp.concatenate(
            [
                eight(v)
                for v in (norm1_gain, norm1_bias, query_bias, value_bias, out_bias, norm2_gain)
            ],
            axis=2,
        )
        row1 = jnp.concatenate([eight(v) for v in (norm2_bias, down_bias, up_bias)], axis=2)
        a_parts = [
            jnp.concatenate(
                [
                    full(qkv_cols).reshape(OWNERS, OWN, 3 * HW),
                    row0,
                    row1,
                    jnp.zeros((OWNERS, 14, 3 * HW), BF16),
                ],
                axis=1,
            )
        ]
        four_bits = [list(range(OWNERS))]
        o_parts = [full(out_weight).reshape(OWNERS, OWN, WIDTH)]
        w_parts = [mine(up_weight), mine(down_weight.T)]
        w_plan = [((0, o), (1, o), o) for o in range(OWNERS)]
        o_plan = [(0, o, o) for o in range(OWNERS)]

    ends = jnp.cumsum(doc_lengths.reshape(-1), dtype=jnp.int32)
    zs = jnp.arange(ULY, dtype=jnp.int32) ^ z
    bs = jnp.arange(BLK, dtype=jnp.int32) ^ b
    within = jnp.arange(ROWS, dtype=jnp.int32)
    kplace = ((zs[None, :, None] * BLK + bs[:, None, None]) * ROWS + within).reshape(KEYS)
    kseg = jnp.sum((kplace[:, None] >= ends[None, :]).astype(jnp.int32), axis=1)
    valid = pad_mask.reshape(ULY, BLK, ROWS)
    valid = xor_order(xor_order(valid, 0, z), 1, b).transpose(1, 0, 2).reshape(KEYS)
    kcode = jnp.where(valid > 0, kseg, kplace + 64)
    qcodes = jnp.stack([kseg[:GROUP], kplace[:GROUP] + 64])

    n1, q_cols, k_rows = lax.optimization_barrier((n1, qcodes.T, kcode[None, :]))
    q, kv, h1, w_qkv, vv = call(
        functools.partial(qkv_kernel, four_bits),
        [
            sds((GROUP, HW), BF16),
            sds((GROUP, 2 * HW), BF16),
            sds((GROUP, WIDTH), BF16),
            sds((WIDTH, 3 * HW), BF16),
            sds((OWNERS, 16, 3 * HW), BF16),
        ],
        [tab, n0, n1, n2, n3, *a_parts],
        flops=2 * GROUP * WIDTH * 3 * HW,
    )
    q_rows, late = lax.optimization_barrier((qcodes, kcode, kv))[:2]
    k_cols = late[:, None]
    cb = cot.astype(BF16)
    if near:
        kv_y = swap(after(kv, w_parts[2]), "blk", 2)
        cb_y = swap(after(cb, kv_y), "blk", 2)
        w_parts[4] = cross(after(w_mine[0], kv), 4)
        w_parts[5] = cross(after(w_mine[1], kv), 5)
        o_0 = jnp.stack([out_weight, swap(after(out_weight, kv), "dp", 1)])
        o_0c = swap(o_0, "blk", 1)
        o_2 = swap(after(o_0, kv_y), "blk", 2)
    else:
        kv_y = swap(kv, "blk", 2)
    kv_c = swap(kv, "blk", 1)
    kv_yc = swap(kv_y, "blk", 1)
    if near:
        cb_c = swap(after(cb, kv), "blk", 1)
        w_parts[1] = cross(after(w_mine[1], kv), 1)
        kv_yc = after(kv_yc, o_0c, w_parts[1], cb_c)
    kvs = [kv, kv_c, kv_y, kv_yc]

    def around(array):
        near_y = swap(array, "blk", 2)
        return [array, swap(array, "blk", 1), near_y, swap(near_y, "blk", 1)]

    if near:
        w_parts[3] = cross(after(w_mine[3], kv_y), 3)
    else:
        cbs = around(cb)

    *attn_slots, attn_all, lse = call(
        attend_kernel,
        [sds((ROWS, HW), BF16)] * ULY + [sds((GROUP, HW), BF16), sds((GROUP, 128), F32)],
        [tab, q, *kvs, q_cols, k_rows],
        flops=4 * GROUP * KEYS * HW,
    )
    if near:
        attn_slots = after(attn_slots, w_parts[4], w_parts[5], o_2)
        o_2c = swap(after(o_2, attn_slots[0]), "blk", 1)
        o_parts = [o_0, o_2, o_0c, o_2c]
    attn = [attn_slots[0]] + [swap(attn_slots[k], "uly", k) for k in (1, 2, 3)]
    resid, h2, ow = call(
        functools.partial(mix_kernel, o_plan),
        [sds((ROWS, WIDTH), F32), sds((ROWS, WIDTH), BF16), sds((WIDTH, WIDTH), BF16)],
        [tab, *attn, x, vv, *o_parts],
        scratch=[pltpu.SemaphoreType.DMA((OWNERS,))],
        flops=2 * ROWS * WIDTH * WIDTH,
        in_any=range(7, 7 + len(o_parts)),
    )

    if near:
        w_parts[6] = cross(after(w_mine[2], attn[1]), 6)
        w_parts[7] = cross(after(w_mine[3], attn[2], cb_y, w_parts[3]), 7)
        h2 = after(h2, w_parts[6], w_parts[7])
        cbs = [cb, cb_c, cb_y, swap(after(cb_y, h2), "blk", 1)]
    h2s = around(h2)
    parts = len(w_parts)
    act, dhid, y_keep, y_send, go, *gs = call(
        functools.partial(ffn_kernel, w_plan),
        [sds((GROUP, QUART), BF16)] * 2
        + [sds((2, ROWS, WIDTH), F32), sds((2, ROWS, WIDTH), BF16), sds((ROWS, WIDTH), F32)]
        + [sds((ROWS, WIDTH), BF16)] * 3,
        [tab, *h2s, *cbs, vv, *w_parts],
        scratch=[
            pltpu.VMEM((WIDTH, QUART), BF16),
            pltpu.VMEM((WIDTH, QUART), BF16),
            pltpu.VMEM((GROUP, WIDTH), BF16),
            pltpu.VMEM((GROUP, WIDTH), BF16),
            pltpu.VMEM((1, QUART), F32),
            pltpu.VMEM((GROUP, WIDTH), F32),
            pltpu.VMEM((GROUP, WIDTH), F32),
            pltpu.SemaphoreType.DMA((2 * OWNERS,)),
        ],
        flops=8 * GROUP * WIDTH * QUART,
        in_any=range(10, 10 + parts),
    )
    gs = [swap(g, "blk", k) for k, g in enumerate(gs, 1)]

    y_got = swap(y_send, "blk", 1)
    y_part = (y_keep[1] + y_got[1].astype(F32)).astype(BF16)
    usend, ukeep, dthere, dhere = call(
        ffn_grad_kernel,
        [sds((BLK, OWN, QUART), BF16)] * 4,
        [tab, *h2s, *cbs, dhid, act],
        scratch=[pltpu.VMEM((WIDTH, GROUP), BF16)] * 2,
    )
    go = after(go, usend, dthere, y_part)

    dres, dmix, *dattn_slots, vs2 = call(
        back_mix_kernel,
        [sds((ROWS, WIDTH), F32), sds((ROWS, WIDTH), BF16)]
        + [sds((ROWS, HW), BF16)] * ULY
        + [sds((8, WIDTH), F32)],
        [tab, resid, cot, go, *gs, ow, vv],
        flops=2 * ROWS * WIDTH * WIDTH,
    )
    pair = sds((2, OWN, QUART), BF16)
    one = sds((OWN, QUART), BF16)
    dattn = [dattn_slots[0]] + [swap(dattn_slots[k], "uly", k) for k in (1, 2, 3)]
    if near:
        u_got = swap(usend, "dp", 1)
        d_there = swap(after(dthere, dmix), "blk", 2)
    y_last = swap(after(y_part, dattn[1]), "blk", 2)

    dq, keep_kv, send_kv = call(
        back_attend_kernel,
        [sds((GROUP, HW), BF16), sds((2, GROUP, 2 * HW), BF16), sds((2, GROUP, 2 * HW), BF16)],
        [tab, q, *kvs, *dattn, attn_all, lse, q_rows, k_cols],
        scratch=[pltpu.VMEM((BLK, GROUP, 2 * HW), F32), pltpu.VMEM((GROUP, HW), BF16)],
        flops=10 * GROUP * KEYS * HW,
    )
    if near:
        send_kv = after(send_kv, d_there, y_last)
    got = swap(send_kv, "blk", 1)
    kv_send = add_low(keep_kv[1], got[1])
    kv_got = swap(kv_send, "blk", 2)
    okeep, osend = call(
        out_grad_kernel,
        [sds((4, PANEL, WIDTH), BF16)] * 2,
        [tab, *attn, after(dmix, kv_send), vs2, dhid, cb],
        scratch=[pltpu.VMEM((WIDTH, ROWS), BF16), pltpu.VMEM((OWNERS, 16, WIDTH), BF16)],
    )

    if near:
        dhere, d_there = after(dhere, kv_send), after(d_there, kv_send)
        pieces = [dhere, swap(dhere, "blk", 1), d_there, swap(d_there, "blk", 1)]
        (d_send,) = call(pack_kernel, [sds((BLK, OWN, QUART), BF16)], [tab, *pieces])
        dq = after(dq, d_send, okeep)
    dproj, g_own, g_one, g_send, vs1 = call(
        back_proj_kernel,
        [sds((GROUP, 3 * HW), BF16)]
        + [sds((ROWS, WIDTH), F32)] * 2
        + [sds((2, ROWS, WIDTH), BF16), sds((8, WIDTH), F32)],
        [tab, dq, keep_kv, got, kv_got, w_qkv, n0, n1, n2, n3],
        flops=2 * GROUP * WIDTH * 3 * HW,
    )
    qkeep, qsend = call(
        qkv_grad_kernel,
        [sds((4, PANEL, 3 * HW), BF16)] * 2,
        [tab, h1, dproj, vs1],
        scratch=[pltpu.VMEM((WIDTH, GROUP), BF16), pltpu.VMEM((OWNERS, 16, 3 * HW), BF16)],
    )
    (output,) = call(
        output_kernel,
        [sds((ROWS, WIDTH), F32)],
        [tab, after(resid, dproj), y_keep, y_got, y_last, vv],
    )
    if near:
        o1 = add_low(okeep, swap(after(osend, dproj), "blk", 1))
        u_got = after(u_got, dproj)
        u_there = add_low(ukeep[2:], u_got[2:])
        u_here = add_low(ukeep[:2], u_got[:2])
        q1 = add_low(qkeep, swap(qsend, "blk", 1))
        u_there = swap(u_there, "blk", 2)
        upieces = [u_here, swap(u_here, "blk", 1), u_there, swap(u_there, "blk", 1)]
        ukept, usent = call(functools.partial(split_kernel, 4), [pair] * 2, [tab, *upieces])
        dkept, dsent = call(
            functools.partial(split_add_kernel, 4),
            [pair] * 2,
            [tab, *pieces, after(swap(d_send, "dp", 1), dproj)],
        )
        gates = [q1, dsent, usent]
    else:
        gates = []
    g_got = after(swap(g_send, "uly", 2), *gates)
    g_last = swap((g_one + g_got[1].astype(F32)).astype(BF16), "uly", 1)
    if near:

        def over_uly(kept, sent):
            return call(
                functools.partial(merge_kernel, 5),
                [one] * 2,
                [tab, kept, after(swap(sent, "uly", 1), g_got)],
            )

        def share(total):
            pair = jnp.stack([total, swap(total, "uly", 2)])
            return call(
                final_kernel, [sds((OWN, FF), F32)], [tab, pair, swap(pair, "uly", 1)]
            )[0]

        dkept, dsent = over_uly(dkept, dsent)
        ukept, usent = over_uly(ukept, usent)
        d_total = add_low(dkept, swap(dsent, "uly", 2))
        u_mid = swap(usent, "uly", 2)
        g_last = after(g_last, d_total, usent, output)

        o2 = add_low(o1[:2], swap(o1[2:], "blk", 2))
        o3 = add_low(o2[0], swap(o2[1], "dp", 1))
        u_total = add_low(after(ukept, o3), u_mid)
        grad_down = share(d_total).T
        grad_up = share(u_total)
        o4 = add_low(o3, swap(after(o3, d_total), "uly", 1))
        o5 = o4.astype(F32) + swap(o4, "uly", 2).astype(F32)
        grad_ow = o5[:OWN]
        grad_obias, grad_gain2, grad_shift2 = (o5[OWN, k * OWN : (k + 1) * OWN] for k in range(3))
        grad_ubias, grad_dbias = o5[OWN, 288:672], o5[OWN, 672:768]

        q2 = add_low(q1[:2], swap(q1[2:], "blk", 2))
        q3 = add_low(q2[0], swap(q2[1], "dp", 1))
        q_pair = jnp.stack([q3, swap(q3, "uly", 1)])
        grad_qkv, qvec = call(
            qkv_final_kernel,
            [sds((OWN, 3 * WIDTH), F32), sds((8, 3 * HW), F32)],
            [tab, q_pair, swap(after(q_pair, u_total), "uly", 2)],
        )
        grad_gain1, grad_shift1, grad_qbias, grad_vbias = (
            qvec[0, k * OWN : (k + 1) * OWN] for k in range(4)
        )
    else:

        def owned(array):
            shard = lax.psum_scatter(
                array.astype(F32), axes, scatter_dimension=0, tiled=True
            )
            return lax.psum(shard.astype(BF16), "uly").astype(F32)

        def by_owner(keep, send, order):
            both = jnp.concatenate([keep, send], axis=0)
            return both[jnp.array(order)]

        o8 = by_owner(okeep, osend, [0, 4, 2, 6, 1, 5, 3, 7])
        q8 = by_owner(qkeep, qsend, [0, 4, 2, 6, 1, 5, 3, 7])

        def widen(keep, send, order):
            flat = jnp.concatenate([keep, send], axis=0)[jnp.array(order)]
            flat = flat.reshape(WIDTH, 1, QUART)
            place = (jnp.arange(BLK) == b)[None, :, None]
            return jnp.where(place, flat, jnp.zeros_like(flat)).reshape(WIDTH, FF)

        grad_up = owned(widen(ukeep, usend, range(OWNERS)))
        grad_down = owned(widen(dhere, dthere, [0, 2, 4, 6, 1, 3, 5, 7])).T
        grad_ubias = owned(o8[:, OWN, 288:672].reshape(FF))
        grad_dbias = owned(o8[:, OWN, 672:768].reshape(WIDTH))
        grad_ow = owned(o8[:, :OWN].reshape(WIDTH, WIDTH))
        grad_obias, grad_gain2, grad_shift2 = (
            owned(o8[:, OWN, k * OWN : (k + 1) * OWN].reshape(WIDTH)) for k in range(3)
        )
        mine = q8[:, :OWN].reshape(WIDTH, 3, 1, HW)
        spread = jnp.where(
            (jnp.arange(ULY) == z)[None, None, :, None], mine, jnp.zeros_like(mine)
        )
        grad_qkv = owned(spread.reshape(WIDTH, 3 * WIDTH))
        grad_gain1, grad_shift1, grad_qbias, grad_vbias = (
            owned(q8[:, OWN, k * OWN : (k + 1) * OWN].reshape(WIDTH)) for k in range(4)
        )

    (grad_inputs,) = call(
        back_norm_kernel, [sds((ROWS, WIDTH), F32)], [tab, x, dres, g_own, g_got, g_last, vv]
    )
    return (
        output.reshape(inputs.shape),
        grad_inputs.reshape(inputs.shape),
        grad_qkv,
        grad_qbias,
        grad_vbias,
        grad_ow,
        grad_obias,
        grad_gain1,
        grad_shift1,
        grad_gain2,
        grad_shift2,
        grad_up,
        grad_ubias,
        grad_down,
        grad_dbias,
    )


def solution(mesh):
    rows = P(None, ("dp", "uly", "blk"), None)
    first = P(("dp", "blk"), None)
    flat = P(("dp", "blk"))
    second = P(None, ("dp", "blk"))
    return jax.shard_map(
        body,
        mesh=mesh,
        in_specs=(
            rows,
            rows,
            first,
            flat,
            flat,
            first,
            flat,
            flat,
            flat,
            flat,
            flat,
            first,
            flat,
            second,
            flat,
            P(None, "dp", None),
            P(None, "dp"),
        ),
        out_specs=(
            rows,
            rows,
            first,
            flat,
            flat,
            first,
            flat,
            flat,
            flat,
            flat,
            flat,
            first,
            flat,
            second,
            flat,
        ),
        check_vma=False,
    )
```

```python
import functools

import jax
import jax.numpy as jnp
from jax import lax
from jax.experimental import pallas as pl
from jax.experimental.pallas import tpu as pltpu
from jax.sharding import PartitionSpec as P

HEADS = 12
HEAD_DIM = 64
FF = 3072
F32 = jnp.float32
BF16 = jnp.bfloat16
NEG = -1e30
VMEM_LIMIT = 60 * 1024 * 1024

ROWS = 128
ULY = 4
BLK = 4
GROUP = ROWS * ULY
KEYS = GROUP * BLK
WIDTH = HEADS * HEAD_DIM
HW = WIDTH // ULY
LOCAL_HEADS = HEADS // ULY
OWNERS = 8
OWN = WIDTH // OWNERS
PANEL = OWN + 16
QUART = FF // BLK
STEP = 512
BACK_STEP = 512


def swap(array, axis, by):
    peers = lax.axis_size(axis)
    return lax.ppermute(array, axis, [(i, i ^ by) for i in range(peers)])


def cross(array, by):
    peers = lax.axis_size("dp") * lax.axis_size("blk")
    return lax.ppermute(array, ("dp", "blk"), [(i, i ^ by) for i in range(peers)])


def after(array, *others):
    return lax.optimization_barrier((array, *others))[0]


def vm():
    return pl.BlockSpec(memory_space=pltpu.VMEM)


def anyspace():
    return pl.BlockSpec(memory_space=pl.ANY)


def smem():
    return pl.BlockSpec(memory_space=pltpu.SMEM)


def call(kernel, outs, args, scratch=(), flops=0, in_any=()):
    specs = [smem()] + [anyspace() if i in in_any else vm() for i in range(1, len(args))]
    nbytes = sum(a.size * a.dtype.itemsize for a in args) + sum(
        o.size * o.dtype.itemsize for o in outs
    )
    nbytes = nbytes if flops else 1
    return pl.pallas_call(
        kernel,
        name=getattr(kernel, "func", kernel).__name__,
        out_shape=outs,
        in_specs=specs,
        out_specs=[vm() for _ in outs],
        scratch_shapes=list(scratch),
        cost_estimate=pl.CostEstimate(
            flops=flops, bytes_accessed=nbytes, transcendentals=0
        ),
        compiler_params=pltpu.CompilerParams(vmem_limit_bytes=VMEM_LIMIT),
    )(*args)


def sds(shape, dtype):
    return jax.ShapeDtypeStruct(shape, dtype)


def nn(a, b):
    return lax.dot_general(a, b, (((1,), (0,)), ((), ())), preferred_element_type=F32)


def nt(a, b):
    return lax.dot_general(a, b, (((1,), (1,)), ((), ())), preferred_element_type=F32)


def tn(a, b):
    return lax.dot_general(a, b, (((0,), (0,)), ((), ())), preferred_element_type=F32)


def rows_at(index, size):
    return pl.ds(pl.multiple_of(index * size, 32), size)


def vec(vv_ref, row, lane):
    return jnp.concatenate(
        [vv_ref[o].astype(F32)[row : row + 1, lane : lane + OWN] for o in range(OWNERS)], axis=1
    )


def norm_stats(v):
    mean = jnp.mean(v, axis=-1, keepdims=True)
    cen = v - mean
    var = jnp.mean(cen * cen, axis=-1, keepdims=True)
    r = lax.rsqrt(var + 1e-12)
    return cen * r, r


def norm_kernel(tab, x_ref, n_ref):
    n_ref[...] = norm_stats(x_ref[...])[0].astype(BF16)


def prep_kernel(tab, x_ref, w_ref, *rest):
    vectors, (n_ref, panel_ref) = rest[:9], rest[9:]
    z = tab[1]
    rows = [v[...].astype(F32).reshape(1, v.shape[0]) for v in vectors]
    panel_ref[OWN:, :] = jnp.concatenate(
        [
            jnp.concatenate(rows[:6], axis=1),
            jnp.concatenate(rows[6:], axis=1),
            jnp.zeros((14, 3 * HW), F32),
        ],
        axis=0,
    ).astype(BF16)
    for k in range(ULY):

        @pl.when(z == k)
        def _():
            parts = [w_ref[:, p * WIDTH + k * HW : p * WIDTH + (k + 1) * HW] for p in range(3)]
            panel_ref[:OWN, :] = jnp.concatenate(parts, axis=1)

    n_ref[...] = norm_stats(x_ref[...])[0].astype(BF16)


def quarter(index):
    return pl.ds(pl.multiple_of(index * QUART, 128), QUART)


def ffn_prep_kernel(tab, u_ref, d_ref, *outs):
    b = tab[3]
    for s, ref in enumerate(outs):
        q = quarter(jnp.bitwise_xor(b, s))
        ref[0] = u_ref[:, q]
        ref[1] = d_ref[:, q]


def qkv_kernel(owner_bits, tab, n0, n1, n2, n3, *rest):
    arrays = rest[: len(owner_bits)]
    q_ref, kv_ref, h_ref, w_ref, vv_ref = rest[len(owner_bits) :]
    me, z = tab[0], tab[1]
    for ref, bits in zip(arrays, owner_bits):
        for i, bit in enumerate(bits):
            o = jnp.bitwise_xor(me, bit)
            w_ref[rows_at(o, OWN), :] = ref[i, :OWN, :]
            vv_ref[o] = ref[i, OWN:PANEL, :]
    gain = vec(vv_ref, 0, 0)
    shift = vec(vv_ref, 0, OWN)
    lo = vv_ref[2 * z].astype(F32)
    hi = vv_ref[2 * z + 1].astype(F32)
    zero = jnp.zeros((1, HW), F32)
    bias = jnp.concatenate(
        [
            lo[0:1, 2 * OWN : 3 * OWN],
            hi[0:1, 2 * OWN : 3 * OWN],
            zero,
            lo[0:1, 3 * OWN : 4 * OWN],
            hi[0:1, 3 * OWN : 4 * OWN],
        ],
        axis=1,
    )
    for i, ref in enumerate((n0, n1, n2, n3)):
        rows = slice(i * ROWS, (i + 1) * ROWS)
        h = (ref[...].astype(F32) * gain + shift).astype(BF16)
        h_ref[rows, :] = h
        proj = (nn(h, w_ref[...]) + bias).astype(BF16)
        q_ref[rows, :] = proj[:, :HW] * jnp.asarray(HEAD_DIM ** (-0.5), BF16)
        kv_ref[rows, :] = proj[:, HW:]


def placed(piece, upper):
    zero = jnp.zeros_like(piece)
    return jnp.concatenate([zero, piece] if upper else [piece, zero], axis=1)


def head_cols(h):
    return slice(h * HEAD_DIM, (h + 1) * HEAD_DIM)


def window(index):
    lane = index * HEAD_DIM
    start = lane // 128 * 128
    return slice(start, start + 128), (lane % 128) >= 64


def attend_kernel(tab, q_ref, k0, k1, k2, k3, qc_ref, kc_ref, o0, o1, o2, o3, all_ref, lse_ref):
    kvs = (k0, k1, k2, k3)
    outs = (o0, o1, o2, o3)

    lane = lax.broadcasted_iota(jnp.int32, (STEP, 128), 1)

    def step(i, carry):
        rows = rows_at(i, STEP)
        code1 = qc_ref[rows, 0:1]
        code2 = qc_ref[rows, 1:2]
        masks = []
        for j in range(BLK):
            kc = kc_ref[0:1, j * GROUP : (j + 1) * GROUP]
            masks.append((kc == code1) | (kc == code2))
        heads = []
        lse = jnp.zeros((STEP, 128), F32)
        for h in range(LOCAL_HEADS):
            kwin, kup = window(h)
            vwin, vup = window(LOCAL_HEADS + h)
            qp = placed(q_ref[rows, head_cols(h)], kup)
            scores = [
                jnp.where(masks[j], nt(qp, kvs[j][:, kwin]), NEG) for j in range(BLK)
            ]
            top = functools.reduce(jnp.maximum, [jnp.max(s, axis=1, keepdims=True) for s in scores])
            total = jnp.zeros((STEP, 1), F32)
            acc = jnp.zeros((STEP, 128), F32)
            for j in range(BLK):
                e = jnp.exp(scores[j] - top)
                total = total + jnp.sum(e, axis=1, keepdims=True)
                acc = acc + nn(e.astype(BF16), kvs[j][:, vwin])
            acc = acc[:, 64:] if vup else acc[:, :64]
            heads.append((acc / total).astype(BF16))
            lse = jnp.where(lane == h, top + jnp.log(total), lse)
        all_ref[rows, :] = jnp.concatenate(heads, axis=1)
        lse_ref[rows, :] = lse
        return carry

    lax.fori_loop(0, GROUP // STEP, step, 0)
    for i in range(ULY):
        outs[i][...] = all_ref[i * ROWS : (i + 1) * ROWS, :]


def mix_kernel(plan, tab, a0, a1, a2, a3, x_ref, vv_ref, *rest):
    parts, (resid_ref, h_ref, ow_ref, sems) = rest[:-4], rest[-4:]
    me, z = tab[0], tab[1]
    copies = []
    for index, place, bit in plan:
        copy = pltpu.make_async_copy(
            parts[index].at[place],
            ow_ref.at[rows_at(jnp.bitwise_xor(me, bit), OWN), :],
            sems.at[len(copies)],
        )
        copy.start()
        copies.append(copy)
    acc = x_ref[...] + vec(vv_ref, 0, 4 * OWN)
    for copy in copies:
        copy.wait()
    for j, ref in enumerate((a0, a1, a2, a3)):
        acc = acc + nn(ref[...], ow_ref[rows_at(jnp.bitwise_xor(z, j), HW), :])
    resid_ref[...] = acc
    n, _ = norm_stats(acc)
    h_ref[...] = (n * vec(vv_ref, 0, 5 * OWN) + vec(vv_ref, 1, 0)).astype(BF16)


CHUNK = 256


def ffn_kernel(plan, tab, h0, h1, h2, h3, c0, c1, c2, c3, vv_ref, *rest):
    count = len(rest) - 16
    parts = rest[:count]
    act_ref, dhid_ref, ykeep, ysend, go_ref, g1, g2, g3 = rest[count : count + 8]
    u_ref, d_ref, hall, call_ref, bias_ref, yacc, gacc, sems = rest[count + 8 :]
    me, b = tab[0], tab[3]
    copies = []
    for u_place, d_place, bit in plan:
        rows = rows_at(jnp.bitwise_xor(me, bit), OWN)
        for (index, slot), target in ((u_place, u_ref), (d_place, d_ref)):
            copy = pltpu.make_async_copy(
                parts[index].at[slot], target.at[rows, :], sems.at[len(copies)]
            )
            copy.start()
            copies.append(copy)
    for i, (h_ref, c_ref) in enumerate(((h0, c0), (h1, c1), (h2, c2), (h3, c3))):
        rows = slice(i * ROWS, (i + 1) * ROWS)
        hall[rows, :] = h_ref[...]
        call_ref[rows, :] = c_ref[...]
    for k in range(2):
        bias_ref[:, k * 384 : (k + 1) * 384] = vv_ref[2 * b + k].astype(F32)[1:2, 192:576]
    yacc[...] = jnp.zeros_like(yacc)
    gacc[...] = jnp.zeros_like(gacc)
    for copy in copies:
        copy.wait()

    def step(k, carry):
        cols = pl.ds(pl.multiple_of(k * CHUNK, CHUNK), CHUNK)
        hid = nn(hall[...], u_ref[:, cols]) + bias_ref[:, cols]
        dact = nn(call_ref[...], d_ref[:, cols])
        cdf = 0.5 * (1.0 + lax.erf(hid * 0.7071067811865476))
        act = (hid * cdf).astype(BF16)
        pdf = jnp.exp(-0.5 * hid * hid) * 0.3989422804014327
        dhid = (dact * (cdf + hid * pdf)).astype(BF16)
        act_ref[:, cols] = act
        dhid_ref[:, cols] = dhid
        yacc[...] += nt(act, d_ref[:, cols])
        gacc[...] += nt(dhid, u_ref[:, cols])
        return carry

    lax.fori_loop(0, QUART // CHUNK, step, 0)
    for i, y_ref in enumerate((ykeep, ysend, ykeep, ysend)):
        y_ref[i // 2] = yacc[i * ROWS : (i + 1) * ROWS, :].astype(y_ref.dtype)
    for i, g_ref in enumerate((go_ref, g1, g2, g3)):
        g_ref[...] = gacc[i * ROWS : (i + 1) * ROWS, :].astype(g_ref.dtype)


def ffn_grad_kernel(tab, *refs):
    me = tab[0]
    h_refs, c_refs = refs[:4], refs[4:8]
    dhid_ref, act_ref, usend, ukeep, dthere, dhere, left, left2 = refs[8:]
    for i in range(BLK):
        left[:, i * ROWS : (i + 1) * ROWS] = h_refs[i][...].T
        left2[:, i * ROWS : (i + 1) * ROWS] = c_refs[i][...].T
    for source, right_ref, ref, bits in (
        (left, dhid_ref, usend, (4, 5, 6, 7)),
        (left, dhid_ref, ukeep, (0, 1, 2, 3)),
        (left2, act_ref, dthere, (2, 6, 3, 7)),
        (left2, act_ref, dhere, (0, 4, 1, 5)),
    ):
        for s, bit in enumerate(bits):
            o = jnp.bitwise_xor(me, bit)
            ref[s] = nn(source[rows_at(o, OWN), :], right_ref[...]).astype(BF16)


def back_mix_kernel(
    tab, resid_ref, cot_ref, go_ref, g1, g2, g3, ow_ref, vv_ref, dres_ref, dmix_ref, d0, d1, d2, d3, vs_ref
):
    z = tab[1]
    grad = go_ref[...] + g1[...].astype(F32) + g2[...].astype(F32) + g3[...].astype(F32)
    n, r = norm_stats(resid_ref[...])
    dn = grad * vec(vv_ref, 0, 5 * OWN)
    dres = cot_ref[...] + r * (
        dn
        - jnp.mean(dn, axis=-1, keepdims=True)
        - n * jnp.mean(dn * n, axis=-1, keepdims=True)
    )
    dres_ref[...] = dres
    dmix = dres.astype(BF16)
    dmix_ref[...] = dmix
    for j, ref in enumerate((d0, d1, d2, d3)):
        ref[...] = nt(dmix, ow_ref[rows_at(jnp.bitwise_xor(z, j), HW), :]).astype(BF16)
    vs_ref[0:1, :] = jnp.sum(dmix.astype(F32), axis=0, keepdims=True)
    vs_ref[1:2, :] = jnp.sum(grad * n, axis=0, keepdims=True)
    vs_ref[2:3, :] = jnp.sum(grad, axis=0, keepdims=True)
    vs_ref[3:8, :] = jnp.zeros((5, WIDTH), F32)


def out_grad_kernel(tab, a0, a1, a2, a3, dmix_ref, vs_ref, dhid_ref, c_ref, keep, send, left, vrow):
    me, z, b = tab[0], tab[1], tab[3]
    for j, ref in enumerate((a0, a1, a2, a3)):
        left[rows_at(jnp.bitwise_xor(z, j), HW), :] = ref[...].astype(F32).T.astype(BF16)
    vs = vs_ref[...]
    usum = jnp.sum(dhid_ref[...].astype(F32), axis=0, keepdims=True)
    csum = jnp.sum(c_ref[...].astype(F32), axis=0, keepdims=True)
    for o in range(OWNERS):
        part = usum[:, (o % 2) * 384 : (o % 2 + 1) * 384]
        row = jnp.concatenate(
            [vs[k : k + 1, o * OWN : (o + 1) * OWN] for k in range(3)]
            + [jnp.where(b == o // 2, part, 0.0), csum[:, o * OWN : (o + 1) * OWN]],
            axis=1,
        )
        vrow[o] = jnp.broadcast_to(row, (16, WIDTH)).astype(BF16)
    for ref, base in ((send, 1), (keep, 0)):
        for s in range(4):
            o = jnp.bitwise_xor(me, base + (s // 2) * 2 + (s % 2) * 4)
            ref[s, :OWN, :] = nn(left[rows_at(o, OWN), :], dmix_ref[...]).astype(BF16)
            ref[s, OWN:, :] = vrow[o]


def back_attend_kernel(
    tab,
    q_ref,
    k0,
    k1,
    k2,
    k3,
    g0,
    g1,
    g2,
    g3,
    all_ref,
    lse_ref,
    qr_ref,
    kcol_ref,
    dq_ref,
    keep,
    send,
    acc,
    gall,
):
    kvs = (k0, k1, k2, k3)
    acc[...] = jnp.zeros_like(acc)
    for i, g_ref in enumerate((g0, g1, g2, g3)):
        gall[i * ROWS : (i + 1) * ROWS, :] = g_ref[...]
    lane = lax.broadcasted_iota(jnp.int32, (BACK_STEP, 128), 1)

    def step(i, carry):
        rows = rows_at(i, BACK_STEP)
        prod = gall[rows, :].astype(F32) * all_ref[rows, :].astype(F32)
        stat = jnp.zeros((BACK_STEP, 128), F32)
        for h in range(LOCAL_HEADS):
            stat = jnp.where(
                lane == h, jnp.sum(prod[:, head_cols(h)], axis=1, keepdims=True), stat
            )
        rowdot = stat.T
        lse = lse_ref[rows, :].T
        code1 = qr_ref[0:1, rows]
        code2 = qr_ref[1:2, rows]
        dq = [jnp.zeros((BACK_STEP, 128), F32) for _ in range(LOCAL_HEADS)]
        for j in range(BLK):
            kc = kcol_ref[j * GROUP : (j + 1) * GROUP, :]
            mask = (kc == code1) | (kc == code2)
            for h in range(LOCAL_HEADS):
                kwin, kup = window(h)
                vwin, vup = window(LOCAL_HEADS + h)
                qp = placed(q_ref[rows, head_cols(h)], kup)
                gp = placed(gall[rows, head_cols(h)], vup)
                kk = kvs[j][:, kwin]
                scores = nt(kk, qp)
                p = jnp.where(mask, jnp.exp(scores - lse[h : h + 1, :]), 0.0)
                dp = nt(kvs[j][:, vwin], gp)
                ds = (p * (dp - rowdot[h : h + 1, :])).astype(BF16)
                acc[j, :, vwin] += nn(p.astype(BF16), gp)
                acc[j, :, kwin] += nn(ds, qp)
                dq[h] = dq[h] + tn(ds, kk)
        parts = []
        for h in range(LOCAL_HEADS):
            _, kup = window(h)
            parts.append(dq[h][:, 64:] if kup else dq[h][:, :64])
        dq_ref[rows, :] = (jnp.concatenate(parts, axis=1) * HEAD_DIM ** (-0.5)).astype(BF16)
        return carry

    lax.fori_loop(0, GROUP // BACK_STEP, step, 0)
    keep[0] = acc[0].astype(BF16)
    keep[1] = acc[2].astype(BF16)
    send[0] = acc[1].astype(BF16)
    send[1] = acc[3].astype(BF16)


def back_proj_kernel(
    tab, dq_ref, keep, got, recv, w_ref, n0, n1, n2, n3, dproj_ref, h0, h1, send, vs_ref
):
    dproj_ref[:, :HW] = dq_ref[...]
    total = keep[0].astype(F32) + got[0].astype(F32) + recv[...].astype(F32)
    dproj_ref[:, HW:] = total.astype(BF16)
    gain = jnp.zeros((1, WIDTH), F32)
    shift = jnp.zeros((1, WIDTH), F32)
    outs = (h0, h1, send.at[0], send.at[1])
    for i, (n_ref, out) in enumerate(zip((n0, n1, n2, n3), outs)):
        rows = slice(i * ROWS, (i + 1) * ROWS)
        grad = nt(dproj_ref[rows, :], w_ref[...])
        out[...] = grad.astype(out.dtype)
        gain = gain + jnp.sum(grad * n_ref[...].astype(F32), axis=0, keepdims=True)
        shift = shift + jnp.sum(grad, axis=0, keepdims=True)
    vs_ref[0:1, :] = gain
    vs_ref[1:2, :] = shift
    cols = jnp.sum(dproj_ref[...].astype(F32), axis=0, keepdims=True)
    vs_ref[2:3, :] = jnp.concatenate([cols, jnp.zeros((1, WIDTH - 3 * HW), F32)], axis=1)
    vs_ref[3:8, :] = jnp.zeros((5, WIDTH), F32)


def qkv_grad_kernel(tab, h_ref, dproj_ref, vs_ref, keep, send, left, vrow):
    me, z = tab[0], tab[1]
    vs = vs_ref[...]
    for o in range(OWNERS):
        row = [vs[k : k + 1, o * OWN : (o + 1) * OWN] for k in range(2)]
        for lane in (0, 2 * HW):
            lane = lane + (o % 2) * OWN
            row.append(jnp.where(z == o // 2, vs[2:3, lane : lane + OWN], 0.0))
        row.append(jnp.zeros((1, 3 * HW - 4 * OWN), F32))
        vrow[o] = jnp.broadcast_to(jnp.concatenate(row, axis=1), (16, 3 * HW)).astype(BF16)
    for i in range(ULY):
        rows = slice(i * ROWS, (i + 1) * ROWS)
        left[:, rows] = h_ref[rows, :].T
    for ref, base in ((keep, 0), (send, 1)):
        for s in range(4):
            o = jnp.bitwise_xor(me, base + (s // 2) * 2 + (s % 2) * 4)
            ref[s, :OWN, :] = nn(left[rows_at(o, OWN), :], dproj_ref[...]).astype(BF16)
            ref[s, OWN:, :] = vrow[o]


def back_norm_kernel(tab, x_ref, dres_ref, h0, got2, got1, vv_ref, out_ref):
    grad = h0[...] + got2[0].astype(F32) + got1[...].astype(F32)
    n, r = norm_stats(x_ref[...])
    dn = grad * vec(vv_ref, 0, 0)
    out_ref[...] = dres_ref[...] + r * (
        dn
        - jnp.mean(dn, axis=-1, keepdims=True)
        - n * jnp.mean(dn * n, axis=-1, keepdims=True)
    )


def output_kernel(tab, resid_ref, keep, got, last, vv_ref, out_ref):
    out_ref[...] = (
        resid_ref[...]
        + keep[0]
        + got[0].astype(F32)
        + last[...].astype(F32)
        + vec(vv_ref, 1, OWN)
    )


def low_sum(a, b):
    return (a.astype(F32) + b.astype(F32)).astype(BF16)


def split_kernel(bit, tab, a_ref, ac_ref, by_ref, byc_ref, keep, send):
    for value, low_out, high_out in ((0, keep, send), (1, send, keep)):

        @pl.when(tab[bit] == value)
        def _():
            low_out[0] = a_ref[0]
            low_out[1] = ac_ref[1]
            high_out[0] = by_ref[0]
            high_out[1] = byc_ref[1]


def pack_kernel(tab, a_ref, ac_ref, by_ref, byc_ref, out_ref):
    for s, (ref, place) in enumerate(((a_ref, 1), (ac_ref, 3), (by_ref, 1), (byc_ref, 3))):
        out_ref[s] = ref[place]


def split_add_kernel(bit, tab, a_ref, ac_ref, by_ref, byc_ref, got, keep, send):
    refs = ((a_ref, 0), (ac_ref, 2), (by_ref, 0), (byc_ref, 2))
    for value, low_out, high_out in ((0, keep, send), (1, send, keep)):

        @pl.when(tab[bit] == value)
        def _():
            for s, (ref, place) in enumerate(refs):
                (low_out, high_out)[s // 2][s % 2] = low_sum(ref[place], got[s])


def merge_kernel(bit, tab, a_ref, b_ref, keep, send):
    for value, low_out, high_out in ((0, keep, send), (1, send, keep)):

        @pl.when(tab[bit] == value)
        def _():
            low_out[...] = low_sum(a_ref[0], b_ref[0])
            high_out[...] = low_sum(a_ref[1], b_ref[1])


def final_kernel(tab, pair, got, out_ref):
    b, odd, high = tab[3], tab[4], tab[5]
    for flip, ref in ((0, pair.at[0]), (1, pair.at[1]), (2, got.at[0]), (3, got.at[1])):
        q = jnp.bitwise_xor(jnp.bitwise_xor(b, 2 * odd + high), flip)
        out_ref[:, quarter(q)] = ref[...].astype(F32)


def qkv_final_kernel(tab, pair, got, out_ref, vec_ref):
    z = tab[1]
    refs = (pair.at[0], pair.at[1], got.at[0], got.at[1])
    for k in range(ULY):

        @pl.when(z == k)
        def _():
            for p in range(3):
                cols = [
                    refs[t ^ k][:OWN, p * HW : (p + 1) * HW].astype(F32) for t in range(ULY)
                ]
                out_ref[:, p * WIDTH : (p + 1) * WIDTH] = jnp.concatenate(cols, axis=1)

    total = jnp.zeros((16, 3 * HW), F32)
    for ref in refs:
        total = total + ref[OWN:, :].astype(F32)
    vec_ref[...] = total[:8, :]


def add_low(a, b):
    return (a.astype(F32) + b.astype(F32)).astype(BF16)


def xor_order(array, axis, index):
    shape = array.shape
    two = array.reshape(shape[:axis] + (2, 2) + shape[axis + 1 :])
    two = jnp.where((index & 1) == 1, jnp.flip(two, axis + 1), two)
    two = jnp.where((index & 2) == 2, jnp.flip(two, axis), two)
    return two.reshape(shape)


def body(
    inputs,
    cotangent,
    qkv_weight,
    query_bias,
    value_bias,
    out_weight,
    out_bias,
    norm1_gain,
    norm1_bias,
    norm2_gain,
    norm2_bias,
    up_weight,
    up_bias,
    down_weight,
    down_bias,
    doc_lengths,
    pad_mask,
):
    dp_count = lax.axis_size("dp")
    near = dp_count == 2
    dp = lax.axis_index("dp")
    z = lax.axis_index("uly")
    b = lax.axis_index("blk")
    core = b & 1
    rank = dp * BLK + b
    me = rank if near else jnp.int32(0)
    tab = jnp.stack([me, z, core, b, z & 1, z >> 1]).astype(jnp.int32)
    own_rows = WIDTH // (dp_count * BLK)
    axes = ("dp", "blk")

    x = inputs.reshape(ROWS, WIDTH)
    cot = cotangent.reshape(ROWS, WIDTH)

    if near:
        vectors = [norm1_gain, norm1_bias, query_bias, value_bias, out_bias, norm2_gain]
        vectors += [norm2_bias, down_bias, up_bias]
        n0, panel = call(
            prep_kernel,
            [sds((ROWS, WIDTH), BF16), sds((PANEL, 3 * HW), BF16)],
            [tab, x, qkv_weight, *vectors],
        )
        n1, n2, n3 = (swap(n0, "uly", k) for k in (1, 2, 3))
        a_0 = jnp.stack([panel, swap(panel, "dp", 1)])
        a_2 = swap(a_0, "blk", 2)
        four_bits = [[0, 4], [2, 6], [1, 5], [3, 7]]
        w_mine = call(
            ffn_prep_kernel,
            [sds((2, OWN, QUART), BF16)] * BLK,
            [tab, up_weight, down_weight.T],
        )
        n1 = after(n1, w_mine[0])
        a_2c = swap(a_2, "blk", 1)
        a_0c = swap(after(a_0, a_2c), "blk", 1)
        a_parts = [a_0, a_2, a_0c, a_2c]
        w_parts = [w_mine[0], None, cross(after(w_mine[2], a_0c), 2)] + [None] * 5
        w_plan = [((i, 0), (i, 1), i) for i in range(OWNERS)]
        o_plan = [
            (i, k, bit) for i, bits in enumerate(four_bits) for k, bit in enumerate(bits)
        ]
    else:
        (n0,) = call(norm_kernel, [sds((ROWS, WIDTH), BF16)], [tab, x])
        n1, n2, n3 = (swap(n0, "uly", k) for k in (1, 2, 3))
        qkv_cols = lax.dynamic_index_in_dim(
            qkv_weight.reshape(own_rows, 3, ULY, HW), z, axis=2, keepdims=False
        ).reshape(own_rows, 3 * HW)

        def full(array):
            return lax.all_gather(array, axes, axis=0, tiled=True)

        def eight(vector):
            return full(vector).reshape(OWNERS, 1, -1)

        def mine(array):
            cols = full(array).reshape(WIDTH, BLK, QUART)
            return lax.dynamic_index_in_dim(cols, b, 1, False).reshape(OWNERS, OWN, QUART)

        row0 = jnp.concatenate(
            [
                eight(v)
                for v in (norm1_gain, norm1_bias, query_bias, value_bias, out_bias, norm2_gain)
            ],
            axis=2,
        )
        row1 = jnp.concatenate([eight(v) for v in (norm2_bias, down_bias, up_bias)], axis=2)
        a_parts = [
            jnp.concatenate(
                [
                    full(qkv_cols).reshape(OWNERS, OWN, 3 * HW),
                    row0,
                    row1,
                    jnp.zeros((OWNERS, 14, 3 * HW), BF16),
                ],
                axis=1,
            )
        ]
        four_bits = [list(range(OWNERS))]
        o_parts = [full(out_weight).reshape(OWNERS, OWN, WIDTH)]
        w_parts = [mine(up_weight), mine(down_weight.T)]
        w_plan = [((0, o), (1, o), o) for o in range(OWNERS)]
        o_plan = [(0, o, o) for o in range(OWNERS)]

    ends = jnp.cumsum(doc_lengths.reshape(-1), dtype=jnp.int32)
    zs = jnp.arange(ULY, dtype=jnp.int32) ^ z
    bs = jnp.arange(BLK, dtype=jnp.int32) ^ b
    within = jnp.arange(ROWS, dtype=jnp.int32)
    kplace = ((zs[None, :, None] * BLK + bs[:, None, None]) * ROWS + within).reshape(KEYS)
    kseg = jnp.sum((kplace[:, None] >= ends[None, :]).astype(jnp.int32), axis=1)
    valid = pad_mask.reshape(ULY, BLK, ROWS)
    valid = xor_order(xor_order(valid, 0, z), 1, b).transpose(1, 0, 2).reshape(KEYS)
    kcode = jnp.where(valid > 0, kseg, kplace + 64)
    qcodes = jnp.stack([kseg[:GROUP], kplace[:GROUP] + 64])

    n1, k_rows = lax.optimization_barrier((n1, kcode[None, :]))
    q, kv, h1, w_qkv, vv = call(
        functools.partial(qkv_kernel, four_bits),
        [
            sds((GROUP, HW), BF16),
            sds((GROUP, 2 * HW), BF16),
            sds((GROUP, WIDTH), BF16),
            sds((WIDTH, 3 * HW), BF16),
            sds((OWNERS, 16, 3 * HW), BF16),
        ],
        [tab, n0, n1, n2, n3, *a_parts],
        flops=2 * GROUP * WIDTH * 3 * HW,
    )
    q_rows, late = lax.optimization_barrier((qcodes, kcode, kv))[:2]
    k_cols = late[:, None]
    q_cols = q_rows.T
    cb = cot.astype(BF16)
    if near:
        kv_y = swap(after(kv, w_parts[2]), "blk", 2)
        cb_y = swap(after(cb, kv_y), "blk", 2)
        w_parts[4] = cross(after(w_mine[0], kv), 4)
        w_parts[5] = cross(after(w_mine[1], kv), 5)
        o_0 = jnp.stack([out_weight, swap(after(out_weight, kv), "dp", 1)])
        o_0c = swap(o_0, "blk", 1)
        o_2 = swap(after(o_0, kv_y), "blk", 2)
    else:
        kv_y = swap(kv, "blk", 2)
    kv_c = swap(kv, "blk", 1)
    kv_yc = swap(kv_y, "blk", 1)
    if near:
        cb_c = swap(after(cb, kv), "blk", 1)
        w_parts[1] = cross(after(w_mine[1], kv), 1)
        kv_yc = after(kv_yc, o_0c, w_parts[1], cb_c)
    kvs = [kv, kv_c, kv_y, kv_yc]

    def around(array):
        near_y = swap(array, "blk", 2)
        return [array, swap(array, "blk", 1), near_y, swap(near_y, "blk", 1)]

    if near:
        w_parts[3] = cross(after(w_mine[3], kv_y), 3)
    else:
        cbs = around(cb)

    *attn_slots, attn_all, lse = call(
        attend_kernel,
        [sds((ROWS, HW), BF16)] * ULY + [sds((GROUP, HW), BF16), sds((GROUP, 128), F32)],
        [tab, q, *kvs, q_cols, k_rows],
        flops=4 * GROUP * KEYS * HW,
    )
    if near:
        attn_slots = after(attn_slots, w_parts[4], w_parts[5], o_2)
        o_2c = swap(after(o_2, attn_slots[0]), "blk", 1)
        o_parts = [o_0, o_2, o_0c, o_2c]
    attn = [attn_slots[0]] + [swap(attn_slots[k], "uly", k) for k in (1, 2, 3)]
    resid, h2, ow = call(
        functools.partial(mix_kernel, o_plan),
        [sds((ROWS, WIDTH), F32), sds((ROWS, WIDTH), BF16), sds((WIDTH, WIDTH), BF16)],
        [tab, *attn, x, vv, *o_parts],
        scratch=[pltpu.SemaphoreType.DMA((OWNERS,))],
        flops=2 * ROWS * WIDTH * WIDTH,
        in_any=range(7, 7 + len(o_parts)),
    )

    if near:
        w_parts[6] = cross(after(w_mine[2], attn[1]), 6)
        w_parts[7] = cross(after(w_mine[3], attn[2], cb_y, w_parts[3]), 7)
        h2 = after(h2, w_parts[6], w_parts[7])
        cbs = [cb, cb_c, cb_y, swap(after(cb_y, h2), "blk", 1)]
    h2s = around(h2)
    parts = len(w_parts)
    act, dhid, y_keep, y_send, go, *gs = call(
        functools.partial(ffn_kernel, w_plan),
        [sds((GROUP, QUART), BF16)] * 2
        + [sds((2, ROWS, WIDTH), F32), sds((2, ROWS, WIDTH), BF16), sds((ROWS, WIDTH), F32)]
        + [sds((ROWS, WIDTH), BF16)] * 3,
        [tab, *h2s, *cbs, vv, *w_parts],
        scratch=[
            pltpu.VMEM((WIDTH, QUART), BF16),
            pltpu.VMEM((WIDTH, QUART), BF16),
            pltpu.VMEM((GROUP, WIDTH), BF16),
            pltpu.VMEM((GROUP, WIDTH), BF16),
            pltpu.VMEM((1, QUART), F32),
            pltpu.VMEM((GROUP, WIDTH), F32),
            pltpu.VMEM((GROUP, WIDTH), F32),
            pltpu.SemaphoreType.DMA((2 * OWNERS,)),
        ],
        flops=8 * GROUP * WIDTH * QUART,
        in_any=range(10, 10 + parts),
    )
    gs = [swap(g, "blk", k) for k, g in enumerate(gs, 1)]

    y_got = swap(y_send, "blk", 1)
    y_part = (y_keep[1] + y_got[1].astype(F32)).astype(BF16)
    usend, ukeep, dthere, dhere = call(
        ffn_grad_kernel,
        [sds((BLK, OWN, QUART), BF16)] * 4,
        [tab, *h2s, *cbs, dhid, act],
        scratch=[pltpu.VMEM((WIDTH, GROUP), BF16)] * 2,
    )
    go = after(go, usend, dthere, y_part)

    dres, dmix, *dattn_slots, vs2 = call(
        back_mix_kernel,
        [sds((ROWS, WIDTH), F32), sds((ROWS, WIDTH), BF16)]
        + [sds((ROWS, HW), BF16)] * ULY
        + [sds((8, WIDTH), F32)],
        [tab, resid, cot, go, *gs, ow, vv],
        flops=2 * ROWS * WIDTH * WIDTH,
    )
    pair = sds((2, OWN, QUART), BF16)
    one = sds((OWN, QUART), BF16)
    dattn = [dattn_slots[0]] + [swap(dattn_slots[k], "uly", k) for k in (1, 2, 3)]
    if near:
        u_got = swap(usend, "dp", 1)
        d_there = swap(after(dthere, dmix), "blk", 2)
    y_last = swap(after(y_part, dattn[1]), "blk", 2)

    dq, keep_kv, send_kv = call(
        back_attend_kernel,
        [sds((GROUP, HW), BF16), sds((2, GROUP, 2 * HW), BF16), sds((2, GROUP, 2 * HW), BF16)],
        [tab, q, *kvs, *dattn, attn_all, lse, q_rows, k_cols],
        scratch=[pltpu.VMEM((BLK, GROUP, 2 * HW), F32), pltpu.VMEM((GROUP, HW), BF16)],
        flops=10 * GROUP * KEYS * HW,
    )
    if near:
        send_kv = after(send_kv, d_there, y_last)
    got = swap(send_kv, "blk", 1)
    kv_send = add_low(keep_kv[1], got[1])
    kv_got = swap(kv_send, "blk", 2)
    okeep, osend = call(
        out_grad_kernel,
        [sds((4, PANEL, WIDTH), BF16)] * 2,
        [tab, *attn, after(dmix, kv_send), vs2, dhid, cb],
        scratch=[pltpu.VMEM((WIDTH, ROWS), BF16), pltpu.VMEM((OWNERS, 16, WIDTH), BF16)],
    )

    if near:
        dhere, d_there = after(dhere, kv_send), after(d_there, kv_send)
        pieces = [dhere, swap(dhere, "blk", 1), d_there, swap(d_there, "blk", 1)]
        (d_send,) = call(pack_kernel, [sds((BLK, OWN, QUART), BF16)], [tab, *pieces])
        dq = after(dq, d_send, okeep)
    dproj, g_own, g_one, g_send, vs1 = call(
        back_proj_kernel,
        [sds((GROUP, 3 * HW), BF16)]
        + [sds((ROWS, WIDTH), F32)] * 2
        + [sds((2, ROWS, WIDTH), BF16), sds((8, WIDTH), F32)],
        [tab, dq, keep_kv, got, kv_got, w_qkv, n0, n1, n2, n3],
        flops=2 * GROUP * WIDTH * 3 * HW,
    )
    qkeep, qsend = call(
        qkv_grad_kernel,
        [sds((4, PANEL, 3 * HW), BF16)] * 2,
        [tab, h1, dproj, vs1],
        scratch=[pltpu.VMEM((WIDTH, GROUP), BF16), pltpu.VMEM((OWNERS, 16, 3 * HW), BF16)],
    )
    (output,) = call(
        output_kernel,
        [sds((ROWS, WIDTH), F32)],
        [tab, after(resid, dproj), y_keep, y_got, y_last, vv],
    )
    if near:
        o1 = add_low(okeep, swap(after(osend, dproj), "blk", 1))
        u_got = after(u_got, dproj)
        u_there = add_low(ukeep[2:], u_got[2:])
        u_here = add_low(ukeep[:2], u_got[:2])
        q1 = add_low(qkeep, swap(qsend, "blk", 1))
        u_there = swap(u_there, "blk", 2)
        upieces = [u_here, swap(u_here, "blk", 1), u_there, swap(u_there, "blk", 1)]
        ukept, usent = call(functools.partial(split_kernel, 4), [pair] * 2, [tab, *upieces])
        dkept, dsent = call(
            functools.partial(split_add_kernel, 4),
            [pair] * 2,
            [tab, *pieces, after(swap(d_send, "dp", 1), dproj)],
        )
        gates = [q1, dsent, usent]
    else:
        gates = []
    g_got = after(swap(g_send, "uly", 2), *gates)
    g_last = swap((g_one + g_got[1].astype(F32)).astype(BF16), "uly", 1)
    if near:

        def over_uly(kept, sent):
            return call(
                functools.partial(merge_kernel, 5),
                [one] * 2,
                [tab, kept, after(swap(sent, "uly", 1), g_got)],
            )

        def share(total):
            pair = jnp.stack([total, swap(total, "uly", 2)])
            return call(
                final_kernel, [sds((OWN, FF), F32)], [tab, pair, swap(pair, "uly", 1)]
            )[0]

        dkept, dsent = over_uly(dkept, dsent)
        ukept, usent = over_uly(ukept, usent)
        d_total = add_low(dkept, swap(dsent, "uly", 2))
        u_mid = swap(usent, "uly", 2)
        g_last = after(g_last, d_total, usent, output)

        o2 = add_low(o1[:2], swap(o1[2:], "blk", 2))
        o3 = add_low(o2[0], swap(o2[1], "dp", 1))
        u_total = add_low(after(ukept, o3), u_mid)
        grad_down = share(d_total).T
        grad_up = share(u_total)
        o4 = add_low(o3, swap(after(o3, d_total), "uly", 1))
        o5 = o4.astype(F32) + swap(o4, "uly", 2).astype(F32)
        grad_ow = o5[:OWN]
        grad_obias, grad_gain2, grad_shift2 = (o5[OWN, k * OWN : (k + 1) * OWN] for k in range(3))
        grad_ubias, grad_dbias = o5[OWN, 288:672], o5[OWN, 672:768]

        q2 = add_low(q1[:2], swap(q1[2:], "blk", 2))
        q3 = add_low(q2[0], swap(q2[1], "dp", 1))
        q_pair = jnp.stack([q3, swap(q3, "uly", 1)])
        grad_qkv, qvec = call(
            qkv_final_kernel,
            [sds((OWN, 3 * WIDTH), F32), sds((8, 3 * HW), F32)],
            [tab, q_pair, swap(after(q_pair, u_total), "uly", 2)],
        )
        grad_gain1, grad_shift1, grad_qbias, grad_vbias = (
            qvec[0, k * OWN : (k + 1) * OWN] for k in range(4)
        )
    else:

        def owned(array):
            shard = lax.psum_scatter(
                array.astype(F32), axes, scatter_dimension=0, tiled=True
            )
            return lax.psum(shard.astype(BF16), "uly").astype(F32)

        def by_owner(keep, send, order):
            both = jnp.concatenate([keep, send], axis=0)
            return both[jnp.array(order)]

        o8 = by_owner(okeep, osend, [0, 4, 2, 6, 1, 5, 3, 7])
        q8 = by_owner(qkeep, qsend, [0, 4, 2, 6, 1, 5, 3, 7])

        def widen(keep, send, order):
            flat = jnp.concatenate([keep, send], axis=0)[jnp.array(order)]
            flat = flat.reshape(WIDTH, 1, QUART)
            place = (jnp.arange(BLK) == b)[None, :, None]
            return jnp.where(place, flat, jnp.zeros_like(flat)).reshape(WIDTH, FF)

        grad_up = owned(widen(ukeep, usend, range(OWNERS)))
        grad_down = owned(widen(dhere, dthere, [0, 2, 4, 6, 1, 3, 5, 7])).T
        grad_ubias = owned(o8[:, OWN, 288:672].reshape(FF))
        grad_dbias = owned(o8[:, OWN, 672:768].reshape(WIDTH))
        grad_ow = owned(o8[:, :OWN].reshape(WIDTH, WIDTH))
        grad_obias, grad_gain2, grad_shift2 = (
            owned(o8[:, OWN, k * OWN : (k + 1) * OWN].reshape(WIDTH)) for k in range(3)
        )
        mine = q8[:, :OWN].reshape(WIDTH, 3, 1, HW)
        spread = jnp.where(
            (jnp.arange(ULY) == z)[None, None, :, None], mine, jnp.zeros_like(mine)
        )
        grad_qkv = owned(spread.reshape(WIDTH, 3 * WIDTH))
        grad_gain1, grad_shift1, grad_qbias, grad_vbias = (
            owned(q8[:, OWN, k * OWN : (k + 1) * OWN].reshape(WIDTH)) for k in range(4)
        )

    (grad_inputs,) = call(
        back_norm_kernel, [sds((ROWS, WIDTH), F32)], [tab, x, dres, g_own, g_got, g_last, vv]
    )
    return (
        output.reshape(inputs.shape),
        grad_inputs.reshape(inputs.shape),
        grad_qkv,
        grad_qbias,
        grad_vbias,
        grad_ow,
        grad_obias,
        grad_gain1,
        grad_shift1,
        grad_gain2,
        grad_shift2,
        grad_up,
        grad_ubias,
        grad_down,
        grad_dbias,
    )


def solution(mesh):
    rows = P(None, ("dp", "uly", "blk"), None)
    first = P(("dp", "blk"), None)
    flat = P(("dp", "blk"))
    second = P(None, ("dp", "blk"))
    return jax.shard_map(
        body,
        mesh=mesh,
        in_specs=(
            rows,
            rows,
            first,
            flat,
            flat,
            first,
            flat,
            flat,
            flat,
            flat,
            flat,
            first,
            flat,
            second,
            flat,
            P(None, "dp", None),
            P(None, "dp"),
        ),
        out_specs=(
            rows,
            rows,
            first,
            flat,
            flat,
            first,
            flat,
            flat,
            flat,
            flat,
            flat,
            first,
            flat,
            second,
            flat,
        ),
        check_vma=False,
    )
```
